32 devices in a mesh: dp: 4 (over y, x), seq: 8 (over z, core).
Axes of the slice: x: 2, y: 2, z: 4, core: 2. Of those that a mesh axis runs over, the one named last changes fastest.
Arguments:
- tokens: float32 [16, 2048, 768], P('dp', 'seq')
- lengths: int32 [16], P('dp'), may hold values from 1024 to 2048
- keep: int32 [16, 2048], P('dp', 'seq'), may hold values from 0 to 1, as said below
- w_query: float32 [768, 768], replicated, may hold values from -0.21875 to 0.21875
- b_query: float32 [768], replicated, may hold values from -3 to 3
- w_key: float32 [768, 768], replicated, may hold values from -0.21875 to 0.21875
- w_value: float32 [768, 768], replicated, may hold values from -0.21875 to 0.21875
- b_value: float32 [768], replicated, may hold values from -3 to 3
- conv_weight: float32 [12, 33], replicated, may hold values from -0.5 to 0.5
- w_out: float32 [768, 768], replicated, may hold values from -0.4375 to 0.4375
- b_out: float32 [768], replicated, may hold values from -2 to 2
- gain_one: float32 [768], replicated, may hold values from 0.5 to 1.5
- shift_one: float32 [768], replicated, may hold values from -2 to 2
- w_up: float32 [768, 3072], replicated, may hold values from -0.21875 to 0.21875
- b_up: float32 [3072], replicated, may hold values from -2 to 2
- w_down: float32 [3072, 768], replicated, may hold values from -0.109375 to 0.109375
- b_down: float32 [768], replicated, may hold values from -2 to 2
- gain_two: float32 [768], replicated, may hold values from 0.5 to 1.5
- shift_two: float32 [768], replicated, may hold values from -2 to 2
- cotangent: float32 [16, 2048, 768], P('dp', 'seq'), may hold values from -6 to 6
Outputs:
- output: float32 [16, 2048, 768], P('dp', 'seq')
- grad_tokens: float32 [16, 2048, 768], P('dp', 'seq')
- grad_w_query: float32 [768, 768], P('dp', 'seq')
- grad_b_query: float32 [768], replicated
- grad_w_key: float32 [768, 768], P('dp', 'seq')
- grad_w_value: float32 [768, 768], P('dp', 'seq')
- grad_b_value: float32 [768], replicated
- grad_conv: float32 [12, 33], replicated
- grad_w_out: float32 [768, 768], P('dp', 'seq')
- grad_b_out: float32 [768], replicated
- grad_gain_one: float32 [768], replicated
- grad_shift_one: float32 [768], replicated
- grad_w_up: float32 [768, 3072], P('dp', 'seq')
- grad_b_up: float32 [3072], replicated
- grad_w_down: float32 [3072, 768], P('dp', 'seq')
- grad_b_down: float32 [768], replicated
- grad_gain_two: float32 [768], replicated
- grad_shift_two: float32 [768], replicated
The draws below stay inside these ranges and needn't reach their ends.
Inputs may be any that keep to these rules, and one draw needn't show every extreme that they name: `keep`: in every item, a run of 66 consecutive positions within the first 1024 positions is 0; elsewhere a position is 1 with probability 17 / 20.
All inputs are finite; a program needn't handle non-finite values.
Results may differ from the reference program's by a relative error of at most 0.0003.
Values sent between devices are 32-bit elements; how exact they have to be, the bound alone decides.
A program may use at most 384 MiB of HBM per device.

```python
import jax
import jax.numpy as jnp
from jax import lax

D = 768
HEADS = 12
FF = 3072
MARKS = 64
NEWTON = 6
KERNEL = 33
LEN = 2048
ITEMS = 16


def draw_tokens(key, part):
    noise_key, coarse_key = jax.random.split(key)
    noise = jax.random.normal(noise_key, (ITEMS, LEN, D), jnp.float32)
    coarse = jax.random.normal(coarse_key, (ITEMS, LEN // 32, D), jnp.float32)
    smooth = jnp.repeat(coarse, 32, axis=1)
    return 0.6 * noise + 0.9 * smooth


def draw_keep(key, part):
    coin_key, start_key = jax.random.split(jax.random.fold_in(key, 7))
    run_length = 2 * LEN // MARKS + 2
    coins = jax.random.randint(coin_key, (ITEMS, LEN), 0, 20)
    starts = jax.random.randint(start_key, (ITEMS, 1), 0, LEN // 2 - run_length + 1)
    position = jnp.arange(LEN, dtype=jnp.int32)[None, :]
    inside_run = (position >= starts) & (position < starts + run_length)
    return jnp.where(inside_run | (coins >= 17), 0, 1).astype(jnp.int32)


def set_ends(values, key, least, high):
    place = [jax.random.randint(jax.random.fold_in(key, axis), (), 0, length) for axis, length in enumerate(values.shape)]
    main_axis = values.shape.index(max(values.shape))
    beside = place[:main_axis] + [(place[main_axis] + 1) % values.shape[main_axis]] + place[main_axis + 1:]
    return values.at[tuple(place)].set(least).at[tuple(beside)].set(high)


def block_levels(stream_key, extent, cuts, least, top_value):
    level, own = 1.0, jax.random.fold_in(stream_key, 6)
    for dim, blocks in cuts:
        steps = jnp.exp(jax.random.uniform(jax.random.fold_in(own, dim), (blocks,), jnp.float32, least / len(cuts), top_value / len(cuts)))
        level = level * jnp.repeat(steps, extent[dim] // blocks).reshape([-1 if axis == dim else 1 for axis in range(len(extent))])
    return level


def normal_values(key, dims, deviation, most, cuts=(), kind=jnp.bfloat16):
    values = deviation * jax.random.normal(key, dims, jnp.float32)
    if cuts:
        values = values * block_levels(key, dims, cuts, -0.22, 0.18)
    return jnp.clip(values, -most, most).astype(kind)


def setup_inputs(seed: int = 0) -> dict:
    arg_keys = jax.random.split(jax.random.key(seed), 21)
    tokens = draw_tokens(jax.random.fold_in(arg_keys[20], 71), 0)
    lengths = set_ends(jax.random.randint(arg_keys[1], (ITEMS,), LEN // 2, LEN + 1), jax.random.fold_in(arg_keys[1], 1), LEN // 2, LEN).astype(jnp.int32)
    keep = draw_keep(jax.random.fold_in(arg_keys[20], 71), 0)
    w_query = normal_values(arg_keys[3], (D, D), D ** -0.5, 0.21875, (), jnp.float32)
    b_query = normal_values(arg_keys[4], (D,), 0.5, 3.0, (), jnp.float32)
    w_key = normal_values(arg_keys[5], (D, D), D ** -0.5, 0.21875, (), jnp.float32)
    w_value = normal_values(arg_keys[6], (D, D), D ** -0.5, 0.21875, (), jnp.float32)
    b_value = normal_values(arg_keys[7], (D,), 0.5, 3.0, (), jnp.float32)
    conv_weight = normal_values(arg_keys[8], (HEADS, KERNEL), 0.08, 0.5, (), jnp.float32)
    w_out = normal_values(arg_keys[9], (D, D), (D // 4) ** -0.5, 0.4375, (), jnp.float32)
    b_out = normal_values(arg_keys[10], (D,), 0.3, 2.0, (), jnp.float32)
    gain_one = jnp.clip(1.0 + 0.1 * jax.random.normal(arg_keys[11], (D,), jnp.float32), 0.5, 1.5)
    shift_one = normal_values(arg_keys[12], (D,), 0.3, 2.0, (), jnp.float32)
    w_up = normal_values(arg_keys[13], (D, FF), D ** -0.5, 0.21875, (), jnp.float32)
    b_up = normal_values(arg_keys[14], (FF,), 0.3, 2.0, (), jnp.float32)
    w_down = normal_values(arg_keys[15], (FF, D), FF ** -0.5, 0.109375, (), jnp.float32)
    b_down = normal_values(arg_keys[16], (D,), 0.3, 2.0, (), jnp.float32)
    gain_two = jnp.clip(1.0 + 0.1 * jax.random.normal(arg_keys[17], (D,), jnp.float32), 0.5, 1.5)
    shift_two = normal_values(arg_keys[18], (D,), 0.3, 2.0, (), jnp.float32)
    cotangent = normal_values(arg_keys[19], (ITEMS, LEN, D), 1.0, 6.0, ((0, 4), (1, 8)), jnp.float32)
    return {"tokens": tokens, "lengths": lengths, "keep": keep, "w_query": w_query, "b_query": b_query, "w_key": w_key, "w_value": w_value, "b_value": b_value, "conv_weight": conv_weight, "w_out": w_out, "b_out": b_out, "gain_one": gain_one, "shift_one": shift_one, "w_up": w_up, "b_up": b_up, "w_down": w_down, "b_down": b_down, "gain_two": gain_two, "shift_two": shift_two, "cotangent": cotangent}


highest = lax.Precision.HIGHEST
epsilon = 1e-05

@jax.custom_vjp
def low(v):
    return lax.optimization_barrier(v.astype(jnp.bfloat16)).astype(jnp.float32)

@jax.custom_vjp
def low_back(v):
    return v

def low_keep(v):
    return (low(v), None)

def low_pass(kept, grad):
    return (grad,)

def back_keep(v):
    return (v, None)

def back_low(kept, grad):
    return (low(grad),)
low.defvjp(low_keep, low_pass)
low_back.defvjp(back_keep, back_low)

def newton(kernel):
    identity = jnp.eye(kernel.shape[-1], dtype=jnp.float32)
    approx = jnp.swapaxes(kernel, -1, -2) / lax.optimization_barrier(jnp.sum(kernel * kernel, axis=(-2, -1), keepdims=True))
    for iteration in range(NEWTON):
        product = jnp.einsum('...ij,...jk->...ik', kernel, approx, precision=highest)
        nested = 7.0 * identity - product
        nested = 15.0 * identity - jnp.einsum('...ij,...jk->...ik', product, nested, precision=highest)
        nested = 13.0 * identity - jnp.einsum('...ij,...jk->...ik', product, nested, precision=highest)
        approx = 0.25 * jnp.einsum('...ij,...jk->...ik', approx, nested, precision=highest)
    return approx

def normalize(inputs):
    center = inputs - lax.optimization_barrier(jnp.mean(inputs, axis=-1, keepdims=True))
    return center * lax.rsqrt(lax.optimization_barrier(jnp.mean(center * center, axis=-1, keepdims=True)) + epsilon)

def forward(tokens, params, usable, member):
    w_query, b_query, w_key, w_value, b_value, conv_weight, w_out, b_out, gain_one, shift_one, w_up, b_up, w_down, b_down, gain_two, shift_two = params
    length_all, width = tokens.shape
    heads, taps = conv_weight.shape
    head_size = width // heads
    margin = taps // 2
    factor = head_size ** (-0.25)
    queries = (jnp.dot(tokens, w_query, precision=highest) + b_query) * factor
    key_rows = jnp.dot(tokens, w_key, precision=highest) * factor
    values = jnp.dot(tokens, w_value, precision=highest) + b_value
    divisor = jnp.maximum(lax.optimization_barrier(jnp.sum(member, axis=0)), 1.0)[:, None]
    land_query = jnp.dot(member.T, queries, precision=highest) / divisor
    land_key = jnp.dot(member.T, key_rows, precision=highest) / divisor
    query_heads = queries.reshape(length_all, heads, head_size)
    key_heads = key_rows.reshape(length_all, heads, head_size)
    value_heads = values.reshape(length_all, heads, head_size)
    land_q = land_query.reshape(MARKS, heads, head_size)
    land_k = land_key.reshape(MARKS, heads, head_size)
    kernel_one = jax.nn.softmax(jnp.einsum('jhe,the->hjt', land_k, query_heads, precision=highest), axis=1)
    kernel_two = jax.nn.softmax(jnp.einsum('ihe,jhe->hij', land_q, land_k, precision=highest), axis=-1)
    scores_three = jnp.einsum('ihe,the->hit', land_q, key_heads, precision=highest)
    masked = jnp.where(usable[None, None, :] > 0, scores_three, -1e+30)
    largest = lax.optimization_barrier(jnp.max(masked, axis=-1, keepdims=True))
    weights = jnp.exp(masked - largest) * usable[None, None, :]
    kernel_three = weights / lax.optimization_barrier(jnp.sum(weights, axis=-1, keepdims=True))
    context = jnp.einsum('hit,the->hie', kernel_three, value_heads, precision=highest)
    inverse = newton(kernel_two)
    mixed_context = jnp.einsum('hij,hje->hie', inverse, context, precision=highest)
    nystrom = jnp.einsum('hjt,hje->the', kernel_one, mixed_context, precision=highest)
    masked_values = value_heads * usable[:, None, None]
    padded = jnp.pad(masked_values, ((margin, margin), (0, 0), (0, 0)))
    conv_out = jnp.zeros_like(masked_values)
    for tap_index in range(taps):
        conv_out = conv_out + conv_weight[:, tap_index][None, :, None] * padded[tap_index:tap_index + length_all]
    attn_input = (nystrom + conv_out).reshape(length_all, width)
    attention = jnp.dot(attn_input, w_out, precision=highest) + b_out
    hidden_one = normalize(tokens + attention) * gain_one + shift_one
    act_up = jax.nn.gelu(jnp.dot(hidden_one, w_up, precision=highest) + b_up, approximate=False)
    down_out = jnp.dot(act_up, w_down, precision=highest) + b_down
    return normalize(hidden_one + down_out) * gain_two + shift_two

def add_up(acc_one, acc_two):
    return acc_one + acc_two

def reference(tokens, lengths, keep, w_query, b_query, w_key, w_value, b_value, conv_weight, w_out, b_out, gain_one, shift_one, w_up, b_up, w_down, b_down, gain_two, shift_two, cotangent):
    params = (w_query, b_query, w_key, w_value, b_value, conv_weight, w_out, b_out, gain_one, shift_one, w_up, b_up, w_down, b_down, gain_two, shift_two)
    position = jnp.arange(LEN, dtype=jnp.int32)
    landmark_ids = jnp.arange(MARKS, dtype=jnp.int32)

    def one_item(totals, inputs):
        item_tokens, item_length, item_keep, item_cot = inputs
        inside = position < item_length
        usable = (inside & (item_keep > 0)).astype(jnp.float32)
        segment = jnp.where(inside, position * MARKS // item_length, MARKS).astype(jnp.int32)
        member = (segment[:, None] == landmark_ids[None, :]).astype(jnp.float32) * usable[:, None]

        def run_layer(layer_tokens, layer_params):
            return forward(layer_tokens, layer_params, usable, member)
        result, pullback = jax.vjp(run_layer, item_tokens, params)
        grad_item, grad_params = pullback(item_cot)
        totals = jax.tree.map(add_up, totals, grad_params)
        return (totals, (result, grad_item))
    zero_grads = jax.tree.map(jnp.zeros_like, params)
    totals, outputs = lax.scan(one_item, zero_grads, (tokens, lengths, keep, cotangent))
    output, grad_tokens = outputs
    return (output, grad_tokens, totals[0], totals[1], totals[2], totals[3], totals[4], totals[5], totals[6], totals[7], totals[8], totals[9], totals[10], totals[11], totals[12], totals[13], totals[14], totals[15])
```

```python
import functools

import jax
import jax.numpy as jnp
from jax import lax
from jax.experimental import pallas as pl
from jax.experimental.pallas import tpu as pltpu
from jax.sharding import PartitionSpec as P

MARKS = 64
NEWTON = 6
PAIR = 128
HIGH = lax.Precision.HIGH
epsilon = 1e-05
f32 = jnp.float32
bf16 = jnp.bfloat16
VM = pltpu.VMEM
LIMIT = 66 * 1024 * 1024


def split(x):
    hi = x.astype(bf16)
    return hi, (x - hi.astype(f32)).astype(bf16)


def dg(a, b, ca, cb):
    return lax.dot_general(a, b, (((ca,), (cb,)), ((), ())), preferred_element_type=f32)


def dots(a, b, ca, cb):
    return dg(a[0], b[0], ca, cb) + dg(a[0], b[1], ca, cb) + dg(a[1], b[0], ca, cb)


def dot3(a, b, ca=1, cb=0):
    return dots(split(a), split(b), ca, cb)


def lane_low(shape):
    return lax.broadcasted_iota(jnp.int32, shape, len(shape) - 1) < PAIR // 2


def spread(compact):
    low = lane_low(compact.shape)
    zero = jnp.zeros_like(compact)
    return jnp.concatenate([jnp.where(low, compact, zero), jnp.where(low, zero, compact)], axis=0)


def compacted(block):
    half = block.shape[0] // 2
    return jnp.where(lane_low((half, block.shape[1])), block[:half], block[half:])


def row_of(column):
    return jnp.transpose(jnp.broadcast_to(column, (PAIR, PAIR)))[0:1, :]


def column_of(row):
    return jnp.transpose(jnp.broadcast_to(row, (PAIR, PAIR)))


def diagonal_mask():
    rows = lax.broadcasted_iota(jnp.int32, (PAIR, PAIR), 0) < PAIR // 2
    return rows == lane_low((PAIR, PAIR))


def block_sum(x):
    halves = x.reshape(2, x.shape[0] // 2, x.shape[1])
    total = jnp.sum(halves, axis=1, keepdims=True)
    return jnp.broadcast_to(total, halves.shape).reshape(x.shape)


def block_max(x):
    halves = x.reshape(2, x.shape[0] // 2, x.shape[1])
    total = jnp.max(halves, axis=1, keepdims=True)
    return jnp.broadcast_to(total, halves.shape).reshape(x.shape)


def params(**more):
    return pltpu.CompilerParams(vmem_limit_bytes=LIMIT, **more)


def whole(shape):
    return pl.BlockSpec(shape, lambda *_: (0,) * len(shape))


def per_item(shape):
    return pl.BlockSpec((1,) + shape, lambda i, *_: (i,) + (0,) * len(shape))


def land_item(ref, item, me, into):
    rows = ref.shape[1]
    count = MARKS // rows
    for part in range(count):
        slot = jnp.bitwise_xor(item * count + part, me)
        into[part * rows : (part + 1) * rows, :] = ref[slot]


def scores_kernel(n, per, pairs, me_ref, q_ref, k_ref, v_ref, lq_ref, lk_ref, use_ref, *rest):
    k1_ref, w3_ref, top_ref = rest[:3]
    outs = rest[3 : 3 + n]
    lq_s, lk_s, chunk = rest[3 + n :]
    item = pl.program_id(0)
    me = me_ref[0]
    stats = per * MARKS

    @pl.when(item == 0)
    def _():
        chunk[...] = jnp.zeros_like(chunk)

    land_item(lq_ref, item, me, lq_s)
    land_item(lk_ref, item, me, lk_s)
    use = use_ref[0]
    for p in range(pairs):
        lanes = slice(p * PAIR, (p + 1) * PAIR)
        q = q_ref[0, :, lanes]
        s1 = dot3(spread(lk_s[:, lanes]), q, 1, 1)
        e1 = jnp.exp(s1 - block_max(s1))
        k1_ref[0, lanes, :] = e1 / block_sum(e1)
        s3 = dot3(spread(lq_s[:, lanes]), k_ref[0, :, lanes], 1, 1)
        masked = jnp.where(use > 0, s3, -1e30)
        top = jnp.max(masked, axis=1, keepdims=True)
        w3 = jnp.exp(masked - top) * use
        w3_ref[0, lanes, :] = w3
        total = jnp.sum(w3, axis=1, keepdims=True)
        weighted = compacted(dot3(w3, v_ref[0, :, lanes]))
        top_row = row_of(top)
        top_ref[0, p : p + 1, :] = top_row
        g = item * pairs + p
        owner, place = g // per, g % per
        chunk[owner, pl.ds(pl.multiple_of(place * MARKS, MARKS), MARKS), :] = weighted
        chunk[owner, pl.ds(stats + 2 * place, 1), :] = top_row
        chunk[owner, pl.ds(stats + 2 * place + 1, 1), :] = row_of(total)

    @pl.when(item == pl.num_programs(0) - 1)
    def _():
        for k in range(n):
            outs[k][...] = chunk[jnp.bitwise_xor(me, k)]


def scores_call(me, q, k, v, lq, lk, use_row, n, per, pairs, chunk_rows):
    items, span, width = q.shape
    out_shape = [
        jax.ShapeDtypeStruct((items, width, span), f32),
        jax.ShapeDtypeStruct((items, width, span), f32),
        jax.ShapeDtypeStruct((items, 8, PAIR), f32),
    ] + [jax.ShapeDtypeStruct((chunk_rows, PAIR), f32)] * n
    return pl.pallas_call(
        functools.partial(scores_kernel, n, per, pairs),
        out_shape=out_shape,
        grid_spec=pltpu.PrefetchScalarGridSpec(
            num_scalar_prefetch=1,
            grid=(items,),
            in_specs=[per_item((span, width))] * 3
            + [whole(lq.shape), whole(lk.shape), per_item((1, span))],
            out_specs=[per_item((width, span))] * 2
            + [per_item((8, PAIR))]
            + [whole((chunk_rows, PAIR))] * n,
            scratch_shapes=[
                VM((MARKS, width), f32),
                VM((MARKS, width), f32),
                VM((n, chunk_rows, PAIR), f32),
            ],
        ),
        compiler_params=params(),
        name="scores",
    )(me, q, k, v, lq, lk, use_row)


def owned_land(per, pairs, items, me, ref, into):
    rows = ref.shape[1]
    count = MARKS // rows
    for place in range(per):
        g = jnp.minimum(me * per + place, items * pairs - 1)
        item, p = g // pairs, g % pairs
        lanes = pl.ds(pl.multiple_of(p * PAIR, PAIR), PAIR)
        for part in range(count):
            slot = jnp.bitwise_xor(item * count + part, me)
            into[place, part * rows : (part + 1) * rows, :] = ref[slot, :, lanes]


def newton_step(a, z, eye):
    pr = dot3(a, z)
    n1 = 7.0 * eye - pr
    n2 = 15.0 * eye - dot3(pr, n1)
    n3 = 13.0 * eye - dot3(pr, n2)
    return pr, n1, n2, n3


def unit():
    rows = lax.broadcasted_iota(jnp.int32, (PAIR, PAIR), 0)
    return (rows == lax.broadcasted_iota(jnp.int32, (PAIR, PAIR), 1)).astype(f32)


def head_total(x):
    return block_sum(jnp.sum(x, axis=1, keepdims=True))


def newton_kernel(per, pairs, items, me_ref, lq_ref, lk_ref, a_ref, z_ref, lqo_ref, lko_ref):
    me = me_ref[0]
    owned_land(per, pairs, items, me, lq_ref, lqo_ref)
    owned_land(per, pairs, items, me, lk_ref, lko_ref)
    diagonal = diagonal_mask()
    eye = unit()
    for place in range(per):
        s2 = dot3(spread(lqo_ref[place]), spread(lko_ref[place]), 1, 1)
        s2 = jnp.where(diagonal, s2, -1e30)
        e2 = jnp.exp(s2 - jnp.max(s2, axis=1, keepdims=True))
        e2 = jnp.where(diagonal, e2, 0.0)
        a = e2 / jnp.sum(e2, axis=1, keepdims=True)
        a_ref[place] = a
        z_ref[0, place] = jnp.transpose(a) / head_total(a * a)

    def lap(step, _):
        for place in range(per):
            z = z_ref[step, place]
            _, _, _, n3 = newton_step(a_ref[place], z, eye)
            z_ref[step + 1, place] = 0.25 * dot3(z, n3)
        return 0

    lax.fori_loop(0, NEWTON, lap, 0)


def newton_call(me, lq, lk, per, pairs, items):
    small = jax.ShapeDtypeStruct((per, MARKS, PAIR), f32)
    square = jax.ShapeDtypeStruct((per, PAIR, PAIR), f32)
    steps = jax.ShapeDtypeStruct((NEWTON + 1, per, PAIR, PAIR), f32)
    return pl.pallas_call(
        functools.partial(newton_kernel, per, pairs, items),
        out_shape=[square, steps, small, small],
        in_specs=[
            pl.BlockSpec(memory_space=pltpu.SMEM),
            pl.BlockSpec(memory_space=VM),
            pl.BlockSpec(memory_space=VM),
        ],
        out_specs=[pl.BlockSpec(memory_space=VM)] * 4,
        compiler_params=params(),
        name="newton",
    )(me, lq, lk)


def context_kernel(n, per, *refs):
    chunks = refs[:n]
    z_ref, ctx_ref, out_ref = refs[n:]
    stats = per * MARKS
    out_ref[...] = jnp.zeros_like(out_ref)
    for place in range(per):
        tops = [c[stats + 2 * place : stats + 2 * place + 1, :] for c in chunks]
        largest = functools.reduce(jnp.maximum, tops)
        total = jnp.zeros_like(largest)
        weighted = jnp.zeros((MARKS, PAIR), f32)
        for k in range(n):
            scale = jnp.exp(tops[k] - largest)
            total = total + scale * chunks[k][stats + 2 * place + 1 : stats + 2 * place + 2, :]
            scales = compacted(column_of(scale))
            weighted = weighted + scales * chunks[k][place * MARKS : (place + 1) * MARKS, :]
        context = weighted / compacted(column_of(total))
        ctx_ref[place] = context
        mixed = dot3(z_ref[NEWTON, place], spread(context))
        out_ref[place * MARKS : (place + 1) * MARKS, :] = compacted(mixed)
        out_ref[stats + 2 * place : stats + 2 * place + 1, :] = largest
        out_ref[stats + 2 * place + 1 : stats + 2 * place + 2, :] = total


def context_call(chunks, z, per):
    rows = chunks[0].shape[0]
    n = len(chunks)
    return pl.pallas_call(
        functools.partial(context_kernel, n, per),
        out_shape=[
            jax.ShapeDtypeStruct((per, MARKS, PAIR), f32),
            jax.ShapeDtypeStruct((rows, PAIR), f32),
        ],
        in_specs=[pl.BlockSpec(memory_space=VM)] * (n + 1),
        out_specs=[pl.BlockSpec(memory_space=VM)] * 2,
        compiler_params=params(),
        name="context",
    )(*chunks, z)


def toeplitz(taps_row, rows):
    wide = jnp.broadcast_to(taps_row, (rows, 2 * PAIR))
    return pltpu.roll(wide, 0, 1, stride=1, stride_axis=0)


def keep_taps(taps_ref, into, heads):
    for h in range(heads):
        hi, lo = split(toeplitz(taps_ref[h : h + 1, :], PAIR))
        into[0, h] = hi
        into[1, h] = lo


def keep_window(win, left, middle, right, margin, span):
    for rows, part in (
        (slice(0, margin), left),
        (slice(margin, margin + span), middle),
        (slice(margin + span, 2 * margin + span), right),
    ):
        hi, lo = split(part)
        win[0, rows, :] = hi
        win[1, rows, :] = lo


def convolve(taps, win, p, block, window):
    lanes = slice(p * PAIR, (p + 1) * PAIR)
    rows = slice(block * PAIR, block * PAIR + window)
    v = (win[0, rows, lanes], win[1, rows, lanes])
    halves = []
    for h in (2 * p, 2 * p + 1):
        t = (taps[0, h, :, :window], taps[1, h, :, :window])
        halves.append(dots(t, v, 1, 0))
    return jnp.where(lane_low((PAIR, PAIR)), halves[0], halves[1])


def slot_of(g, per, me):
    return jnp.bitwise_xor(g // per, me), g % per


def mix_kernel(n, per, pairs, margin, me_ref, *refs):
    blocks = refs[:n]
    k1_ref, v_ref, use_ref, left_ref, right_ref, taps_ref, out_ref, held, taps, win = refs[n:]
    item = pl.program_id(0)
    me = me_ref[0]
    span = v_ref.shape[1]
    window = PAIR + 2 * margin

    @pl.when(item == 0)
    def _():
        for k in range(n):
            held[k] = blocks[k][...]
        keep_taps(taps_ref, taps, 2 * pairs)

    keep_window(win, left_ref[0], v_ref[0] * use_ref[0], right_ref[0], margin, span)
    for p in range(pairs):
        lanes = slice(p * PAIR, (p + 1) * PAIR)
        slot, place = slot_of(item * pairs + p, per, me)
        mixed = held[slot, pl.ds(pl.multiple_of(place * MARKS, MARKS), MARKS), :]
        nystrom = dot3(k1_ref[0, lanes, :], spread(mixed), 0, 0)
        for block in range(span // PAIR):
            rows = slice(block * PAIR, (block + 1) * PAIR)
            out_ref[0, rows, lanes] = nystrom[rows] + convolve(taps, win, p, block, window)


def mix_call(me, blocks, k1, v, use_col, left, right, taps, per, pairs, margin):
    items, span, width = v.shape
    n = len(blocks)
    rows = blocks[0].shape[0]
    return pl.pallas_call(
        functools.partial(mix_kernel, n, per, pairs, margin),
        out_shape=jax.ShapeDtypeStruct((items, span, width), f32),
        grid_spec=pltpu.PrefetchScalarGridSpec(
            num_scalar_prefetch=1,
            grid=(items,),
            in_specs=[whole((rows, PAIR))] * n
            + [per_item((width, span)), per_item((span, width)), per_item((span, 1))]
            + [per_item((margin, width))] * 2
            + [whole(taps.shape)],
            out_specs=per_item((span, width)),
            scratch_shapes=[
                VM((n, rows, PAIR), f32),
                VM((2, 2 * pairs, PAIR, 2 * PAIR), bf16),
                VM((2, span + 2 * margin, width), bf16),
            ],
        ),
        compiler_params=params(),
        name="mix",
    )(me, *blocks, k1, v, use_col, left, right, taps)


def erf(x):
    x = jnp.clip(x, -3.832506856900711, 3.832506856900711)
    s = x * x
    a = 0.00022905065861350646
    for c in (0.0034082910107109506, 0.050955695062380861, 0.18520832239976145, 1.128379143519084):
        a = a * s + c
    b = -1.1791602954361697e-7
    for c in (
        0.000023547966471313185,
        0.0010179625278914885,
        0.014070470171167667,
        0.11098505178285362,
        0.49746925110067538,
        1.0,
    ):
        b = b * s + c
    return x * a / b


def normalize(x):
    center = x - jnp.mean(x, axis=-1, keepdims=True)
    inv_root = lax.rsqrt(jnp.mean(center * center, axis=-1, keepdims=True) + epsilon)
    return center * inv_root, inv_root


def norm_back(grad, scaled, inv_root):
    first = jnp.mean(grad, axis=-1, keepdims=True)
    second = jnp.mean(grad * scaled, axis=-1, keepdims=True)
    return inv_root * (grad - first - scaled * second)


def rows_kernel(
    ff_tile,
    x_ref,
    tok_ref,
    cot_ref,
    wo_h,
    wo_l,
    wu_h,
    wu_l,
    wd_h,
    wd_l,
    vec_ref,
    bup_ref,
    out_ref,
    act_ref,
    u_ref,
    r2_ref,
    h1_ref,
    r1_ref,
    og_ref,
    sums_ref,
    bsum_ref,
    slope,
):
    @pl.when(pl.program_id(0) == 0)
    def _():
        sums_ref[...] = jnp.zeros_like(sums_ref)
        bsum_ref[...] = jnp.zeros_like(bsum_ref)

    b_out, gain_one, shift_one = vec_ref[0:1, :], vec_ref[1:2, :], vec_ref[2:3, :]
    b_down, gain_two, shift_two = vec_ref[3:4, :], vec_ref[4:5, :], vec_ref[5:6, :]
    wo = (wo_h[...], wo_l[...])
    attention = dots(split(x_ref[...]), wo, 1, 0) + b_out
    scaled_one, root_one = normalize(tok_ref[...] + attention)
    hidden = scaled_one * gain_one + shift_one
    h1_ref[...] = hidden
    hs = split(hidden)
    ff = wu_h.shape[1]
    tiles = [slice(c, c + ff_tile) for c in range(0, ff, ff_tile)]
    down = b_down
    for c in tiles:
        pre = dots(hs, (wu_h[:, c], wu_l[:, c]), 1, 0) + bup_ref[:, c]
        phi = 0.5 + 0.5 * erf(pre * 0.7071067811865476)
        slope[:, c] = phi + pre * (0.3989422804014327 * jnp.exp(-0.5 * pre * pre))
        act = pre * phi
        act_ref[:, c] = act
        down = down + dots(split(act), (wd_h[c, :], wd_l[c, :]), 1, 0)
    scaled_two, root_two = normalize(hidden + down)
    out_ref[...] = scaled_two * gain_two + shift_two
    cot = cot_ref[...]
    r2 = norm_back(cot * gain_two, scaled_two, root_two)
    r2_ref[...] = r2
    rs = split(r2)
    grad_hidden = r2
    for c in tiles:
        u = dots(rs, (wd_h[c, :], wd_l[c, :]), 1, 1) * slope[:, c]
        u_ref[:, c] = u
        bsum_ref[:, c] += jnp.sum(u, axis=0, keepdims=True)
        grad_hidden = grad_hidden + dots(split(u), (wu_h[:, c], wu_l[:, c]), 1, 1)
    r1 = norm_back(grad_hidden * gain_one, scaled_one, root_one)
    r1_ref[...] = r1
    og_ref[...] = dots(split(r1), wo, 1, 1)
    for row, value in enumerate(
        (cot * scaled_two, cot, r2, grad_hidden * scaled_one, grad_hidden, r1)
    ):
        sums_ref[row : row + 1, :] += jnp.sum(value, axis=0, keepdims=True)


def rows_call(x, tokens, cotangent, wo, wu, wd, vectors, b_up):
    rows, width = x.shape
    ff = wu[0].shape[1]
    tile = 256
    ff_tile = 768
    wide = pl.BlockSpec((tile, width), lambda i: (i, 0))
    hidden = pl.BlockSpec((tile, ff), lambda i: (i, 0))

    def fixed(a):
        return pl.BlockSpec(a.shape, lambda i: (0, 0), pipeline_mode=pl.Buffered(1))

    narrow = jax.ShapeDtypeStruct((rows, width), f32)
    broad = jax.ShapeDtypeStruct((rows, ff), f32)
    return pl.pallas_call(
        functools.partial(rows_kernel, ff_tile),
        out_shape=[
            narrow,
            broad,
            broad,
            narrow,
            narrow,
            narrow,
            narrow,
            jax.ShapeDtypeStruct((8, width), f32),
            jax.ShapeDtypeStruct((1, ff), f32),
        ],
        grid=(rows // tile,),
        in_specs=[wide] * 3
        + [fixed(a) for a in (*wo, *wu, *wd)]
        + [fixed(vectors), fixed(b_up)],
        out_specs=[wide, hidden, hidden, wide, wide, wide, wide]
        + [pl.BlockSpec((8, width), lambda i: (0, 0)), pl.BlockSpec((1, ff), lambda i: (0, 0))],
        scratch_shapes=[VM((tile, ff), f32)],
        compiler_params=params(),
        name="rows",
    )(x, tokens, cotangent, *wo, *wu, *wd, vectors, b_up)


def one_back_kernel(n, per, pairs, me_ref, *refs):
    blocks = refs[:n]
    k1_ref, og_ref, q_ref, lk_ref = refs[n : n + 4]
    gq_ref = refs[n + 4]
    outs = refs[n + 5 : 2 * n + 5]
    held, lk_s, chunk = refs[2 * n + 5 :]
    item = pl.program_id(0)
    me = me_ref[0]

    @pl.when(item == 0)
    def _():
        chunk[...] = jnp.zeros_like(chunk)
        for k in range(n):
            held[k] = blocks[k][...]

    land_item(lk_ref, item, me, lk_s)
    for p in range(pairs):
        lanes = slice(p * PAIR, (p + 1) * PAIR)
        g = item * pairs + p
        slot, place = slot_of(g, per, me)
        mixed = spread(held[slot, pl.ds(pl.multiple_of(place * MARKS, MARKS), MARKS), :])
        k1 = k1_ref[0, lanes, :]
        og = split(og_ref[0, :, lanes])
        part_mixed = compacted(dots(split(k1), og, 1, 0))
        grad = dots(split(mixed), og, 1, 1)
        scores = k1 * (grad - block_sum(k1 * grad))
        ss = split(scores)
        gq_ref[0, :, lanes] = dots(ss, split(spread(lk_s[:, lanes])), 0, 0)
        part_key = compacted(dots(ss, split(q_ref[0, :, lanes]), 1, 0))
        owner = g // per
        chunk[owner, pl.ds(pl.multiple_of(place * 2 * MARKS, 2 * MARKS), MARKS), :] = part_mixed
        chunk[owner, pl.ds(pl.multiple_of(place * 2 * MARKS + MARKS, MARKS), MARKS), :] = part_key

    @pl.when(item == pl.num_programs(0) - 1)
    def _():
        for k in range(n):
            outs[k][...] = chunk[jnp.bitwise_xor(me, k)]


def one_back_call(me, blocks, k1, og, q, lk, per, pairs):
    items, span, width = q.shape
    n = len(blocks)
    rows = blocks[0].shape[0]
    out_rows = 2 * per * MARKS
    return pl.pallas_call(
        functools.partial(one_back_kernel, n, per, pairs),
        out_shape=[jax.ShapeDtypeStruct((items, span, width), f32)]
        + [jax.ShapeDtypeStruct((out_rows, PAIR), f32)] * n,
        grid_spec=pltpu.PrefetchScalarGridSpec(
            num_scalar_prefetch=1,
            grid=(items,),
            in_specs=[whole((rows, PAIR))] * n
            + [per_item((width, span)), per_item((span, width)), per_item((span, width))]
            + [whole(lk.shape)],
            out_specs=[per_item((span, width))] + [whole((out_rows, PAIR))] * n,
            scratch_shapes=[
                VM((n, rows, PAIR), f32),
                VM((MARKS, width), f32),
                VM((n, out_rows, PAIR), f32),
            ],
        ),
        compiler_params=params(),
        name="one_back",
    )(me, *blocks, k1, og, q, lk)


def conv_back_kernel(pairs, margin, og_ref, gl_ref, gr_ref, v_ref, vl_ref, vr_ref, use_ref, taps_ref, *refs):
    gv_ref, gtaps_ref, taps, gwin, vwin, acc = refs
    item = pl.program_id(0)
    span = v_ref.shape[1]
    window = PAIR + 2 * margin

    @pl.when(item == 0)
    def _():
        keep_taps(taps_ref, taps, 2 * pairs)
        acc[...] = jnp.zeros_like(acc)

    use = use_ref[0]
    keep_window(gwin, gl_ref[0], og_ref[0], gr_ref[0], margin, span)
    keep_window(vwin, vl_ref[0], v_ref[0] * use, vr_ref[0], margin, span)
    for p in range(pairs):
        lanes = slice(p * PAIR, (p + 1) * PAIR)
        for block in range(span // PAIR):
            rows = slice(block * PAIR, (block + 1) * PAIR)
            gv_ref[0, rows, lanes] = convolve(taps, gwin, p, block, window) * use[rows]
            inner = slice(margin + block * PAIR, margin + (block + 1) * PAIR)
            outer = slice(block * PAIR, block * PAIR + window)
            v = (vwin[0, outer, lanes], vwin[1, outer, lanes])
            low = lane_low((PAIR, PAIR))
            hi, lo = gwin[0, inner, lanes], gwin[1, inner, lanes]
            zero = jnp.zeros_like(hi)
            acc[2 * p] += dots((jnp.where(low, hi, zero), jnp.where(low, lo, zero)), v, 1, 1)
            acc[2 * p + 1] += dots((jnp.where(low, zero, hi), jnp.where(low, zero, lo)), v, 1, 1)

    @pl.when(item == pl.num_programs(0) - 1)
    def _():
        rows = lax.broadcasted_iota(jnp.int32, (PAIR, PAIR), 0)
        flip = (rows + lax.broadcasted_iota(jnp.int32, (PAIR, PAIR), 1) == PAIR - 1).astype(bf16)
        for h in range(2 * pairs):
            c = acc[h]
            c = jnp.concatenate([c, jnp.zeros((PAIR, 2 * PAIR - window), f32)], axis=1)
            hi = c.astype(bf16)
            rest = c - hi.astype(f32)
            mid = rest.astype(bf16)
            low = (rest - mid.astype(f32)).astype(bf16)
            c = dg(flip, hi, 1, 0) + dg(flip, mid, 1, 0) + dg(flip, low, 1, 0)
            c = pltpu.roll(c, 0, 1, stride=1, stride_axis=0)
            gtaps_ref[h : h + 1, :] = jnp.sum(c, axis=0, keepdims=True)


def conv_back_call(og, gleft, gright, v, vleft, vright, use_col, taps, pairs, margin):
    items, span, width = v.shape
    window = PAIR + 2 * margin
    wide, edge = per_item((span, width)), per_item((margin, width))
    rows = -(-2 * pairs // 8) * 8
    return pl.pallas_call(
        functools.partial(conv_back_kernel, pairs, margin),
        out_shape=[
            jax.ShapeDtypeStruct((items, span, width), f32),
            jax.ShapeDtypeStruct((rows, 2 * PAIR), f32),
        ],
        grid=(items,),
        in_specs=[wide, edge, edge, wide, edge, edge, per_item((span, 1)), whole(taps.shape)],
        out_specs=[wide, whole((rows, 2 * PAIR))],
        scratch_shapes=[
            VM((2, 2 * pairs, PAIR, 2 * PAIR), bf16),
            VM((2, span + 2 * margin, width), bf16),
            VM((2, span + 2 * margin, width), bf16),
            VM((2 * pairs, PAIR, window), f32),
        ],
        compiler_params=params(),
        name="conv_back",
    )(og, gleft, gright, v, vleft, vright, use_col, taps)


def context_back_kernel(n, per, *refs):
    chunks = refs[:n]
    z_ref, ctx_ref, out_ref, gm_ref, key_ref = refs[n:]
    stats = per * MARKS
    out_ref[...] = jnp.zeros_like(out_ref)
    for place in range(per):
        rows = slice(place * 2 * MARKS, place * 2 * MARKS + MARKS)
        more = slice(place * 2 * MARKS + MARKS, (place + 1) * 2 * MARKS)
        mixed = sum(c[rows, :] for c in chunks)
        gm_ref[place] = mixed
        key_ref[place] = sum(c[more, :] for c in chunks)
        grad = dot3(jnp.transpose(z_ref[NEWTON, place]), spread(mixed))
        out_ref[place * MARKS : (place + 1) * MARKS, :] = compacted(grad)
        dot = jnp.sum(grad * spread(ctx_ref[place]), axis=1, keepdims=True)
        out_ref[stats + place : stats + place + 1, :] = row_of(dot)


def context_back_call(chunks, z, ctx, per, rows):
    n = len(chunks)
    small = jax.ShapeDtypeStruct((per, MARKS, PAIR), f32)
    return pl.pallas_call(
        functools.partial(context_back_kernel, n, per),
        out_shape=[jax.ShapeDtypeStruct((rows, PAIR), f32), small, small],
        in_specs=[pl.BlockSpec(memory_space=VM)] * (n + 2),
        out_specs=[pl.BlockSpec(memory_space=VM)] * 3,
        compiler_params=params(),
        name="context_back",
    )(*chunks, z, ctx)


def newton_back_kernel(per, gm_ref, key_ref, ctx_ref, a_ref, z_ref, lq_ref, lk_ref, gq_ref, gk_ref, gz, ga):
    diagonal = diagonal_mask()
    eye = unit()
    for place in range(per):
        start = dot3(spread(gm_ref[place]), spread(ctx_ref[place]), 1, 1)
        gz[place] = jnp.where(diagonal, start, 0.0)
        ga[place] = jnp.zeros((PAIR, PAIR), f32)

    def lap(back, _):
        step = NEWTON - 1 - back
        for place in range(per):
            a, z, g = a_ref[place], z_ref[step, place], 0.25 * gz[place]
            pr, n1, n2, n3 = newton_step(a, z, eye)
            back_three = dot3(jnp.transpose(z), g)
            turned = jnp.transpose(pr)
            back_two = -dot3(turned, back_three)
            back_one = -dot3(turned, back_two)
            grad = -dot3(back_three, n2, 1, 1) - dot3(back_two, n1, 1, 1) - back_one
            ga[place] += dot3(grad, z, 1, 1)
            gz[place] = dot3(g, n3, 1, 1) + dot3(jnp.transpose(a), grad)
        return 0

    lax.fori_loop(0, NEWTON, lap, 0)
    for place in range(per):
        a, g = a_ref[place], jnp.transpose(gz[place])
        norm = head_total(a * a)
        slope = -head_total(g * a) / (norm * norm)
        grad = ga[place] + g / norm + 2.0 * slope * a
        scores = a * (grad - jnp.sum(a * grad, axis=1, keepdims=True))
        gq_ref[place] = compacted(dot3(scores, spread(lk_ref[place])))
        gk_ref[place] = key_ref[place] + compacted(
            dot3(jnp.transpose(scores), spread(lq_ref[place]))
        )


def newton_back_call(gm, key, ctx, a, z, lq, lk):
    per = gm.shape[0]
    small = jax.ShapeDtypeStruct(gm.shape, f32)
    return pl.pallas_call(
        functools.partial(newton_back_kernel, per),
        out_shape=[small, small],
        in_specs=[pl.BlockSpec(memory_space=VM)] * 7,
        out_specs=[pl.BlockSpec(memory_space=VM)] * 2,
        scratch_shapes=[VM((per, PAIR, PAIR), f32)] * 2,
        compiler_params=params(),
        name="newton_back",
    )(gm, key, ctx, a, z, lq, lk)


def three_back_kernel(n, per, pairs, me_ref, *refs):
    grads, blocks = refs[:n], refs[n : 2 * n]
    w3_ref, top_ref, v_ref, k_ref, gvc_ref, lq_ref = refs[2 * n : 2 * n + 6]
    gv_ref, gk_ref = refs[2 * n + 6 : 2 * n + 8]
    outs = refs[2 * n + 8 : 3 * n + 8]
    held, stat, lq_s, chunk = refs[3 * n + 8 :]
    item = pl.program_id(0)
    me = me_ref[0]
    stats = per * MARKS

    @pl.when(item == 0)
    def _():
        chunk[...] = jnp.zeros_like(chunk)
        for k in range(n):
            held[k] = grads[k][...]
            stat[k] = blocks[k][stats:, :]

    land_item(lq_ref, item, me, lq_s)
    for p in range(pairs):
        lanes = slice(p * PAIR, (p + 1) * PAIR)
        g = item * pairs + p
        slot, place = slot_of(g, per, me)
        grad = split(spread(held[slot, pl.ds(pl.multiple_of(place * MARKS, MARKS), MARKS), :]))
        row_dot = column_of(held[slot, pl.ds(stats + place, 1), :])
        largest = stat[slot, pl.ds(2 * place, 1), :]
        total = stat[slot, pl.ds(2 * place + 1, 1), :]
        scale = column_of(jnp.exp(top_ref[0, p : p + 1, :] - largest) / total)
        k3 = w3_ref[0, lanes, :] * scale[:, 0:1]
        gk3 = dots(grad, split(v_ref[0, :, lanes]), 1, 1)
        scores = split(k3 * (gk3 - row_dot[:, 0:1]))
        gv_ref[0, :, lanes] = gvc_ref[0, :, lanes] + dots(split(k3), grad, 0, 0)
        gk_ref[0, :, lanes] = dots(scores, split(spread(lq_s[:, lanes])), 0, 0)
        part = compacted(dots(scores, split(k_ref[0, :, lanes]), 1, 0))
        chunk[g // per, pl.ds(pl.multiple_of(place * MARKS, MARKS), MARKS), :] = part

    @pl.when(item == pl.num_programs(0) - 1)
    def _():
        for k in range(n):
            outs[k][...] = chunk[jnp.bitwise_xor(me, k)]


def three_back_call(me, grads, blocks, w3, top, v, k, gv_conv, lq, per, pairs):
    items, span, width = v.shape
    n = len(blocks)
    rows = blocks[0].shape[0]
    stats = per * MARKS
    wide = per_item((span, width))
    shape = jax.ShapeDtypeStruct((items, span, width), f32)
    return pl.pallas_call(
        functools.partial(three_back_kernel, n, per, pairs),
        out_shape=[shape, shape] + [jax.ShapeDtypeStruct((stats, PAIR), f32)] * n,
        grid_spec=pltpu.PrefetchScalarGridSpec(
            num_scalar_prefetch=1,
            grid=(items,),
            in_specs=[whole((rows, PAIR))] * (2 * n)
            + [per_item((width, span)), per_item((8, PAIR)), wide, wide, wide, whole(lq.shape)],
            out_specs=[wide, wide] + [whole((stats, PAIR))] * n,
            scratch_shapes=[
                VM((n, rows, PAIR), f32),
                VM((n, rows - stats, PAIR), f32),
                VM((MARKS, width), f32),
                VM((n, stats, PAIR), f32),
            ],
        ),
        compiler_params=params(),
        name="three_back",
    )(me, *grads, *blocks, w3, top, v, k, gv_conv, lq)


def land_back_kernel(n, per, pairs, factor, me_ref, *refs):
    blocks = refs[:n]
    gq_ref, gk_ref, gv_ref, mem_ref, inv_ref = refs[n : n + 5]
    oq_ref, ok_ref, sums_ref, held, inv_s = refs[n + 5 :]
    item = pl.program_id(0)
    me = me_ref[0]
    half = per * MARKS

    @pl.when(item == 0)
    def _():
        sums_ref[...] = jnp.zeros_like(sums_ref)
        for k in range(n):
            held[k] = blocks[k][...]

    land_item(inv_ref, item, me, inv_s)
    member = mem_ref[0].astype(bf16)
    inv = inv_s[...]
    for p in range(pairs):
        lanes = slice(p * PAIR, (p + 1) * PAIR)
        slot, place = slot_of(item * pairs + p, per, me)
        for ref, out, base in ((gq_ref, oq_ref, 0), (gk_ref, ok_ref, half)):
            grad = held[slot, pl.ds(pl.multiple_of(base + place * MARKS, MARKS), MARKS), :]
            hi, lo = split(grad * inv)
            landed = dg(member, hi, 0, 0) + dg(member, lo, 0, 0)
            out[0, :, lanes] = (ref[0, :, lanes] + landed) * factor
        sums_ref[0:1, lanes] += jnp.sum(oq_ref[0, :, lanes], axis=0, keepdims=True)
        sums_ref[1:2, lanes] += jnp.sum(gv_ref[0, :, lanes], axis=0, keepdims=True)


def land_back_call(me, blocks, gq, gk, gv, member_t, inv, per, pairs, factor):
    items, span, width = gq.shape
    n = len(blocks)
    rows = blocks[0].shape[0]
    wide = per_item((span, width))
    shape = jax.ShapeDtypeStruct((items, span, width), f32)
    return pl.pallas_call(
        functools.partial(land_back_kernel, n, per, pairs, factor),
        out_shape=[shape, shape, jax.ShapeDtypeStruct((8, width), f32)],
        grid_spec=pltpu.PrefetchScalarGridSpec(
            num_scalar_prefetch=1,
            grid=(items,),
            in_specs=[whole((rows, PAIR))] * n
            + [wide, wide, wide, per_item((MARKS, span)), whole(inv.shape)],
            out_specs=[wide, wide, whole((8, width))],
            scratch_shapes=[VM((n, rows, PAIR), f32), VM((MARKS, PAIR), f32)],
        ),
        compiler_params=params(),
        name="land_back",
    )(me, *blocks, gq, gk, gv, member_t, inv)


def swap(x, axis, offset):
    count = lax.axis_size(axis)
    return lax.ppermute(x, axis, [(i, i ^ offset) for i in range(count)])


def exchange(chunks):
    return [chunks[0]] + [swap(chunks[k], "seq", k) for k in range(1, len(chunks))]


def gathered(x):
    count = lax.axis_size("seq")
    slots = [None] * count
    for k in range(0, count, 2):
        slots[k] = swap(x, "seq", k) if k else x
    for k in range(0, count, 2):
        slots[k + 1] = swap(slots[k], "seq", 1)
    return slots


def edges(x, margin):
    count = lax.axis_size("seq")
    left = lax.ppermute(x[:, -margin:], "seq", [(i, i + 1) for i in range(count - 1)])
    right = lax.ppermute(x[:, :margin], "seq", [(i + 1, i) for i in range(count - 1)])
    return left, right


def bit_of(axis, bit):
    return lax.axis_index(axis) // bit % 2


def halve_rows(x, bit):
    blocks, rows, columns = x.shape
    y = x.reshape(blocks // 2, 2, rows, columns)
    mine = bit_of("seq", bit)
    keep = lax.dynamic_index_in_dim(y, mine, 1, False)
    send = lax.dynamic_index_in_dim(y, 1 - mine, 1, False)
    return keep + swap(send, "seq", bit)


def halve_columns(x, bits, bit):
    mine = bit_of("dp", bit)
    columns = x.shape[2]
    groups = 2 ** bits.index(bit)
    size = columns // (2 * groups)

    def pick(which):
        parts = [
            lax.dynamic_slice_in_dim(x, 2 * g * size + which * size, size, 2)
            for g in range(groups)
        ]
        return parts[0] if groups == 1 else jnp.concatenate(parts, axis=2)

    return pick(mine) + swap(pick(1 - mine), "dp", bit)


def powers(axis):
    count = lax.axis_size(axis)
    return [2**i for i in range(count.bit_length() - 1)]


def scatter_sum(x, order):
    seq_bits, dp_bits = powers("seq"), powers("dp")[::-1]
    count = lax.axis_size("seq")
    x = x.reshape(count, x.shape[0] // count, x.shape[1])
    x = halve_rows(x, seq_bits.pop(0))
    for axis in order:
        if axis == "z" and seq_bits:
            x = halve_rows(x, seq_bits.pop(0))
        elif axis in "xy" and dp_bits:
            half = len(powers("dp")) // 2
            low = [b for b in dp_bits if b < 2**half]
            high = [b for b in dp_bits if b >= 2**half]
            chosen = (low if axis == "x" else high) or dp_bits
            x = halve_columns(x, dp_bits, chosen[0])
            dp_bits.remove(chosen[0])
    while seq_bits:
        x = halve_rows(x, seq_bits.pop(0))
    while dp_bits:
        x = halve_columns(x, dp_bits, dp_bits[0])
        dp_bits.pop(0)
    return x[0]


def sum_everywhere(x):
    for axis in ("seq", "dp"):
        for bit in powers(axis):
            x = x + swap(x, axis, bit)
    return x


def rounded_pair(w):
    hi = lax.reduce_precision(w, 8, 7)
    return hi.astype(bf16), (w - hi).astype(bf16)


def product(a, b, ca, cb):
    return lax.dot_general(a, b, (((ca,), (cb,)), ((), ())), precision=HIGH)


def on_device(
    tokens,
    lengths,
    keep,
    w_query,
    b_query,
    w_key,
    w_value,
    b_value,
    conv_weight,
    w_out,
    b_out,
    gain_one,
    shift_one,
    w_up,
    b_up,
    w_down,
    b_down,
    gain_two,
    shift_two,
    cotangent,
):
    items, span, width = tokens.shape
    heads, taps = conv_weight.shape
    head_size = width // heads
    margin = taps // 2
    factor = head_size ** (-0.25)
    pairs = heads // 2
    n = lax.axis_size("seq")
    per = -(-items * pairs // n)
    chunk_rows = per * MARKS + 8
    me_index = lax.axis_index("seq")
    me = me_index.astype(jnp.int32).reshape(1)
    position = me_index * span + jnp.arange(span, dtype=jnp.int32)
    inside = position[None, :] < lengths[:, None]
    usable = (inside & (keep > 0)).astype(f32)
    use_row, use_col = usable[:, None, :], usable[:, :, None]
    segment = jnp.where(inside, position[None, :] * MARKS // lengths[:, None], MARKS)
    marks = jnp.arange(MARKS, dtype=jnp.int32)
    member_t = (segment[:, None, :] == marks[None, :, None]).astype(f32) * use_row

    sums = jnp.einsum("imt,itd->imd", member_t, tokens, precision=HIGH)
    counts = jnp.broadcast_to(jnp.sum(member_t, axis=2, keepdims=True), (items, MARKS, PAIR))
    sums = jnp.concatenate([sums, counts], axis=2).reshape(n, items * MARKS // n, width + PAIR)
    parts = [lax.dynamic_index_in_dim(sums, me_index ^ k, 0, False) for k in range(n)]
    land = jnp.stack(gathered(sum(exchange(parts))))
    divisor = jnp.maximum(land[:, :, width:], 1.0)
    inverse_divisor = 1.0 / divisor
    filled = land[:, :, width : width + 1] / divisor[:, :, :1]
    land_tokens = (land[:, :, :width] / divisor[:, :, :1]).reshape(items * MARKS, width)
    land_q = product(land_tokens, w_query, 1, 0).reshape(n, -1, width)
    land_q = (land_q + filled * b_query) * factor
    land_k = product(land_tokens, w_key, 1, 0).reshape(n, -1, width) * factor

    rows = tokens.reshape(items * span, width)
    values = (product(rows, w_value, 1, 0) + b_value).reshape(items, span, width)
    queries = ((product(rows, w_query, 1, 0) + b_query) * factor).reshape(items, span, width)
    key_rows = (product(rows, w_key, 1, 0) * factor).reshape(items, span, width)
    vleft, vright = edges(values * use_col, margin)
    taps_forward = jnp.pad(conv_weight, ((0, 4), (0, 2 * PAIR - taps)))
    taps_backward = jnp.pad(conv_weight[:, ::-1], ((0, 4), (0, 2 * PAIR - taps)))

    k1, w3, top, *chunks = scores_call(
        me, queries, key_rows, values, land_q, land_k, use_row, n, per, pairs, chunk_rows
    )
    chunks = exchange(chunks)
    kernel_two, z, owned_q, owned_k = newton_call(me, land_q, land_k, per, pairs, items)
    context, mixed = context_call(chunks, z, per)
    mixed = gathered(mixed)
    attn_input = mix_call(
        me, mixed, k1, values, use_col, vleft, vright, taps_forward, per, pairs, margin
    )

    vectors = jnp.stack(
        [b_out, gain_one, shift_one, b_down, gain_two, shift_two, b_out, b_out]
    )
    x = attn_input.reshape(items * span, width)
    output, act, u, r2, hidden, r1, og, row_sums, up_sums = rows_call(
        x,
        rows,
        cotangent.reshape(items * span, width),
        rounded_pair(w_out),
        rounded_pair(w_up),
        rounded_pair(w_down),
        vectors,
        b_up[None, :],
    )
    og = og.reshape(items, span, width)
    gleft, gright = edges(og, margin)
    grad_queries, *chunks = one_back_call(me, mixed, k1, og, queries, land_k, per, pairs)
    chunks = exchange(chunks)

    grad_w_down = scatter_sum(product(r2, act, 0, 0), "yxzz")
    grad_w_up = scatter_sum(product(u, hidden, 0, 0), "xzyz")
    grad_w_out = scatter_sum(product(r1, x, 0, 0), "zyxz")
    gv_conv, grad_taps = conv_back_call(
        og, gleft, gright, values, vleft, vright, use_col, taps_backward, pairs, margin
    )

    grad_context, grad_mixed, part_key = context_back_call(chunks, z, context, per, chunk_rows)
    grad_context = gathered(grad_context)
    own_q, own_k = newton_back_call(
        grad_mixed, part_key, context, kernel_two, z, owned_q, owned_k
    )
    grad_values, grad_keys, *chunks = three_back_call(
        me, grad_context, mixed, w3, top, values, key_rows, gv_conv, land_q, per, pairs
    )
    own_q = own_q.reshape(per * MARKS, PAIR) + sum(exchange(chunks))
    land_grads = gathered(jnp.concatenate([own_q, own_k.reshape(per * MARKS, PAIR)]))
    grad_queries, grad_keys, late_sums = land_back_call(
        me, land_grads, grad_queries, grad_keys, grad_values, member_t, inverse_divisor,
        per, pairs, factor,
    )
    grad_queries = grad_queries.reshape(items * span, width)
    grad_keys = grad_keys.reshape(items * span, width)
    grad_values = grad_values.reshape(items * span, width)
    grad_w_value = scatter_sum(product(grad_values, rows, 0, 0), "zyxz")
    grad_w_query = scatter_sum(product(grad_queries, rows, 0, 0), "yxzz")
    grad_w_key = scatter_sum(product(grad_keys, rows, 0, 0), "xzyz")
    grad_tokens = (
        r1
        + product(grad_values, w_value, 1, 1)
        + product(grad_queries, w_query, 1, 1)
        + product(grad_keys, w_key, 1, 1)
    )

    early = sum_everywhere(
        jnp.concatenate([row_sums.reshape(-1), up_sums.reshape(-1), grad_taps.reshape(-1)]).reshape(
            -1, PAIR
        )
    ).reshape(-1)
    late = sum_everywhere(late_sums)
    row_sums = early[: 8 * width].reshape(8, width)
    ff = w_up.shape[1]
    up_sums = early[8 * width : 8 * width + ff]
    grad_taps = early[8 * width + ff :].reshape(-1, 2 * PAIR)
    grad_conv = grad_taps[:heads, PAIR - 1 : PAIR - 1 + taps]
    return (
        output.reshape(tokens.shape),
        grad_tokens.reshape(tokens.shape),
        grad_w_query.T,
        late[0],
        grad_w_key.T,
        grad_w_value.T,
        late[1],
        grad_conv,
        grad_w_out.T,
        row_sums[5],
        row_sums[3],
        row_sums[4],
        grad_w_up.T,
        up_sums,
        grad_w_down.T,
        row_sums[2],
        row_sums[0],
        row_sums[1],
    )


def solution(mesh):
    rows = P("dp", "seq", None)
    block = P("dp", "seq")
    in_specs = (rows, P("dp"), block) + (P(),) * 16 + (rows,)
    out_specs = (
        rows, rows, block, P(), block, block, P(), P(), block,
        P(), P(), P(), block, P(), block, P(), P(), P(),
    )
    return jax.shard_map(
        on_device, mesh=mesh, in_specs=in_specs, out_specs=out_specs, check_vma=False
    )
```

```python
import functools

import jax
import jax.numpy as jnp
from jax import lax
from jax.experimental import pallas as pl
from jax.experimental.pallas import tpu as pltpu
from jax.sharding import PartitionSpec as P

MARKS = 64
NEWTON = 6
PAIR = 128
HIGH = lax.Precision.HIGH
epsilon = 1e-05
f32 = jnp.float32
bf16 = jnp.bfloat16
VM = pltpu.VMEM
LIMIT = 66 * 1024 * 1024


def split(x):
    hi = x.astype(bf16)
    return hi, (x - hi.astype(f32)).astype(bf16)


def dg(a, b, ca, cb):
    return lax.dot_general(a, b, (((ca,), (cb,)), ((), ())), preferred_element_type=f32)


def dots(a, b, ca, cb):
    return dg(a[0], b[0], ca, cb) + dg(a[0], b[1], ca, cb) + dg(a[1], b[0], ca, cb)


def dot3(a, b, ca=1, cb=0):
    return dots(split(a), split(b), ca, cb)


def lane_low(shape):
    return lax.broadcasted_iota(jnp.int32, shape, len(shape) - 1) < PAIR // 2


def spread(compact):
    low = lane_low(compact.shape)
    zero = jnp.zeros_like(compact)
    return jnp.concatenate([jnp.where(low, compact, zero), jnp.where(low, zero, compact)], axis=0)


def compacted(block):
    half = block.shape[0] // 2
    return jnp.where(lane_low((half, block.shape[1])), block[:half], block[half:])


def row_of(column):
    return jnp.transpose(jnp.broadcast_to(column, (PAIR, PAIR)))[0:1, :]


def column_of(row):
    return jnp.transpose(jnp.broadcast_to(row, (PAIR, PAIR)))


def diagonal_mask():
    rows = lax.broadcasted_iota(jnp.int32, (PAIR, PAIR), 0) < PAIR // 2
    return rows == lane_low((PAIR, PAIR))


def block_sum(x):
    halves = x.reshape(2, x.shape[0] // 2, x.shape[1])
    total = jnp.sum(halves, axis=1, keepdims=True)
    return jnp.broadcast_to(total, halves.shape).reshape(x.shape)


def block_max(x):
    halves = x.reshape(2, x.shape[0] // 2, x.shape[1])
    total = jnp.max(halves, axis=1, keepdims=True)
    return jnp.broadcast_to(total, halves.shape).reshape(x.shape)


def params(**more):
    return pltpu.CompilerParams(vmem_limit_bytes=LIMIT, **more)


def whole(shape):
    return pl.BlockSpec(shape, lambda *_: (0,) * len(shape))


def per_item(shape):
    return pl.BlockSpec((1,) + shape, lambda i, *_: (i,) + (0,) * len(shape))


class Seat:
    def __init__(self, n):
        self.n, self.nz = n, n // 2
        self.me = lax.axis_index("seq")
        self.core = lax.rem(self.me, 2)
        self.z = self.me // 2
        self.owner = self.core * self.nz + self.z
        self.partner = self.me + 1 - 2 * self.core
        self.extra = lax.rem(self.me + 2 * self.core - 1 + n, n)

    def ahead(self, j):
        return lax.rem(self.z + j, self.nz)

    def behind(self, j):
        return lax.rem(self.z - j + self.nz, self.nz)

    def at(self, z):
        return 2 * z + self.core

    def hello(self, edges):
        others = [self.partner] + [self.at(self.ahead(j)) for j in range(1, self.nz)]
        if edges:
            others.append(self.extra)
        barrier = pltpu.get_barrier_semaphore()
        for other in others:
            pl.semaphore_signal(barrier, inc=1, device_id={"seq": other}, device_id_type=MESH)
        pl.semaphore_wait(barrier, len(others))


MESH = pl.DeviceIdType.MESH


def remote(src, dst, send, recv, device):
    return pltpu.make_async_remote_copy(
        src_ref=src, dst_ref=dst, send_sem=send, recv_sem=recv,
        device_id={"seq": device}, device_id_type=MESH,
    )


class Reduce:
    def __init__(self, seat, chunks, first, acc, second, send, recv):
        self.seat, self.chunks, self.first, self.acc, self.second = seat, chunks, first, acc, second
        self.send, self.recv = send, recv
        self.across = remote(chunks.at[1 - seat.core], first, send.at[0], recv.at[0], seat.partner)
        self.along = [
            remote(
                acc.at[seat.ahead(j)], second.at[j - 1], send.at[j], recv.at[j],
                seat.at(seat.ahead(j)),
            )
            for j in range(1, seat.nz)
        ]

    def start(self):
        self.across.start()

    def middle(self, merge):
        self.across.wait()
        for z in range(self.seat.nz):
            self.acc[z] = merge([self.chunks.at[self.seat.core, z], self.first.at[z]])
        for copy in self.along:
            copy.start()

    def finish(self, merge):
        for copy in self.along:
            copy.wait()
        refs = [self.acc.at[self.seat.z]] + [self.second.at[j] for j in range(self.seat.nz - 1)]
        return merge(refs)

    @staticmethod
    def scratch(n, shape):
        nz = n // 2
        return [
            VM((nz,) + shape, f32),
            VM((nz,) + shape, f32),
            VM((nz - 1,) + shape, f32),
            pltpu.SemaphoreType.DMA((nz,)),
            pltpu.SemaphoreType.DMA((nz,)),
        ]


class Gather:
    def __init__(self, seat, out, send, recv):
        own = out.at[seat.core, seat.z]
        self.along = [
            remote(own, own, send.at[j], recv.at[j], seat.at(seat.ahead(j)))
            for j in range(1, seat.nz)
        ]
        self.across = [remote(own, own, send.at[0], recv.at[0], seat.partner)]
        for j in range(1, seat.nz):
            block = out.at[seat.core, seat.behind(j)]
            k = seat.nz + j
            self.across.append(remote(block, block, send.at[k], recv.at[k], seat.partner))

    def start(self):
        for copy in self.along:
            copy.start()
        self.across[0].start()

    def forward(self):
        for copy, onward in zip(self.along, self.across[1:]):
            copy.wait_recv()
            onward.start()

    def finish(self):
        for copy in self.along:
            copy.wait_send()
        for copy in self.across:
            copy.wait()

    @staticmethod
    def scratch(n):
        return [pltpu.SemaphoreType.DMA((n,)), pltpu.SemaphoreType.DMA((n,))]


class Edges:
    def __init__(self, seat, sides, halos, send, recv):
        self.seat, self.halos = seat, halos
        core = seat.core
        self.copies = [
            remote(sides.at[1 - core], halos.at[core], send.at[0], recv.at[0], seat.partner),
            remote(sides.at[core], halos.at[1 - core], send.at[1], recv.at[1], seat.extra),
        ]

    def start(self):
        for copy in self.copies:
            copy.start()

    def finish(self, out):
        for copy in self.copies:
            copy.wait()
        seat = self.seat
        inner = (jnp.where(seat.me > 0, 1.0, 0.0), jnp.where(seat.me < seat.n - 1, 1.0, 0.0))
        for side in range(2):
            out[side] = self.halos[side] * inner[side]

    @staticmethod
    def scratch(shape):
        return [VM(shape, f32), pltpu.SemaphoreType.DMA((2,)), pltpu.SemaphoreType.DMA((2,))]


def add_all(refs):
    return functools.reduce(lambda x, y: x + y, [r[...] for r in refs])


def project_kernel(n, items, factor, tok_ref, mem_ref, wq_ref, wk_ref, wv_ref, vec_ref,
                   q_ref, k_ref, v_ref, lq_ref, lk_ref, inv_ref,
                   sums, land, halves, *scratch):
    seat = Seat(n)
    rows = items * MARKS // n
    width = tok_ref.shape[2]
    reduce = Reduce(seat, sums, *scratch[:5])
    gather = Gather(seat, land, *scratch[5:])
    seat.hello(False)
    for item in range(items):
        member = mem_ref[item].astype(bf16)
        hi, lo = split(tok_ref[item])
        total = dg(member, hi, 1, 0) + dg(member, lo, 1, 0)
        count = jnp.sum(mem_ref[item], axis=1, keepdims=True)
        for part in range(MARKS // rows):
            c = item * (MARKS // rows) + part
            piece = slice(part * rows, (part + 1) * rows)
            sums[c // seat.nz, c % seat.nz, :, :width] = total[piece]
            sums[c // seat.nz, c % seat.nz, :, width:] = jnp.broadcast_to(
                count[piece], (rows, PAIR)
            )
    reduce.start()
    b_query, b_value = vec_ref[0:1, :], vec_ref[1:2, :]
    for place, w_ref in enumerate((wq_ref, wk_ref, wv_ref)):
        hi, lo = split(w_ref[...])
        halves[2 * place], halves[2 * place + 1] = hi, lo

    def project(place, out_ref, bias, scale):
        def lap(item, _):
            x = split(tok_ref[item])
            y = dots(x, (halves[2 * place], halves[2 * place + 1]), 1, 0)
            y = y if bias is None else y + bias
            out_ref[item] = y if scale is None else y * scale
            return 0

        lax.fori_loop(0, items, lap, 0)

    project(0, q_ref, b_query, factor)
    reduce.middle(add_all)
    project(1, k_ref, None, factor)
    land[seat.core, seat.z] = reduce.finish(add_all)
    gather.start()
    project(2, v_ref, b_value, None)
    gather.forward()
    gather.finish()
    whole_land = land[...].reshape(items * MARKS, width + PAIR)
    divisor = jnp.maximum(whole_land[:, width:], 1.0)
    inv_ref[...] = (1.0 / divisor).reshape(items, MARKS, PAIR)
    filled = whole_land[:, width : width + 1] / divisor[:, 0:1]
    x = split(whole_land[:, :width] / divisor[:, 0:1])
    lq = (dots(x, (halves[0], halves[1]), 1, 0) + filled * b_query) * factor
    lk = dots(x, (halves[2], halves[3]), 1, 0) * factor
    lq_ref[...] = lq.reshape(items, MARKS, width)
    lk_ref[...] = lk.reshape(items, MARKS, width)


def project_call(tokens, member_t, w_query, w_key, w_value, vectors, n, factor):
    items, span, width = tokens.shape
    rows = items * MARKS // n
    big = jax.ShapeDtypeStruct((items, span, width), f32)
    small = jax.ShapeDtypeStruct((items, MARKS, width), f32)
    return pl.pallas_call(
        functools.partial(project_kernel, n, items, factor),
        out_shape=[big, big, big, small, small, jax.ShapeDtypeStruct((items, MARKS, PAIR), f32)],
        in_specs=[pl.BlockSpec(memory_space=VM)] * 6,
        out_specs=[pl.BlockSpec(memory_space=VM)] * 6,
        scratch_shapes=[
            VM((2, n // 2, rows, width + PAIR), f32),
            VM((2, n // 2, rows, width + PAIR), f32),
            VM((6, width, width), bf16),
        ]
        + Reduce.scratch(n, (rows, width + PAIR))
        + Gather.scratch(n),
        compiler_params=params(collective_id=0, has_side_effects=True),
        name="project",
    )(tokens, member_t, w_query, w_key, w_value, vectors)


def scores_kernel(per, pairs, q_ref, k_ref, v_ref, lq_ref, lk_ref, use_ref, k1_ref, w3_ref, top_ref, chunk):
    item = pl.program_id(0)
    stats = per * MARKS

    @pl.when(item == 0)
    def _():
        chunk[...] = jnp.zeros_like(chunk)

    use = use_ref[0]
    for p in range(pairs):
        lanes = slice(p * PAIR, (p + 1) * PAIR)
        q = q_ref[0, :, lanes]
        s1 = dot3(spread(lk_ref[0, :, lanes]), q, 1, 1)
        e1 = jnp.exp(s1 - block_max(s1))
        k1_ref[0, lanes, :] = e1 / block_sum(e1)
        s3 = dot3(spread(lq_ref[0, :, lanes]), k_ref[0, :, lanes], 1, 1)
        masked = jnp.where(use > 0, s3, -1e30)
        top = jnp.max(masked, axis=1, keepdims=True)
        w3 = jnp.exp(masked - top) * use
        w3_ref[0, lanes, :] = w3
        total = jnp.sum(w3, axis=1, keepdims=True)
        weighted = compacted(dot3(w3, v_ref[0, :, lanes]))
        top_row = row_of(top)
        top_ref[0, p : p + 1, :] = top_row
        g = item * pairs + p
        owner, place = g // per, g % per
        chunk[owner, pl.ds(pl.multiple_of(place * MARKS, MARKS), MARKS), :] = weighted
        chunk[owner, pl.ds(stats + 2 * place, 1), :] = top_row
        chunk[owner, pl.ds(stats + 2 * place + 1, 1), :] = row_of(total)


def scores_call(q, k, v, lq, lk, use_row, n, per, pairs, chunk_rows):
    items, span, width = q.shape
    return pl.pallas_call(
        functools.partial(scores_kernel, per, pairs),
        out_shape=[
            jax.ShapeDtypeStruct((items, width, span), f32),
            jax.ShapeDtypeStruct((items, width, span), f32),
            jax.ShapeDtypeStruct((items, 8, PAIR), f32),
            jax.ShapeDtypeStruct((n, chunk_rows, PAIR), f32),
        ],
        grid=(items,),
        in_specs=[per_item((span, width))] * 3
        + [per_item((MARKS, width))] * 2
        + [per_item((1, span))],
        out_specs=[per_item((width, span))] * 2
        + [per_item((8, PAIR)), whole((n, chunk_rows, PAIR))],
        compiler_params=params(),
        name="scores",
    )(q, k, v, lq, lk, use_row)


def owned_land(seat, per, pairs, ref, into):
    for place in range(per):
        g = lax.rem(seat.owner * per + place, ref.shape[0] * pairs)
        item, p = g // pairs, lax.rem(g, pairs)
        into[place] = ref[item, :, pl.ds(pl.multiple_of(p * PAIR, PAIR), PAIR)]


def newton_step(a, z, eye):
    pr = dot3(a, z)
    n1 = 7.0 * eye - pr
    n2 = 15.0 * eye - dot3(pr, n1)
    n3 = 13.0 * eye - dot3(pr, n2)
    return pr, n1, n2, n3


def unit():
    rows = lax.broadcasted_iota(jnp.int32, (PAIR, PAIR), 0)
    return (rows == lax.broadcasted_iota(jnp.int32, (PAIR, PAIR), 1)).astype(f32)


def head_total(x):
    return block_sum(jnp.sum(x, axis=1, keepdims=True))


def merged(per, refs):
    stats = per * MARKS
    weights, rest = [], []
    for place in range(per):
        tops = [r[stats + 2 * place : stats + 2 * place + 1, :] for r in refs]
        largest = functools.reduce(jnp.maximum, tops)
        total = jnp.zeros_like(largest)
        weighted = jnp.zeros((MARKS, PAIR), f32)
        for r, top in zip(refs, tops):
            scale = jnp.exp(top - largest)
            total = total + scale * r[stats + 2 * place + 1 : stats + 2 * place + 2, :]
            scales = compacted(column_of(scale))
            weighted = weighted + scales * r[place * MARKS : (place + 1) * MARKS, :]
        weights.append(weighted)
        rest += [largest, total]
    filler = jnp.zeros((refs[0].shape[0] - stats - 2 * per, PAIR), f32)
    return jnp.concatenate(weights + rest + [filler], axis=0)


def exchange_kernel(n, per, pairs, chunk_ref, lq_ref, lk_ref, side_ref,
                    a_ref, z_ref, lqo_ref, lko_ref, ctx_ref, out_ref, halo_ref, mine, *scratch):
    seat = Seat(n)
    merge = functools.partial(merged, per)
    reduce = Reduce(seat, chunk_ref, *scratch[:5])
    gather = Gather(seat, out_ref, *scratch[5:7])
    edges = Edges(seat, side_ref, *scratch[7:])
    seat.hello(True)
    reduce.start()
    edges.start()
    owned_land(seat, per, pairs, lq_ref, lqo_ref)
    owned_land(seat, per, pairs, lk_ref, lko_ref)
    diagonal = diagonal_mask()
    eye = unit()
    for place in range(per):
        s2 = dot3(spread(lqo_ref[place]), spread(lko_ref[place]), 1, 1)
        s2 = jnp.where(diagonal, s2, -1e30)
        e2 = jnp.exp(s2 - jnp.max(s2, axis=1, keepdims=True))
        e2 = jnp.where(diagonal, e2, 0.0)
        a = e2 / jnp.sum(e2, axis=1, keepdims=True)
        a_ref[place] = a
        z_ref[0, place] = jnp.transpose(a) / head_total(a * a)
    reduce.middle(merge)

    def lap(step, _):
        for place in range(per):
            z = z_ref[step, place]
            _, _, _, n3 = newton_step(a_ref[place], z, eye)
            z_ref[step + 1, place] = 0.25 * dot3(z, n3)
        return 0

    lax.fori_loop(0, NEWTON, lap, 0)
    mine[...] = reduce.finish(merge)
    stats = per * MARKS
    block = out_ref.at[seat.core, seat.z]
    block[stats:, :] = mine[stats:, :]
    for place in range(per):
        rows = slice(place * MARKS, (place + 1) * MARKS)
        total = mine[stats + 2 * place + 1 : stats + 2 * place + 2, :]
        context = mine[rows, :] / compacted(column_of(total))
        ctx_ref[place] = context
        block[rows, :] = compacted(dot3(z_ref[NEWTON, place], spread(context)))
    gather.start()
    edges.finish(halo_ref)
    gather.forward()
    gather.finish()


def exchange_call(chunks, lq, lk, sides, n, per, pairs):
    rows = chunks.shape[1]
    small = jax.ShapeDtypeStruct((per, MARKS, PAIR), f32)
    blocks = (2, n // 2, rows, PAIR)
    out = pl.pallas_call(
        functools.partial(exchange_kernel, n, per, pairs),
        out_shape=[
            jax.ShapeDtypeStruct((per, PAIR, PAIR), f32),
            jax.ShapeDtypeStruct((NEWTON + 1, per, PAIR, PAIR), f32),
            small,
            small,
            small,
            jax.ShapeDtypeStruct(blocks, f32),
            jax.ShapeDtypeStruct(sides.shape, f32),
        ],
        in_specs=[pl.BlockSpec(memory_space=VM)] * 4,
        out_specs=[pl.BlockSpec(memory_space=VM)] * 7,
        scratch_shapes=[VM((rows, PAIR), f32)]
        + Reduce.scratch(n, (rows, PAIR))
        + Gather.scratch(n)
        + Edges.scratch(sides.shape),
        compiler_params=params(collective_id=1, has_side_effects=True),
        name="exchange",
    )(chunks.reshape(blocks), lq, lk, sides)
    return list(out[:5]) + [out[5].reshape(n, rows, PAIR), out[6]]


def toeplitz(taps_row, rows):
    wide = jnp.broadcast_to(taps_row, (rows, 2 * PAIR))
    return pltpu.roll(wide, 0, 1, stride=1, stride_axis=0)


def keep_taps(taps_ref, into, heads):
    for h in range(heads):
        hi, lo = split(toeplitz(taps_ref[h : h + 1, :], PAIR))
        into[0, h] = hi
        into[1, h] = lo


def keep_window(win, left, middle, right, margin, span):
    for rows, part in (
        (slice(0, margin), left),
        (slice(margin, margin + span), middle),
        (slice(margin + span, 2 * margin + span), right),
    ):
        hi, lo = split(part)
        win[0, rows, :] = hi
        win[1, rows, :] = lo


def convolve(taps, win, p, block, window):
    lanes = slice(p * PAIR, (p + 1) * PAIR)
    rows = slice(block * PAIR, block * PAIR + window)
    v = (win[0, rows, lanes], win[1, rows, lanes])
    halves = []
    for h in (2 * p, 2 * p + 1):
        t = (taps[0, h, :, :window], taps[1, h, :, :window])
        halves.append(dots(t, v, 1, 0))
    return jnp.where(lane_low((PAIR, PAIR)), halves[0], halves[1])


def owned_by(g, per):
    return g // per, g % per


def mix_kernel(per, pairs, margin, held, k1_ref, v_ref, use_ref, left_ref, right_ref, taps_ref, out_ref, taps, win):
    item = pl.program_id(0)
    span = v_ref.shape[1]
    window = PAIR + 2 * margin

    @pl.when(item == 0)
    def _():
        keep_taps(taps_ref, taps, 2 * pairs)

    keep_window(win, left_ref[0, 0], v_ref[0] * use_ref[0], right_ref[0, 0], margin, span)
    for p in range(pairs):
        lanes = slice(p * PAIR, (p + 1) * PAIR)
        slot, place = owned_by(item * pairs + p, per)
        mixed = held[slot, pl.ds(pl.multiple_of(place * MARKS, MARKS), MARKS), :]
        nystrom = dot3(k1_ref[0, lanes, :], spread(mixed), 0, 0)
        for block in range(span // PAIR):
            rows = slice(block * PAIR, (block + 1) * PAIR)
            out_ref[0, rows, lanes] = nystrom[rows] + convolve(taps, win, p, block, window)


def halo_specs(margin, width):
    return [
        pl.BlockSpec((1, 1, margin, width), lambda i, side=side: (side, i, 0, 0))
        for side in range(2)
    ]


def mix_call(blocks, k1, v, use_col, halos, taps, per, pairs, margin):
    items, span, width = v.shape
    return pl.pallas_call(
        functools.partial(mix_kernel, per, pairs, margin),
        out_shape=jax.ShapeDtypeStruct((items, span, width), f32),
        grid=(items,),
        in_specs=[whole(blocks.shape)]
        + [per_item((width, span)), per_item((span, width)), per_item((span, 1))]
        + halo_specs(margin, width)
        + [whole(taps.shape)],
        out_specs=per_item((span, width)),
        scratch_shapes=[
            VM((2, 2 * pairs, PAIR, 2 * PAIR), bf16),
            VM((2, span + 2 * margin, width), bf16),
        ],
        compiler_params=params(),
        name="mix",
    )(blocks, k1, v, use_col, halos, halos, taps)


def erf(x):
    x = jnp.clip(x, -3.832506856900711, 3.832506856900711)
    s = x * x
    a = 0.00022905065861350646
    for c in (0.0034082910107109506, 0.050955695062380861, 0.18520832239976145, 1.128379143519084):
        a = a * s + c
    b = -1.1791602954361697e-7
    for c in (
        0.000023547966471313185,
        0.0010179625278914885,
        0.014070470171167667,
        0.11098505178285362,
        0.49746925110067538,
        1.0,
    ):
        b = b * s + c
    return x * a / b


def normalize(x):
    center = x - jnp.mean(x, axis=-1, keepdims=True)
    inv_root = lax.rsqrt(jnp.mean(center * center, axis=-1, keepdims=True) + epsilon)
    return center * inv_root, inv_root


def norm_back(grad, scaled, inv_root):
    first = jnp.mean(grad, axis=-1, keepdims=True)
    second = jnp.mean(grad * scaled, axis=-1, keepdims=True)
    return inv_root * (grad - first - scaled * second)


def rows_kernel(
    ff_tile,
    x_ref,
    tok_ref,
    cot_ref,
    wo_h,
    wo_l,
    wu_h,
    wu_l,
    wd_h,
    wd_l,
    vec_ref,
    bup_ref,
    out_ref,
    act_ref,
    u_ref,
    r2_ref,
    h1_ref,
    r1_ref,
    og_ref,
    sums_ref,
    bsum_ref,
    slope,
):
    @pl.when(pl.program_id(0) == 0)
    def _():
        sums_ref[...] = jnp.zeros_like(sums_ref)
        bsum_ref[...] = jnp.zeros_like(bsum_ref)

    b_out, gain_one, shift_one = vec_ref[0:1, :], vec_ref[1:2, :], vec_ref[2:3, :]
    b_down, gain_two, shift_two = vec_ref[3:4, :], vec_ref[4:5, :], vec_ref[5:6, :]
    wo = (wo_h[...], wo_l[...])
    attention = dots(split(x_ref[...]), wo, 1, 0) + b_out
    scaled_one, root_one = normalize(tok_ref[...] + attention)
    hidden = scaled_one * gain_one + shift_one
    h1_ref[...] = hidden
    hs = split(hidden)
    ff = wu_h.shape[1]
    tiles = [slice(c, c + ff_tile) for c in range(0, ff, ff_tile)]
    down = b_down
    for c in tiles:
        pre = dots(hs, (wu_h[:, c], wu_l[:, c]), 1, 0) + bup_ref[:, c]
        phi = 0.5 + 0.5 * erf(pre * 0.7071067811865476)
        slope[:, c] = phi + pre * (0.3989422804014327 * jnp.exp(-0.5 * pre * pre))
        act = pre * phi
        act_ref[:, c] = act
        down = down + dots(split(act), (wd_h[c, :], wd_l[c, :]), 1, 0)
    scaled_two, root_two = normalize(hidden + down)
    out_ref[...] = scaled_two * gain_two + shift_two
    cot = cot_ref[...]
    r2 = norm_back(cot * gain_two, scaled_two, root_two)
    r2_ref[...] = r2
    rs = split(r2)
    grad_hidden = r2
    for c in tiles:
        u = dots(rs, (wd_h[c, :], wd_l[c, :]), 1, 1) * slope[:, c]
        u_ref[:, c] = u
        bsum_ref[:, c] += jnp.sum(u, axis=0, keepdims=True)
        grad_hidden = grad_hidden + dots(split(u), (wu_h[:, c], wu_l[:, c]), 1, 1)
    r1 = norm_back(grad_hidden * gain_one, scaled_one, root_one)
    r1_ref[...] = r1
    og_ref[...] = dots(split(r1), wo, 1, 1)
    for row, value in enumerate(
        (cot * scaled_two, cot, r2, grad_hidden * scaled_one, grad_hidden, r1)
    ):
        sums_ref[row : row + 1, :] += jnp.sum(value, axis=0, keepdims=True)


def rows_call(x, tokens, cotangent, wo, wu, wd, vectors, b_up):
    rows, width = x.shape
    ff = wu[0].shape[1]
    tile = 256
    ff_tile = 768
    wide = pl.BlockSpec((tile, width), lambda i: (i, 0))
    hidden = pl.BlockSpec((tile, ff), lambda i: (i, 0))

    def fixed(a):
        return pl.BlockSpec(a.shape, lambda i: (0, 0), pipeline_mode=pl.Buffered(1))

    narrow = jax.ShapeDtypeStruct((rows, width), f32)
    broad = jax.ShapeDtypeStruct((rows, ff), f32)
    return pl.pallas_call(
        functools.partial(rows_kernel, ff_tile),
        out_shape=[
            narrow,
            broad,
            broad,
            narrow,
            narrow,
            narrow,
            narrow,
            jax.ShapeDtypeStruct((8, width), f32),
            jax.ShapeDtypeStruct((1, ff), f32),
        ],
        grid=(rows // tile,),
        in_specs=[wide] * 3
        + [fixed(a) for a in (*wo, *wu, *wd)]
        + [fixed(vectors), fixed(b_up)],
        out_specs=[wide, hidden, hidden, wide, wide, wide, wide]
        + [pl.BlockSpec((8, width), lambda i: (0, 0)), pl.BlockSpec((1, ff), lambda i: (0, 0))],
        scratch_shapes=[VM((tile, ff), f32)],
        compiler_params=params(),
        name="rows",
    )(x, tokens, cotangent, *wo, *wu, *wd, vectors, b_up)


def one_back_kernel(per, pairs, held, k1_ref, og_ref, q_ref, lk_ref, gq_ref, chunk):
    item = pl.program_id(0)

    @pl.when(item == 0)
    def _():
        chunk[...] = jnp.zeros_like(chunk)

    for p in range(pairs):
        lanes = slice(p * PAIR, (p + 1) * PAIR)
        owner, place = owned_by(item * pairs + p, per)
        mixed = spread(held[owner, pl.ds(pl.multiple_of(place * MARKS, MARKS), MARKS), :])
        k1 = k1_ref[0, lanes, :]
        og = split(og_ref[0, :, lanes])
        part_mixed = compacted(dots(split(k1), og, 1, 0))
        grad = dots(split(mixed), og, 1, 1)
        scores = k1 * (grad - block_sum(k1 * grad))
        ss = split(scores)
        gq_ref[0, :, lanes] = dots(ss, split(spread(lk_ref[0, :, lanes])), 0, 0)
        part_key = compacted(dots(ss, split(q_ref[0, :, lanes]), 1, 0))
        chunk[owner, pl.ds(pl.multiple_of(place * 2 * MARKS, 2 * MARKS), MARKS), :] = part_mixed
        chunk[owner, pl.ds(pl.multiple_of(place * 2 * MARKS + MARKS, MARKS), MARKS), :] = part_key


def one_back_call(blocks, k1, og, q, lk, per, pairs):
    items, span, width = q.shape
    out = (blocks.shape[0], 2 * per * MARKS, PAIR)
    wide = per_item((span, width))
    return pl.pallas_call(
        functools.partial(one_back_kernel, per, pairs),
        out_shape=[
            jax.ShapeDtypeStruct((items, span, width), f32),
            jax.ShapeDtypeStruct(out, f32),
        ],
        grid=(items,),
        in_specs=[whole(blocks.shape), per_item((width, span)), wide, wide]
        + [per_item((MARKS, width))],
        out_specs=[wide, whole(out)],
        compiler_params=params(),
        name="one_back",
    )(blocks, k1, og, q, lk)


def conv_back_kernel(pairs, margin, og_ref, gl_ref, gr_ref, v_ref, vl_ref, vr_ref, use_ref, taps_ref, *refs):
    gv_ref, gtaps_ref, taps, gwin, vwin, acc = refs
    item = pl.program_id(0)
    span = v_ref.shape[1]
    window = PAIR + 2 * margin

    @pl.when(item == 0)
    def _():
        keep_taps(taps_ref, taps, 2 * pairs)
        acc[...] = jnp.zeros_like(acc)

    use = use_ref[0]
    keep_window(gwin, gl_ref[0, 0], og_ref[0], gr_ref[0, 0], margin, span)
    keep_window(vwin, vl_ref[0, 0], v_ref[0] * use, vr_ref[0, 0], margin, span)
    for p in range(pairs):
        lanes = slice(p * PAIR, (p + 1) * PAIR)
        for block in range(span // PAIR):
            rows = slice(block * PAIR, (block + 1) * PAIR)
            gv_ref[0, rows, lanes] = convolve(taps, gwin, p, block, window) * use[rows]
            inner = slice(margin + block * PAIR, margin + (block + 1) * PAIR)
            outer = slice(block * PAIR, block * PAIR + window)
            v = (vwin[0, outer, lanes], vwin[1, outer, lanes])
            low = lane_low((PAIR, PAIR))
            hi, lo = gwin[0, inner, lanes], gwin[1, inner, lanes]
            zero = jnp.zeros_like(hi)
            acc[2 * p] += dots((jnp.where(low, hi, zero), jnp.where(low, lo, zero)), v, 1, 1)
            acc[2 * p + 1] += dots((jnp.where(low, zero, hi), jnp.where(low, zero, lo)), v, 1, 1)

    @pl.when(item == pl.num_programs(0) - 1)
    def _():
        rows = lax.broadcasted_iota(jnp.int32, (PAIR, PAIR), 0)
        flip = (rows + lax.broadcasted_iota(jnp.int32, (PAIR, PAIR), 1) == PAIR - 1).astype(bf16)
        for h in range(2 * pairs):
            c = acc[h]
            c = jnp.concatenate([c, jnp.zeros((PAIR, 2 * PAIR - window), f32)], axis=1)
            hi = c.astype(bf16)
            rest = c - hi.astype(f32)
            mid = rest.astype(bf16)
            low = (rest - mid.astype(f32)).astype(bf16)
            c = dg(flip, hi, 1, 0) + dg(flip, mid, 1, 0) + dg(flip, low, 1, 0)
            c = pltpu.roll(c, 0, 1, stride=1, stride_axis=0)
            gtaps_ref[h : h + 1, :] = jnp.sum(c, axis=0, keepdims=True)


def conv_back_call(og, ghalos, v, vhalos, use_col, taps, pairs, margin):
    items, span, width = v.shape
    window = PAIR + 2 * margin
    wide, edge = per_item((span, width)), halo_specs(margin, width)
    rows = -(-2 * pairs // 8) * 8
    return pl.pallas_call(
        functools.partial(conv_back_kernel, pairs, margin),
        out_shape=[
            jax.ShapeDtypeStruct((items, span, width), f32),
            jax.ShapeDtypeStruct((rows, 2 * PAIR), f32),
        ],
        grid=(items,),
        in_specs=[wide, *edge, wide, *edge, per_item((span, 1)), whole(taps.shape)],
        out_specs=[wide, whole((rows, 2 * PAIR))],
        scratch_shapes=[
            VM((2, 2 * pairs, PAIR, 2 * PAIR), bf16),
            VM((2, span + 2 * margin, width), bf16),
            VM((2, span + 2 * margin, width), bf16),
            VM((2 * pairs, PAIR, window), f32),
        ],
        compiler_params=params(),
        name="conv_back",
    )(og, ghalos, ghalos, v, vhalos, vhalos, use_col, taps)


def exchange_back_kernel(n, per, chunk_ref, side_ref, ctx_ref, a_ref, z_ref, lq_ref, lk_ref,
                         out_ref, gq_ref, gk_ref, halo_ref, gm, gz, ga, *scratch):
    seat = Seat(n)
    reduce = Reduce(seat, chunk_ref, *scratch[:5])
    gather = Gather(seat, out_ref, *scratch[5:7])
    edges = Edges(seat, side_ref, *scratch[7:])
    seat.hello(True)
    reduce.start()
    edges.start()
    reduce.middle(add_all)
    diagonal = diagonal_mask()
    eye = unit()
    stats = per * MARKS
    gm[...] = reduce.finish(add_all)
    block = out_ref.at[seat.core, seat.z]
    block[stats:, :] = jnp.zeros((block.shape[0] - stats, PAIR), f32)
    for place in range(per):
        mixed = spread(gm[place * 2 * MARKS : place * 2 * MARKS + MARKS, :])
        context = spread(ctx_ref[place])
        grad = dot3(jnp.transpose(z_ref[NEWTON, place]), mixed)
        block[place * MARKS : (place + 1) * MARKS, :] = compacted(grad)
        dot = jnp.sum(grad * context, axis=1, keepdims=True)
        block[stats + place : stats + place + 1, :] = row_of(dot)
        gz[place] = jnp.where(diagonal, dot3(mixed, context, 1, 1), 0.0)
        ga[place] = jnp.zeros((PAIR, PAIR), f32)
    gather.start()

    def lap(back, _):
        step = NEWTON - 1 - back
        for place in range(per):
            a, z, g = a_ref[place], z_ref[step, place], 0.25 * gz[place]
            pr, n1, n2, n3 = newton_step(a, z, eye)
            back_three = dot3(jnp.transpose(z), g)
            turned = jnp.transpose(pr)
            back_two = -dot3(turned, back_three)
            back_one = -dot3(turned, back_two)
            grad = -dot3(back_three, n2, 1, 1) - dot3(back_two, n1, 1, 1) - back_one
            ga[place] += dot3(grad, z, 1, 1)
            gz[place] = dot3(g, n3, 1, 1) + dot3(jnp.transpose(a), grad)
        return 0

    lax.fori_loop(0, NEWTON - 1, lap, 0)
    gather.forward()
    lax.fori_loop(NEWTON - 1, NEWTON, lap, 0)
    for place in range(per):
        a, g = a_ref[place], jnp.transpose(gz[place])
        norm = head_total(a * a)
        slope = -head_total(g * a) / (norm * norm)
        grad = ga[place] + g / norm + 2.0 * slope * a
        scores = a * (grad - jnp.sum(a * grad, axis=1, keepdims=True))
        gq_ref[place] = compacted(dot3(scores, spread(lk_ref[place])))
        gk_ref[place] = gm[place * 2 * MARKS + MARKS : (place + 1) * 2 * MARKS, :] + compacted(
            dot3(jnp.transpose(scores), spread(lq_ref[place]))
        )
    edges.finish(halo_ref)
    gather.finish()


def exchange_back_call(chunks, sides, ctx, a, z, lq, lk, n, rows):
    per = ctx.shape[0]
    small = jax.ShapeDtypeStruct(ctx.shape, f32)
    chunk = chunks.shape[1:]
    blocks = (2, n // 2, rows, PAIR)
    out = pl.pallas_call(
        functools.partial(exchange_back_kernel, n, per),
        out_shape=[
            jax.ShapeDtypeStruct(blocks, f32),
            small,
            small,
            jax.ShapeDtypeStruct(sides.shape, f32),
        ],
        in_specs=[pl.BlockSpec(memory_space=VM)] * 7,
        out_specs=[pl.BlockSpec(memory_space=VM)] * 4,
        scratch_shapes=[VM(chunk, f32)]
        + [VM((per, PAIR, PAIR), f32)] * 2
        + Reduce.scratch(n, chunk)
        + Gather.scratch(n)
        + Edges.scratch(sides.shape),
        compiler_params=params(collective_id=2, has_side_effects=True),
        name="exchange_back",
    )(chunks.reshape((2, n // 2) + chunk), sides, ctx, a, z, lq, lk)
    return [out[0].reshape(n, rows, PAIR)] + list(out[1:])


def three_back_kernel(per, pairs, held, stat, w3_ref, top_ref, v_ref, k_ref, gvc_ref, lq_ref,
                      gv_ref, gk_ref, chunk):
    item = pl.program_id(0)
    stats = per * MARKS

    @pl.when(item == 0)
    def _():
        chunk[...] = jnp.zeros_like(chunk)

    for p in range(pairs):
        lanes = slice(p * PAIR, (p + 1) * PAIR)
        owner, place = owned_by(item * pairs + p, per)
        grad = split(spread(held[owner, pl.ds(pl.multiple_of(place * MARKS, MARKS), MARKS), :]))
        row_dot = column_of(held[owner, pl.ds(stats + place, 1), :])
        largest = stat[owner, pl.ds(stats + 2 * place, 1), :]
        total = stat[owner, pl.ds(stats + 2 * place + 1, 1), :]
        scale = column_of(jnp.exp(top_ref[0, p : p + 1, :] - largest) / total)
        k3 = w3_ref[0, lanes, :] * scale[:, 0:1]
        gk3 = dots(grad, split(v_ref[0, :, lanes]), 1, 1)
        scores = split(k3 * (gk3 - row_dot[:, 0:1]))
        gv_ref[0, :, lanes] = gvc_ref[0, :, lanes] + dots(split(k3), grad, 0, 0)
        gk_ref[0, :, lanes] = dots(scores, split(spread(lq_ref[0, :, lanes])), 0, 0)
        part = compacted(dots(scores, split(k_ref[0, :, lanes]), 1, 0))
        chunk[owner, pl.ds(pl.multiple_of(place * MARKS, MARKS), MARKS), :] = part


def three_back_call(grads, blocks, w3, top, v, k, gv_conv, lq, per, pairs):
    items, span, width = v.shape
    out = (blocks.shape[0], per * MARKS, PAIR)
    wide = per_item((span, width))
    shape = jax.ShapeDtypeStruct((items, span, width), f32)
    return pl.pallas_call(
        functools.partial(three_back_kernel, per, pairs),
        out_shape=[shape, shape, jax.ShapeDtypeStruct(out, f32)],
        grid=(items,),
        in_specs=[whole(blocks.shape)] * 2
        + [per_item((width, span)), per_item((8, PAIR)), wide, wide, wide]
        + [per_item((MARKS, width))],
        out_specs=[wide, wide, whole(out)],
        compiler_params=params(),
        name="three_back",
    )(grads, blocks, w3, top, v, k, gv_conv, lq)


def land_exchange_kernel(n, per, chunk_ref, q_ref, k_ref, out_ref, *scratch):
    seat = Seat(n)
    reduce = Reduce(seat, chunk_ref, *scratch[:5])
    gather = Gather(seat, out_ref, *scratch[5:])
    seat.hello(False)
    reduce.start()
    reduce.middle(add_all)
    half = per * MARKS
    block = out_ref.at[seat.core, seat.z]
    block[half:, :] = k_ref[...]
    block[:half, :] = q_ref[...] + reduce.finish(add_all)
    gather.start()
    gather.forward()
    gather.finish()


def land_exchange_call(chunks, own_q, own_k, n):
    per = own_q.shape[0]
    half = per * MARKS
    blocks = (2, n // 2, 2 * half, PAIR)
    return pl.pallas_call(
        functools.partial(land_exchange_kernel, n, per),
        out_shape=jax.ShapeDtypeStruct(blocks, f32),
        in_specs=[pl.BlockSpec(memory_space=VM)] * 3,
        out_specs=pl.BlockSpec(memory_space=VM),
        scratch_shapes=Reduce.scratch(n, (half, PAIR)) + Gather.scratch(n),
        compiler_params=params(collective_id=3, has_side_effects=True),
        name="land_exchange",
    )(chunks.reshape(2, n // 2, half, PAIR), own_q.reshape(half, PAIR), own_k.reshape(half, PAIR)).reshape(
        n, 2 * half, PAIR
    )


def land_back_kernel(per, pairs, factor, held, gq_ref, gk_ref, gv_ref, mem_ref, inv_ref, oq_ref, ok_ref, sums_ref):
    item = pl.program_id(0)
    half = per * MARKS

    @pl.when(item == 0)
    def _():
        sums_ref[...] = jnp.zeros_like(sums_ref)

    member = mem_ref[0].astype(bf16)
    inv = inv_ref[0]
    for p in range(pairs):
        lanes = slice(p * PAIR, (p + 1) * PAIR)
        slot, place = owned_by(item * pairs + p, per)
        for ref, out, base in ((gq_ref, oq_ref, 0), (gk_ref, ok_ref, half)):
            grad = held[slot, pl.ds(pl.multiple_of(base + place * MARKS, MARKS), MARKS), :]
            hi, lo = split(grad * inv)
            landed = dg(member, hi, 0, 0) + dg(member, lo, 0, 0)
            out[0, :, lanes] = (ref[0, :, lanes] + landed) * factor
        sums_ref[0:1, lanes] += jnp.sum(oq_ref[0, :, lanes], axis=0, keepdims=True)
        sums_ref[1:2, lanes] += jnp.sum(gv_ref[0, :, lanes], axis=0, keepdims=True)


def land_back_call(blocks, gq, gk, gv, member_t, inv, per, pairs, factor):
    items, span, width = gq.shape
    wide = per_item((span, width))
    shape = jax.ShapeDtypeStruct((items, span, width), f32)
    return pl.pallas_call(
        functools.partial(land_back_kernel, per, pairs, factor),
        out_shape=[shape, shape, jax.ShapeDtypeStruct((8, width), f32)],
        grid=(items,),
        in_specs=[whole(blocks.shape), wide, wide, wide]
        + [per_item((MARKS, span)), per_item((MARKS, PAIR))],
        out_specs=[wide, wide, whole((8, width))],
        compiler_params=params(),
        name="land_back",
    )(blocks, gq, gk, gv, member_t, inv)


def swap(x, axis, offset):
    count = lax.axis_size(axis)
    return lax.ppermute(x, axis, [(i, i ^ offset) for i in range(count)])


def both_sides(x, margin):
    return jnp.stack([x[:, :margin], x[:, -margin:]])


def bit_of(axis, bit):
    return lax.axis_index(axis) // bit % 2


def halve_rows(x, bit):
    blocks, rows, columns = x.shape
    y = x.reshape(blocks // 2, 2, rows, columns)
    mine = bit_of("seq", bit)
    keep = lax.dynamic_index_in_dim(y, mine, 1, False)
    send = lax.dynamic_index_in_dim(y, 1 - mine, 1, False)
    return keep + swap(send, "seq", bit)


def halve_columns(x, bits, bit):
    mine = bit_of("dp", bit)
    columns = x.shape[2]
    groups = 2 ** bits.index(bit)
    size = columns // (2 * groups)

    def pick(which):
        parts = [
            lax.dynamic_slice_in_dim(x, 2 * g * size + which * size, size, 2)
            for g in range(groups)
        ]
        return parts[0] if groups == 1 else jnp.concatenate(parts, axis=2)

    return pick(mine) + swap(pick(1 - mine), "dp", bit)


def powers(axis):
    count = lax.axis_size(axis)
    return [2**i for i in range(count.bit_length() - 1)]


def scatter_sum(x, order):
    seq_bits, dp_bits = powers("seq"), powers("dp")[::-1]
    count = lax.axis_size("seq")
    x = x.reshape(count, x.shape[0] // count, x.shape[1])
    x = halve_rows(x, seq_bits.pop(0))
    for axis in order:
        if axis == "z" and seq_bits:
            x = halve_rows(x, seq_bits.pop(0))
        elif axis in "xy" and dp_bits:
            half = len(powers("dp")) // 2
            low = [b for b in dp_bits if b < 2**half]
            high = [b for b in dp_bits if b >= 2**half]
            chosen = (low if axis == "x" else high) or dp_bits
            x = halve_columns(x, dp_bits, chosen[0])
            dp_bits.remove(chosen[0])
    while seq_bits:
        x = halve_rows(x, seq_bits.pop(0))
    while dp_bits:
        x = halve_columns(x, dp_bits, dp_bits[0])
        dp_bits.pop(0)
    return x[0]


def sum_everywhere(x):
    for axis in ("seq", "dp"):
        for bit in powers(axis):
            x = x + swap(x, axis, bit)
    return x


def rounded_pair(w):
    hi = lax.reduce_precision(w, 8, 7)
    return hi.astype(bf16), (w - hi).astype(bf16)


def product(a, b, ca, cb):
    return lax.dot_general(a, b, (((ca,), (cb,)), ((), ())), precision=HIGH)


def on_device(
    tokens,
    lengths,
    keep,
    w_query,
    b_query,
    w_key,
    w_value,
    b_value,
    conv_weight,
    w_out,
    b_out,
    gain_one,
    shift_one,
    w_up,
    b_up,
    w_down,
    b_down,
    gain_two,
    shift_two,
    cotangent,
):
    items, span, width = tokens.shape
    heads, taps = conv_weight.shape
    head_size = width // heads
    margin = taps // 2
    factor = head_size ** (-0.25)
    pairs = heads // 2
    n = lax.axis_size("seq")
    per = -(-items * pairs // n)
    chunk_rows = per * MARKS + 8
    position = lax.axis_index("seq") * span + jnp.arange(span, dtype=jnp.int32)
    inside = position[None, :] < lengths[:, None]
    usable = (inside & (keep > 0)).astype(f32)
    use_row, use_col = usable[:, None, :], usable[:, :, None]
    segment = jnp.where(inside, position[None, :] * MARKS // lengths[:, None], MARKS)
    marks = jnp.arange(MARKS, dtype=jnp.int32)
    member_t = (segment[:, None, :] == marks[None, :, None]).astype(f32) * use_row
    rows = tokens.reshape(items * span, width)
    taps_forward = jnp.pad(conv_weight, ((0, 4), (0, 2 * PAIR - taps)))
    taps_backward = jnp.pad(conv_weight[:, ::-1], ((0, 4), (0, 2 * PAIR - taps)))

    queries, key_rows, values, land_q, land_k, inverse_divisor = project_call(
        tokens, member_t, w_query, w_key, w_value, jnp.stack([b_query, b_value]), n, factor
    )
    k1, w3, top, chunks = scores_call(
        queries, key_rows, values, land_q, land_k, use_row, n, per, pairs, chunk_rows
    )
    use_sides = both_sides(use_col, margin)
    kernel_two, z, owned_q, owned_k, context, mixed, vhalos = exchange_call(
        chunks, land_q, land_k, both_sides(values, margin) * use_sides, n, per, pairs
    )
    attn_input = mix_call(mixed, k1, values, use_col, vhalos, taps_forward, per, pairs, margin)

    vectors = jnp.stack(
        [b_out, gain_one, shift_one, b_down, gain_two, shift_two, b_out, b_out]
    )
    x = attn_input.reshape(items * span, width)
    output, act, u, r2, hidden, r1, og, row_sums, up_sums = rows_call(
        x,
        rows,
        cotangent.reshape(items * span, width),
        rounded_pair(w_out),
        rounded_pair(w_up),
        rounded_pair(w_down),
        vectors,
        b_up[None, :],
    )
    og = og.reshape(items, span, width)
    grad_queries, chunks = one_back_call(mixed, k1, og, queries, land_k, per, pairs)
    grad_context, own_q, own_k, ghalos = exchange_back_call(
        chunks, both_sides(og, margin), context, kernel_two, z, owned_q, owned_k, n, chunk_rows
    )
    gv_conv, grad_taps = conv_back_call(
        og, ghalos, values, vhalos, use_col, taps_backward, pairs, margin
    )
    grad_values, grad_keys, chunks = three_back_call(
        grad_context, mixed, w3, top, values, key_rows, gv_conv, land_q, per, pairs
    )
    land_grads = land_exchange_call(chunks, own_q, own_k, n)
    grad_queries, grad_keys, late_sums = land_back_call(
        land_grads, grad_queries, grad_keys, grad_values, member_t, inverse_divisor,
        per, pairs, factor,
    )
    grad_w_down = scatter_sum(product(r2, act, 0, 0), "yxzz")
    grad_w_up = scatter_sum(product(u, hidden, 0, 0), "xzyz")
    grad_w_out = scatter_sum(product(r1, x, 0, 0), "zyxz")
    grad_queries = grad_queries.reshape(items * span, width)
    grad_keys = grad_keys.reshape(items * span, width)
    grad_values = grad_values.reshape(items * span, width)
    grad_w_value = scatter_sum(product(grad_values, rows, 0, 0), "zyxz")
    grad_w_query = scatter_sum(product(grad_queries, rows, 0, 0), "yxzz")
    grad_w_key = scatter_sum(product(grad_keys, rows, 0, 0), "xzyz")
    grad_tokens = (
        r1
        + product(grad_values, w_value, 1, 1)
        + product(grad_queries, w_query, 1, 1)
        + product(grad_keys, w_key, 1, 1)
    )

    early = sum_everywhere(
        jnp.concatenate([row_sums.reshape(-1), up_sums.reshape(-1), grad_taps.reshape(-1)]).reshape(
            -1, PAIR
        )
    ).reshape(-1)
    late = sum_everywhere(late_sums)
    row_sums = early[: 8 * width].reshape(8, width)
    ff = w_up.shape[1]
    up_sums = early[8 * width : 8 * width + ff]
    grad_taps = early[8 * width + ff :].reshape(-1, 2 * PAIR)
    grad_conv = grad_taps[:heads, PAIR - 1 : PAIR - 1 + taps]
    return (
        output.reshape(tokens.shape),
        grad_tokens.reshape(tokens.shape),
        grad_w_query.T,
        late[0],
        grad_w_key.T,
        grad_w_value.T,
        late[1],
        grad_conv,
        grad_w_out.T,
        row_sums[5],
        row_sums[3],
        row_sums[4],
        grad_w_up.T,
        up_sums,
        grad_w_down.T,
        row_sums[2],
        row_sums[0],
        row_sums[1],
    )


def solution(mesh):
    rows = P("dp", "seq", None)
    block = P("dp", "seq")
    in_specs = (rows, P("dp"), block) + (P(),) * 16 + (rows,)
    out_specs = (
        rows, rows, block, P(), block, block, P(), P(), block,
        P(), P(), P(), block, P(), block, P(), P(), P(),
    )
    return jax.shard_map(
        on_device, mesh=mesh, in_specs=in_specs, out_specs=out_specs, check_vma=False
    )
```

```python
import functools

import jax
import jax.numpy as jnp
from jax import lax
from jax.experimental import pallas as pl
from jax.experimental.pallas import tpu as pltpu
from jax.sharding import PartitionSpec as P

MARKS = 64
NEWTON = 6
PAIR = 128
HIGH = lax.Precision.HIGH
epsilon = 1e-05
f32 = jnp.float32
bf16 = jnp.bfloat16
VM = pltpu.VMEM
LIMIT = 66 * 1024 * 1024


def split(x):
    hi = x.astype(bf16)
    return hi, (x - hi.astype(f32)).astype(bf16)


def dg(a, b, ca, cb):
    return lax.dot_general(a, b, (((ca,), (cb,)), ((), ())), preferred_element_type=f32)


def dots(a, b, ca, cb):
    return dg(a[0], b[0], ca, cb) + dg(a[0], b[1], ca, cb) + dg(a[1], b[0], ca, cb)


def dot3(a, b, ca=1, cb=0):
    return dots(split(a), split(b), ca, cb)


def lane_low(shape):
    return lax.broadcasted_iota(jnp.int32, shape, len(shape) - 1) < PAIR // 2


def spread(compact):
    low = lane_low(compact.shape)
    zero = jnp.zeros_like(compact)
    return jnp.concatenate([jnp.where(low, compact, zero), jnp.where(low, zero, compact)], axis=0)


def compacted(block):
    half = block.shape[0] // 2
    return jnp.where(lane_low((half, block.shape[1])), block[:half], block[half:])


def row_of(column):
    return jnp.transpose(jnp.broadcast_to(column, (PAIR, PAIR)))[0:1, :]


def column_of(row):
    return jnp.transpose(jnp.broadcast_to(row, (PAIR, PAIR)))


def diagonal_mask():
    rows = lax.broadcasted_iota(jnp.int32, (PAIR, PAIR), 0) < PAIR // 2
    return rows == lane_low((PAIR, PAIR))


def block_sum(x):
    halves = x.reshape(2, x.shape[0] // 2, x.shape[1])
    total = jnp.sum(halves, axis=1, keepdims=True)
    return jnp.broadcast_to(total, halves.shape).reshape(x.shape)


def block_max(x):
    halves = x.reshape(2, x.shape[0] // 2, x.shape[1])
    total = jnp.max(halves, axis=1, keepdims=True)
    return jnp.broadcast_to(total, halves.shape).reshape(x.shape)


def params(**more):
    return pltpu.CompilerParams(vmem_limit_bytes=LIMIT, **more)


def whole(shape):
    return pl.BlockSpec(shape, lambda *_: (0,) * len(shape))


def per_item(shape):
    return pl.BlockSpec((1,) + shape, lambda i, *_: (i,) + (0,) * len(shape))


class Seat:
    def __init__(self, n):
        self.n, self.nz = n, n // 2
        self.me = lax.axis_index("seq")
        self.core = lax.rem(self.me, 2)
        self.z = self.me // 2
        self.owner = self.core * self.nz + self.z
        self.partner = self.me + 1 - 2 * self.core
        self.extra = lax.rem(self.me + 2 * self.core - 1 + n, n)

    def ahead(self, j):
        return lax.rem(self.z + j, self.nz)

    def behind(self, j):
        return lax.rem(self.z - j + self.nz, self.nz)

    def at(self, z):
        return 2 * z + self.core

    def hello(self, edges):
        others = [self.partner] + [self.at(self.ahead(j)) for j in range(1, self.nz)]
        if edges:
            others.append(self.extra)
        barrier = pltpu.get_barrier_semaphore()
        for other in others:
            pl.semaphore_signal(barrier, inc=1, device_id={"seq": other}, device_id_type=MESH)
        pl.semaphore_wait(barrier, len(others))


MESH = pl.DeviceIdType.MESH


def remote(src, dst, send, recv, device):
    return pltpu.make_async_remote_copy(
        src_ref=src, dst_ref=dst, send_sem=send, recv_sem=recv,
        device_id={"seq": device}, device_id_type=MESH,
    )


class Reduce:
    def __init__(self, seat, chunks, first, acc, second, send, recv):
        self.seat, self.chunks, self.first, self.acc, self.second = seat, chunks, first, acc, second
        self.send, self.recv = send, recv
        self.across = remote(chunks.at[1 - seat.core], first, send.at[0], recv.at[0], seat.partner)
        self.along = [
            remote(
                acc.at[seat.ahead(j)], second.at[j - 1], send.at[j], recv.at[j],
                seat.at(seat.ahead(j)),
            )
            for j in range(1, seat.nz)
        ]

    def start(self):
        self.across.start()

    def middle(self, merge):
        self.across.wait()
        for z in range(self.seat.nz):
            self.acc[z] = merge([self.chunks.at[self.seat.core, z], self.first.at[z]])
        for copy in self.along:
            copy.start()

    def finish(self, merge):
        for copy in self.along:
            copy.wait()
        refs = [self.acc.at[self.seat.z]] + [self.second.at[j] for j in range(self.seat.nz - 1)]
        return merge(refs)

    @staticmethod
    def scratch(n, shape):
        nz = n // 2
        return [
            VM((nz,) + shape, f32),
            VM((nz,) + shape, f32),
            VM((nz - 1,) + shape, f32),
            pltpu.SemaphoreType.DMA((nz,)),
            pltpu.SemaphoreType.DMA((nz,)),
        ]


class Gather:
    def __init__(self, seat, out, send, recv):
        own = out.at[seat.core, seat.z]
        self.along = [
            remote(own, own, send.at[j], recv.at[j], seat.at(seat.ahead(j)))
            for j in range(1, seat.nz)
        ]
        self.across = [remote(own, own, send.at[0], recv.at[0], seat.partner)]
        for j in range(1, seat.nz):
            block = out.at[seat.core, seat.behind(j)]
            k = seat.nz + j
            self.across.append(remote(block, block, send.at[k], recv.at[k], seat.partner))

    def start(self):
        for copy in self.along:
            copy.start()
        self.across[0].start()

    def forward(self):
        for copy, onward in zip(self.along, self.across[1:]):
            copy.wait_recv()
            onward.start()

    def finish(self):
        for copy in self.along:
            copy.wait_send()
        for copy in self.across:
            copy.wait()

    @staticmethod
    def scratch(n):
        return [pltpu.SemaphoreType.DMA((n,)), pltpu.SemaphoreType.DMA((n,))]


class Edges:
    def __init__(self, seat, sides, halos, send, recv):
        self.seat, self.halos = seat, halos
        core = seat.core
        self.copies = [
            remote(sides.at[1 - core], halos.at[core], send.at[0], recv.at[0], seat.partner),
            remote(sides.at[core], halos.at[1 - core], send.at[1], recv.at[1], seat.extra),
        ]

    def start(self):
        for copy in self.copies:
            copy.start()

    def finish(self, out):
        for copy in self.copies:
            copy.wait()
        seat = self.seat
        inner = (jnp.where(seat.me > 0, 1.0, 0.0), jnp.where(seat.me < seat.n - 1, 1.0, 0.0))
        for side in range(2):
            out[side] = self.halos[side] * inner[side]

    @staticmethod
    def scratch(shape):
        return [VM(shape, f32), pltpu.SemaphoreType.DMA((2,)), pltpu.SemaphoreType.DMA((2,))]


def add_all(refs):
    return functools.reduce(lambda x, y: x + y, [r[...] for r in refs])


def project_kernel(n, items, factor, tok_ref, mem_ref, wq_ref, wk_ref, wv_ref, vec_ref,
                   q_ref, k_ref, v_ref, lq_ref, lk_ref, inv_ref,
                   sums, land, halves, *scratch):
    seat = Seat(n)
    rows = items * MARKS // n
    width = tok_ref.shape[2]
    reduce = Reduce(seat, sums, *scratch[:5])
    gather = Gather(seat, land, *scratch[5:])
    seat.hello(False)
    for item in range(items):
        member = mem_ref[item].astype(bf16)
        hi, lo = split(tok_ref[item])
        total = dg(member, hi, 1, 0) + dg(member, lo, 1, 0)
        count = jnp.sum(mem_ref[item], axis=1, keepdims=True)
        for part in range(MARKS // rows):
            c = item * (MARKS // rows) + part
            piece = slice(part * rows, (part + 1) * rows)
            sums[c // seat.nz, c % seat.nz, :, :width] = total[piece]
            sums[c // seat.nz, c % seat.nz, :, width:] = jnp.broadcast_to(
                count[piece], (rows, PAIR)
            )
    reduce.start()
    b_query, b_value = vec_ref[0:1, :], vec_ref[1:2, :]
    for place, w_ref in enumerate((wq_ref, wk_ref, wv_ref)):
        hi, lo = split(w_ref[...])
        halves[2 * place], halves[2 * place + 1] = hi, lo

    def project(place, out_ref, bias, scale):
        def lap(item, _):
            x = split(tok_ref[item])
            y = dots(x, (halves[2 * place], halves[2 * place + 1]), 1, 0)
            y = y if bias is None else y + bias
            out_ref[item] = y if scale is None else y * scale
            return 0

        lax.fori_loop(0, items, lap, 0)

    project(0, q_ref, b_query, factor)
    reduce.middle(add_all)
    project(1, k_ref, None, factor)
    land[seat.core, seat.z] = reduce.finish(add_all)
    gather.start()
    project(2, v_ref, b_value, None)
    gather.forward()
    gather.finish()
    whole_land = land[...].reshape(items * MARKS, width + PAIR)
    divisor = jnp.maximum(whole_land[:, width:], 1.0)
    inv_ref[...] = (1.0 / divisor).reshape(items, MARKS, PAIR)
    filled = whole_land[:, width : width + 1] / divisor[:, 0:1]
    x = split(whole_land[:, :width] / divisor[:, 0:1])
    lq = (dots(x, (halves[0], halves[1]), 1, 0) + filled * b_query) * factor
    lk = dots(x, (halves[2], halves[3]), 1, 0) * factor
    lq_ref[...] = lq.reshape(items, MARKS, width)
    lk_ref[...] = lk.reshape(items, MARKS, width)


def project_call(tokens, member_t, w_query, w_key, w_value, vectors, n, factor):
    items, span, width = tokens.shape
    rows = items * MARKS // n
    big = jax.ShapeDtypeStruct((items, span, width), f32)
    small = jax.ShapeDtypeStruct((items, MARKS, width), f32)
    return pl.pallas_call(
        functools.partial(project_kernel, n, items, factor),
        out_shape=[big, big, big, small, small, jax.ShapeDtypeStruct((items, MARKS, PAIR), f32)],
        in_specs=[pl.BlockSpec(memory_space=VM)] * 6,
        out_specs=[pl.BlockSpec(memory_space=VM)] * 6,
        scratch_shapes=[
            VM((2, n // 2, rows, width + PAIR), f32),
            VM((2, n // 2, rows, width + PAIR), f32),
            VM((6, width, width), bf16),
        ]
        + Reduce.scratch(n, (rows, width + PAIR))
        + Gather.scratch(n),
        compiler_params=params(collective_id=0, has_side_effects=True),
        name="project",
    )(tokens, member_t, w_query, w_key, w_value, vectors)


def scores_kernel(per, pairs, q_ref, k_ref, v_ref, lq_ref, lk_ref, use_ref, k1_ref, w3_ref, top_ref, chunk):
    item = pl.program_id(0)
    stats = per * MARKS

    @pl.when(item == 0)
    def _():
        chunk[...] = jnp.zeros_like(chunk)

    use = use_ref[0]
    for p in range(pairs):
        lanes = slice(p * PAIR, (p + 1) * PAIR)
        q = q_ref[0, :, lanes]
        s1 = dot3(spread(lk_ref[0, :, lanes]), q, 1, 1)
        e1 = jnp.exp(s1 - block_max(s1))
        k1_ref[0, lanes, :] = e1 / block_sum(e1)
        s3 = dot3(spread(lq_ref[0, :, lanes]), k_ref[0, :, lanes], 1, 1)
        masked = jnp.where(use > 0, s3, -1e30)
        top = jnp.max(masked, axis=1, keepdims=True)
        w3 = jnp.exp(masked - top) * use
        w3_ref[0, lanes, :] = w3
        total = jnp.sum(w3, axis=1, keepdims=True)
        weighted = compacted(dot3(w3, v_ref[0, :, lanes]))
        top_row = row_of(top)
        top_ref[0, p : p + 1, :] = top_row
        g = item * pairs + p
        owner, place = g // per, g % per
        chunk[owner, pl.ds(pl.multiple_of(place * MARKS, MARKS), MARKS), :] = weighted
        chunk[owner, pl.ds(stats + 2 * place, 1), :] = top_row
        chunk[owner, pl.ds(stats + 2 * place + 1, 1), :] = row_of(total)


def scores_call(q, k, v, lq, lk, use_row, n, per, pairs, chunk_rows):
    items, span, width = q.shape
    return pl.pallas_call(
        functools.partial(scores_kernel, per, pairs),
        out_shape=[
            jax.ShapeDtypeStruct((items, width, span), f32),
            jax.ShapeDtypeStruct((items, width, span), f32),
            jax.ShapeDtypeStruct((items, 8, PAIR), f32),
            jax.ShapeDtypeStruct((n, chunk_rows, PAIR), f32),
        ],
        grid=(items,),
        in_specs=[per_item((span, width))] * 3
        + [per_item((MARKS, width))] * 2
        + [per_item((1, span))],
        out_specs=[per_item((width, span))] * 2
        + [per_item((8, PAIR)), whole((n, chunk_rows, PAIR))],
        compiler_params=params(),
        name="scores",
    )(q, k, v, lq, lk, use_row)


def owned_land(seat, per, pairs, ref, into):
    for place in range(per):
        g = lax.rem(seat.owner * per + place, ref.shape[0] * pairs)
        item, p = g // pairs, lax.rem(g, pairs)
        into[place] = ref[item, :, pl.ds(pl.multiple_of(p * PAIR, PAIR), PAIR)]


def newton_step(a, z, eye):
    pr = dot3(a, z)
    n1 = 7.0 * eye - pr
    n2 = 15.0 * eye - dot3(pr, n1)
    n3 = 13.0 * eye - dot3(pr, n2)
    return pr, n1, n2, n3


def unit():
    rows = lax.broadcasted_iota(jnp.int32, (PAIR, PAIR), 0)
    return (rows == lax.broadcasted_iota(jnp.int32, (PAIR, PAIR), 1)).astype(f32)


def head_total(x):
    return block_sum(jnp.sum(x, axis=1, keepdims=True))


def merged(per, refs):
    stats = per * MARKS
    weights, rest = [], []
    for place in range(per):
        tops = [r[stats + 2 * place : stats + 2 * place + 1, :] for r in refs]
        largest = functools.reduce(jnp.maximum, tops)
        total = jnp.zeros_like(largest)
        weighted = jnp.zeros((MARKS, PAIR), f32)
        for r, top in zip(refs, tops):
            scale = jnp.exp(top - largest)
            total = total + scale * r[stats + 2 * place + 1 : stats + 2 * place + 2, :]
            scales = compacted(column_of(scale))
            weighted = weighted + scales * r[place * MARKS : (place + 1) * MARKS, :]
        weights.append(weighted)
        rest += [largest, total]
    filler = jnp.zeros((refs[0].shape[0] - stats - 2 * per, PAIR), f32)
    return jnp.concatenate(weights + rest + [filler], axis=0)


def exchange_kernel(n, per, pairs, chunk_ref, lq_ref, lk_ref, side_ref,
                    a_ref, z_ref, lqo_ref, lko_ref, ctx_ref, out_ref, halo_ref, mine, *scratch):
    seat = Seat(n)
    merge = functools.partial(merged, per)
    reduce = Reduce(seat, chunk_ref, *scratch[:5])
    gather = Gather(seat, out_ref, *scratch[5:7])
    edges = Edges(seat, side_ref, *scratch[7:])
    seat.hello(True)
    reduce.start()
    edges.start()
    owned_land(seat, per, pairs, lq_ref, lqo_ref)
    owned_land(seat, per, pairs, lk_ref, lko_ref)
    diagonal = diagonal_mask()
    eye = unit()
    for place in range(per):
        s2 = dot3(spread(lqo_ref[place]), spread(lko_ref[place]), 1, 1)
        s2 = jnp.where(diagonal, s2, -1e30)
        e2 = jnp.exp(s2 - jnp.max(s2, axis=1, keepdims=True))
        e2 = jnp.where(diagonal, e2, 0.0)
        a = e2 / jnp.sum(e2, axis=1, keepdims=True)
        a_ref[place] = a
        z_ref[0, place] = jnp.transpose(a) / head_total(a * a)
    reduce.middle(merge)

    def lap(step, _):
        for place in range(per):
            z = z_ref[step, place]
            _, _, _, n3 = newton_step(a_ref[place], z, eye)
            z_ref[step + 1, place] = 0.25 * dot3(z, n3)
        return 0

    lax.fori_loop(0, NEWTON, lap, 0)
    mine[...] = reduce.finish(merge)
    stats = per * MARKS
    block = out_ref.at[seat.core, seat.z]
    block[stats:, :] = mine[stats:, :]
    for place in range(per):
        rows = slice(place * MARKS, (place + 1) * MARKS)
        total = mine[stats + 2 * place + 1 : stats + 2 * place + 2, :]
        context = mine[rows, :] / compacted(column_of(total))
        ctx_ref[place] = context
        block[rows, :] = compacted(dot3(z_ref[NEWTON, place], spread(context)))
    gather.start()
    edges.finish(halo_ref)
    gather.forward()
    gather.finish()


def exchange_call(chunks, lq, lk, sides, n, per, pairs):
    rows = chunks.shape[1]
    small = jax.ShapeDtypeStruct((per, MARKS, PAIR), f32)
    blocks = (2, n // 2, rows, PAIR)
    out = pl.pallas_call(
        functools.partial(exchange_kernel, n, per, pairs),
        out_shape=[
            jax.ShapeDtypeStruct((per, PAIR, PAIR), f32),
            jax.ShapeDtypeStruct((NEWTON + 1, per, PAIR, PAIR), f32),
            small,
            small,
            small,
            jax.ShapeDtypeStruct(blocks, f32),
            jax.ShapeDtypeStruct(sides.shape, f32),
        ],
        in_specs=[pl.BlockSpec(memory_space=VM)] * 4,
        out_specs=[pl.BlockSpec(memory_space=VM)] * 7,
        scratch_shapes=[VM((rows, PAIR), f32)]
        + Reduce.scratch(n, (rows, PAIR))
        + Gather.scratch(n)
        + Edges.scratch(sides.shape),
        compiler_params=params(collective_id=1, has_side_effects=True),
        name="exchange",
    )(chunks.reshape(blocks), lq, lk, sides)
    return list(out[:5]) + [out[5].reshape(n, rows, PAIR), out[6]]


def toeplitz(taps_row, rows):
    wide = jnp.broadcast_to(taps_row, (rows, 2 * PAIR))
    return pltpu.roll(wide, 0, 1, stride=1, stride_axis=0)


def keep_taps(taps_ref, into, heads):
    for h in range(heads):
        hi, lo = split(toeplitz(taps_ref[h : h + 1, :], PAIR))
        into[0, h] = hi
        into[1, h] = lo


def keep_window(win, left, middle, right, margin, span):
    for rows, part in (
        (slice(0, margin), left),
        (slice(margin, margin + span), middle),
        (slice(margin + span, 2 * margin + span), right),
    ):
        hi, lo = split(part)
        win[0, rows, :] = hi
        win[1, rows, :] = lo


def convolve(taps, win, p, block, window):
    lanes = slice(p * PAIR, (p + 1) * PAIR)
    rows = slice(block * PAIR, block * PAIR + window)
    v = (win[0, rows, lanes], win[1, rows, lanes])
    halves = []
    for h in (2 * p, 2 * p + 1):
        t = (taps[0, h, :, :window], taps[1, h, :, :window])
        halves.append(dots(t, v, 1, 0))
    return jnp.where(lane_low((PAIR, PAIR)), halves[0], halves[1])


def owned_by(g, per):
    return g // per, g % per


def mix_kernel(per, pairs, margin, held, k1_ref, v_ref, use_ref, left_ref, right_ref, taps_ref, out_ref, taps, win):
    item = pl.program_id(0)
    span = v_ref.shape[1]
    window = PAIR + 2 * margin

    @pl.when(item == 0)
    def _():
        keep_taps(taps_ref, taps, 2 * pairs)

    keep_window(win, left_ref[0, 0], v_ref[0] * use_ref[0], right_ref[0, 0], margin, span)
    for p in range(pairs):
        lanes = slice(p * PAIR, (p + 1) * PAIR)
        slot, place = owned_by(item * pairs + p, per)
        mixed = held[slot, pl.ds(pl.multiple_of(place * MARKS, MARKS), MARKS), :]
        nystrom = dot3(k1_ref[0, lanes, :], spread(mixed), 0, 0)
        for block in range(span // PAIR):
            rows = slice(block * PAIR, (block + 1) * PAIR)
            out_ref[0, rows, lanes] = nystrom[rows] + convolve(taps, win, p, block, window)


def halo_specs(margin, width):
    return [
        pl.BlockSpec((1, 1, margin, width), lambda i, side=side: (side, i, 0, 0))
        for side in range(2)
    ]


def mix_call(blocks, k1, v, use_col, halos, taps, per, pairs, margin):
    items, span, width = v.shape
    return pl.pallas_call(
        functools.partial(mix_kernel, per, pairs, margin),
        out_shape=jax.ShapeDtypeStruct((items, span, width), f32),
        grid=(items,),
        in_specs=[whole(blocks.shape)]
        + [per_item((width, span)), per_item((span, width)), per_item((span, 1))]
        + halo_specs(margin, width)
        + [whole(taps.shape)],
        out_specs=per_item((span, width)),
        scratch_shapes=[
            VM((2, 2 * pairs, PAIR, 2 * PAIR), bf16),
            VM((2, span + 2 * margin, width), bf16),
        ],
        compiler_params=params(),
        name="mix",
    )(blocks, k1, v, use_col, halos, halos, taps)


def erf(x):
    x = jnp.clip(x, -3.832506856900711, 3.832506856900711)
    s = x * x
    a = 0.00022905065861350646
    for c in (0.0034082910107109506, 0.050955695062380861, 0.18520832239976145, 1.128379143519084):
        a = a * s + c
    b = -1.1791602954361697e-7
    for c in (
        0.000023547966471313185,
        0.0010179625278914885,
        0.014070470171167667,
        0.11098505178285362,
        0.49746925110067538,
        1.0,
    ):
        b = b * s + c
    return x * a / b


def normalize(x):
    center = x - jnp.mean(x, axis=-1, keepdims=True)
    inv_root = lax.rsqrt(jnp.mean(center * center, axis=-1, keepdims=True) + epsilon)
    return center * inv_root, inv_root


def norm_back(grad, scaled, inv_root):
    first = jnp.mean(grad, axis=-1, keepdims=True)
    second = jnp.mean(grad * scaled, axis=-1, keepdims=True)
    return inv_root * (grad - first - scaled * second)


def rows_kernel(
    ff_tile,
    x_ref,
    tok_ref,
    cot_ref,
    wo_h,
    wo_l,
    wu_h,
    wu_l,
    wd_h,
    wd_l,
    vec_ref,
    bup_ref,
    out_ref,
    act_ref,
    u_ref,
    r2_ref,
    h1_ref,
    r1_ref,
    og_ref,
    sums_ref,
    bsum_ref,
    slope,
):
    @pl.when(pl.program_id(0) == 0)
    def _():
        sums_ref[...] = jnp.zeros_like(sums_ref)
        bsum_ref[...] = jnp.zeros_like(bsum_ref)

    b_out, gain_one, shift_one = vec_ref[0:1, :], vec_ref[1:2, :], vec_ref[2:3, :]
    b_down, gain_two, shift_two = vec_ref[3:4, :], vec_ref[4:5, :], vec_ref[5:6, :]
    wo = (wo_h[...], wo_l[...])
    attention = dots(split(x_ref[...]), wo, 1, 0) + b_out
    scaled_one, root_one = normalize(tok_ref[...] + attention)
    hidden = scaled_one * gain_one + shift_one
    h1_ref[...] = hidden
    hs = split(hidden)
    ff = wu_h.shape[1]
    tiles = [slice(c, c + ff_tile) for c in range(0, ff, ff_tile)]
    down = b_down
    for c in tiles:
        pre = dots(hs, (wu_h[:, c], wu_l[:, c]), 1, 0) + bup_ref[:, c]
        phi = 0.5 + 0.5 * erf(pre * 0.7071067811865476)
        slope[:, c] = phi + pre * (0.3989422804014327 * jnp.exp(-0.5 * pre * pre))
        act = pre * phi
        act_ref[:, c] = act
        down = down + dots(split(act), (wd_h[c, :], wd_l[c, :]), 1, 0)
    scaled_two, root_two = normalize(hidden + down)
    out_ref[...] = scaled_two * gain_two + shift_two
    cot = cot_ref[...]
    r2 = norm_back(cot * gain_two, scaled_two, root_two)
    r2_ref[...] = r2
    rs = split(r2)
    grad_hidden = r2
    for c in tiles:
        u = dots(rs, (wd_h[c, :], wd_l[c, :]), 1, 1) * slope[:, c]
        u_ref[:, c] = u
        bsum_ref[:, c] += jnp.sum(u, axis=0, keepdims=True)
        grad_hidden = grad_hidden + dots(split(u), (wu_h[:, c], wu_l[:, c]), 1, 1)
    r1 = norm_back(grad_hidden * gain_one, scaled_one, root_one)
    r1_ref[...] = r1
    og_ref[...] = dots(split(r1), wo, 1, 1)
    for row, value in enumerate(
        (cot * scaled_two, cot, r2, grad_hidden * scaled_one, grad_hidden, r1)
    ):
        sums_ref[row : row + 1, :] += jnp.sum(value, axis=0, keepdims=True)


def rows_call(x, tokens, cotangent, wo, wu, wd, vectors, b_up):
    rows, width = x.shape
    ff = wu[0].shape[1]
    tile = 256
    ff_tile = 768
    wide = pl.BlockSpec((tile, width), lambda i: (i, 0))
    hidden = pl.BlockSpec((tile, ff), lambda i: (i, 0))

    def fixed(a):
        return pl.BlockSpec(a.shape, lambda i: (0, 0), pipeline_mode=pl.Buffered(1))

    narrow = jax.ShapeDtypeStruct((rows, width), f32)
    broad = jax.ShapeDtypeStruct((rows, ff), f32)
    return pl.pallas_call(
        functools.partial(rows_kernel, ff_tile),
        out_shape=[
            narrow,
            broad,
            broad,
            narrow,
            narrow,
            narrow,
            narrow,
            jax.ShapeDtypeStruct((8, width), f32),
            jax.ShapeDtypeStruct((1, ff), f32),
        ],
        grid=(rows // tile,),
        in_specs=[wide] * 3
        + [fixed(a) for a in (*wo, *wu, *wd)]
        + [fixed(vectors), fixed(b_up)],
        out_specs=[wide, hidden, hidden, wide, wide, wide, wide]
        + [pl.BlockSpec((8, width), lambda i: (0, 0)), pl.BlockSpec((1, ff), lambda i: (0, 0))],
        scratch_shapes=[VM((tile, ff), f32)],
        compiler_params=params(),
        name="rows",
    )(x, tokens, cotangent, *wo, *wu, *wd, vectors, b_up)


def one_back_kernel(per, pairs, held, k1_ref, og_ref, q_ref, lk_ref, gq_ref, chunk):
    item = pl.program_id(0)

    @pl.when(item == 0)
    def _():
        chunk[...] = jnp.zeros_like(chunk)

    for p in range(pairs):
        lanes = slice(p * PAIR, (p + 1) * PAIR)
        owner, place = owned_by(item * pairs + p, per)
        mixed = spread(held[owner, pl.ds(pl.multiple_of(place * MARKS, MARKS), MARKS), :])
        k1 = k1_ref[0, lanes, :]
        og = split(og_ref[0, :, lanes])
        part_mixed = compacted(dots(split(k1), og, 1, 0))
        grad = dots(split(mixed), og, 1, 1)
        scores = k1 * (grad - block_sum(k1 * grad))
        ss = split(scores)
        gq_ref[0, :, lanes] = dots(ss, split(spread(lk_ref[0, :, lanes])), 0, 0)
        part_key = compacted(dots(ss, split(q_ref[0, :, lanes]), 1, 0))
        chunk[owner, pl.ds(pl.multiple_of(place * 2 * MARKS, 2 * MARKS), MARKS), :] = part_mixed
        chunk[owner, pl.ds(pl.multiple_of(place * 2 * MARKS + MARKS, MARKS), MARKS), :] = part_key


def one_back_call(blocks, k1, og, q, lk, per, pairs):
    items, span, width = q.shape
    out = (blocks.shape[0], 2 * per * MARKS, PAIR)
    wide = per_item((span, width))
    return pl.pallas_call(
        functools.partial(one_back_kernel, per, pairs),
        out_shape=[
            jax.ShapeDtypeStruct((items, span, width), f32),
            jax.ShapeDtypeStruct(out, f32),
        ],
        grid=(items,),
        in_specs=[whole(blocks.shape), per_item((width, span)), wide, wide]
        + [per_item((MARKS, width))],
        out_specs=[wide, whole(out)],
        compiler_params=params(),
        name="one_back",
    )(blocks, k1, og, q, lk)


def conv_back_kernel(pairs, margin, og_ref, gl_ref, gr_ref, v_ref, vl_ref, vr_ref, use_ref, taps_ref, *refs):
    gv_ref, gtaps_ref, taps, gwin, vwin, acc = refs
    item = pl.program_id(0)
    span = v_ref.shape[1]
    window = PAIR + 2 * margin

    @pl.when(item == 0)
    def _():
        keep_taps(taps_ref, taps, 2 * pairs)
        acc[...] = jnp.zeros_like(acc)

    use = use_ref[0]
    keep_window(gwin, gl_ref[0, 0], og_ref[0], gr_ref[0, 0], margin, span)
    keep_window(vwin, vl_ref[0, 0], v_ref[0] * use, vr_ref[0, 0], margin, span)
    for p in range(pairs):
        lanes = slice(p * PAIR, (p + 1) * PAIR)
        for block in range(span // PAIR):
            rows = slice(block * PAIR, (block + 1) * PAIR)
            gv_ref[0, rows, lanes] = convolve(taps, gwin, p, block, window) * use[rows]
            inner = slice(margin + block * PAIR, margin + (block + 1) * PAIR)
            outer = slice(block * PAIR, block * PAIR + window)
            v = (vwin[0, outer, lanes], vwin[1, outer, lanes])
            low = lane_low((PAIR, PAIR))
            hi, lo = gwin[0, inner, lanes], gwin[1, inner, lanes]
            zero = jnp.zeros_like(hi)
            acc[2 * p] += dots((jnp.where(low, hi, zero), jnp.where(low, lo, zero)), v, 1, 1)
            acc[2 * p + 1] += dots((jnp.where(low, zero, hi), jnp.where(low, zero, lo)), v, 1, 1)

    @pl.when(item == pl.num_programs(0) - 1)
    def _():
        rows = lax.broadcasted_iota(jnp.int32, (PAIR, PAIR), 0)
        flip = (rows + lax.broadcasted_iota(jnp.int32, (PAIR, PAIR), 1) == PAIR - 1).astype(bf16)
        for h in range(2 * pairs):
            c = acc[h]
            c = jnp.concatenate([c, jnp.zeros((PAIR, 2 * PAIR - window), f32)], axis=1)
            hi = c.astype(bf16)
            rest = c - hi.astype(f32)
            mid = rest.astype(bf16)
            low = (rest - mid.astype(f32)).astype(bf16)
            c = dg(flip, hi, 1, 0) + dg(flip, mid, 1, 0) + dg(flip, low, 1, 0)
            c = pltpu.roll(c, 0, 1, stride=1, stride_axis=0)
            gtaps_ref[h : h + 1, :] = jnp.sum(c, axis=0, keepdims=True)


def conv_back_call(og, ghalos, v, vhalos, use_col, taps, pairs, margin):
    items, span, width = v.shape
    window = PAIR + 2 * margin
    wide, edge = per_item((span, width)), halo_specs(margin, width)
    rows = -(-2 * pairs // 8) * 8
    return pl.pallas_call(
        functools.partial(conv_back_kernel, pairs, margin),
        out_shape=[
            jax.ShapeDtypeStruct((items, span, width), f32),
            jax.ShapeDtypeStruct((rows, 2 * PAIR), f32),
        ],
        grid=(items,),
        in_specs=[wide, *edge, wide, *edge, per_item((span, 1)), whole(taps.shape)],
        out_specs=[wide, whole((rows, 2 * PAIR))],
        scratch_shapes=[
            VM((2, 2 * pairs, PAIR, 2 * PAIR), bf16),
            VM((2, span + 2 * margin, width), bf16),
            VM((2, span + 2 * margin, width), bf16),
            VM((2 * pairs, PAIR, window), f32),
        ],
        compiler_params=params(),
        name="conv_back",
    )(og, ghalos, ghalos, v, vhalos, vhalos, use_col, taps)


def exchange_back_kernel(n, per, chunk_ref, side_ref, ctx_ref, a_ref, z_ref, lq_ref, lk_ref,
                         out_ref, gq_ref, gk_ref, halo_ref, gm, gz, ga, *scratch):
    seat = Seat(n)
    reduce = Reduce(seat, chunk_ref, *scratch[:5])
    gather = Gather(seat, out_ref, *scratch[5:7])
    edges = Edges(seat, side_ref, *scratch[7:])
    seat.hello(True)
    reduce.start()
    edges.start()
    reduce.middle(add_all)
    diagonal = diagonal_mask()
    eye = unit()
    stats = per * MARKS
    gm[...] = reduce.finish(add_all)
    block = out_ref.at[seat.core, seat.z]
    block[stats:, :] = jnp.zeros((block.shape[0] - stats, PAIR), f32)
    for place in range(per):
        mixed = spread(gm[place * 2 * MARKS : place * 2 * MARKS + MARKS, :])
        context = spread(ctx_ref[place])
        grad = dot3(jnp.transpose(z_ref[NEWTON, place]), mixed)
        block[place * MARKS : (place + 1) * MARKS, :] = compacted(grad)
        dot = jnp.sum(grad * context, axis=1, keepdims=True)
        block[stats + place : stats + place + 1, :] = row_of(dot)
        gz[place] = jnp.where(diagonal, dot3(mixed, context, 1, 1), 0.0)
        ga[place] = jnp.zeros((PAIR, PAIR), f32)
    gather.start()

    def lap(back, _):
        step = NEWTON - 1 - back
        for place in range(per):
            a, z, g = a_ref[place], z_ref[step, place], 0.25 * gz[place]
            pr, n1, n2, n3 = newton_step(a, z, eye)
            back_three = dot3(jnp.transpose(z), g)
            turned = jnp.transpose(pr)
            back_two = -dot3(turned, back_three)
            back_one = -dot3(turned, back_two)
            grad = -dot3(back_three, n2, 1, 1) - dot3(back_two, n1, 1, 1) - back_one
            ga[place] += dot3(grad, z, 1, 1)
            gz[place] = dot3(g, n3, 1, 1) + dot3(jnp.transpose(a), grad)
        return 0

    lax.fori_loop(0, NEWTON - 1, lap, 0)
    gather.forward()
    lax.fori_loop(NEWTON - 1, NEWTON, lap, 0)
    for place in range(per):
        a, g = a_ref[place], jnp.transpose(gz[place])
        norm = head_total(a * a)
        slope = -head_total(g * a) / (norm * norm)
        grad = ga[place] + g / norm + 2.0 * slope * a
        scores = a * (grad - jnp.sum(a * grad, axis=1, keepdims=True))
        gq_ref[place] = compacted(dot3(scores, spread(lk_ref[place])))
        gk_ref[place] = gm[place * 2 * MARKS + MARKS : (place + 1) * 2 * MARKS, :] + compacted(
            dot3(jnp.transpose(scores), spread(lq_ref[place]))
        )
    edges.finish(halo_ref)
    gather.finish()


def exchange_back_call(chunks, sides, ctx, a, z, lq, lk, n, rows):
    per = ctx.shape[0]
    small = jax.ShapeDtypeStruct(ctx.shape, f32)
    chunk = chunks.shape[1:]
    blocks = (2, n // 2, rows, PAIR)
    out = pl.pallas_call(
        functools.partial(exchange_back_kernel, n, per),
        out_shape=[
            jax.ShapeDtypeStruct(blocks, f32),
            small,
            small,
            jax.ShapeDtypeStruct(sides.shape, f32),
        ],
        in_specs=[pl.BlockSpec(memory_space=VM)] * 7,
        out_specs=[pl.BlockSpec(memory_space=VM)] * 4,
        scratch_shapes=[VM(chunk, f32)]
        + [VM((per, PAIR, PAIR), f32)] * 2
        + Reduce.scratch(n, chunk)
        + Gather.scratch(n)
        + Edges.scratch(sides.shape),
        compiler_params=params(collective_id=2, has_side_effects=True),
        name="exchange_back",
    )(chunks.reshape((2, n // 2) + chunk), sides, ctx, a, z, lq, lk)
    return [out[0].reshape(n, rows, PAIR)] + list(out[1:])


def three_back_kernel(per, pairs, held, stat, w3_ref, top_ref, v_ref, k_ref, gvc_ref, lq_ref,
                      gv_ref, gk_ref, chunk):
    item = pl.program_id(0)
    stats = per * MARKS

    @pl.when(item == 0)
    def _():
        chunk[...] = jnp.zeros_like(chunk)

    for p in range(pairs):
        lanes = slice(p * PAIR, (p + 1) * PAIR)
        owner, place = owned_by(item * pairs + p, per)
        grad = split(spread(held[owner, pl.ds(pl.multiple_of(place * MARKS, MARKS), MARKS), :]))
        row_dot = column_of(held[owner, pl.ds(stats + place, 1), :])
        largest = stat[owner, pl.ds(stats + 2 * place, 1), :]
        total = stat[owner, pl.ds(stats + 2 * place + 1, 1), :]
        scale = column_of(jnp.exp(top_ref[0, p : p + 1, :] - largest) / total)
        k3 = w3_ref[0, lanes, :] * scale[:, 0:1]
        gk3 = dots(grad, split(v_ref[0, :, lanes]), 1, 1)
        scores = split(k3 * (gk3 - row_dot[:, 0:1]))
        gv_ref[0, :, lanes] = gvc_ref[0, :, lanes] + dots(split(k3), grad, 0, 0)
        gk_ref[0, :, lanes] = dots(scores, split(spread(lq_ref[0, :, lanes])), 0, 0)
        part = compacted(dots(scores, split(k_ref[0, :, lanes]), 1, 0))
        chunk[owner, pl.ds(pl.multiple_of(place * MARKS, MARKS), MARKS), :] = part


def three_back_call(grads, blocks, w3, top, v, k, gv_conv, lq, per, pairs):
    items, span, width = v.shape
    out = (blocks.shape[0], per * MARKS, PAIR)
    wide = per_item((span, width))
    shape = jax.ShapeDtypeStruct((items, span, width), f32)
    return pl.pallas_call(
        functools.partial(three_back_kernel, per, pairs),
        out_shape=[shape, shape, jax.ShapeDtypeStruct(out, f32)],
        grid=(items,),
        in_specs=[whole(blocks.shape)] * 2
        + [per_item((width, span)), per_item((8, PAIR)), wide, wide, wide]
        + [per_item((MARKS, width))],
        out_specs=[wide, wide, whole(out)],
        compiler_params=params(),
        name="three_back",
    )(grads, blocks, w3, top, v, k, gv_conv, lq)


def land_exchange_kernel(n, per, chunk_ref, q_ref, k_ref, out_ref, *scratch):
    seat = Seat(n)
    reduce = Reduce(seat, chunk_ref, *scratch[:5])
    gather = Gather(seat, out_ref, *scratch[5:])
    seat.hello(False)
    reduce.start()
    reduce.middle(add_all)
    half = per * MARKS
    block = out_ref.at[seat.core, seat.z]
    block[half:, :] = k_ref[...]
    block[:half, :] = q_ref[...] + reduce.finish(add_all)
    gather.start()
    gather.forward()
    gather.finish()


def land_exchange_call(chunks, own_q, own_k, n):
    per = own_q.shape[0]
    half = per * MARKS
    blocks = (2, n // 2, 2 * half, PAIR)
    return pl.pallas_call(
        functools.partial(land_exchange_kernel, n, per),
        out_shape=jax.ShapeDtypeStruct(blocks, f32),
        in_specs=[pl.BlockSpec(memory_space=VM)] * 3,
        out_specs=pl.BlockSpec(memory_space=VM),
        scratch_shapes=Reduce.scratch(n, (half, PAIR)) + Gather.scratch(n),
        compiler_params=params(collective_id=3, has_side_effects=True),
        name="land_exchange",
    )(chunks.reshape(2, n // 2, half, PAIR), own_q.reshape(half, PAIR), own_k.reshape(half, PAIR)).reshape(
        n, 2 * half, PAIR
    )


def land_back_kernel(per, pairs, factor, held, gq_ref, gk_ref, gv_ref, mem_ref, inv_ref, oq_ref, ok_ref, sums_ref):
    item = pl.program_id(0)
    half = per * MARKS

    @pl.when(item == 0)
    def _():
        sums_ref[...] = jnp.zeros_like(sums_ref)

    member = mem_ref[0].astype(bf16)
    inv = inv_ref[0]
    for p in range(pairs):
        lanes = slice(p * PAIR, (p + 1) * PAIR)
        slot, place = owned_by(item * pairs + p, per)
        for ref, out, base in ((gq_ref, oq_ref, 0), (gk_ref, ok_ref, half)):
            grad = held[slot, pl.ds(pl.multiple_of(base + place * MARKS, MARKS), MARKS), :]
            hi, lo = split(grad * inv)
            landed = dg(member, hi, 0, 0) + dg(member, lo, 0, 0)
            out[0, :, lanes] = (ref[0, :, lanes] + landed) * factor
        sums_ref[0:1, lanes] += jnp.sum(oq_ref[0, :, lanes], axis=0, keepdims=True)
        sums_ref[1:2, lanes] += jnp.sum(gv_ref[0, :, lanes], axis=0, keepdims=True)


def land_back_call(blocks, gq, gk, gv, member_t, inv, per, pairs, factor):
    items, span, width = gq.shape
    wide = per_item((span, width))
    shape = jax.ShapeDtypeStruct((items, span, width), f32)
    return pl.pallas_call(
        functools.partial(land_back_kernel, per, pairs, factor),
        out_shape=[shape, shape, jax.ShapeDtypeStruct((8, width), f32)],
        grid=(items,),
        in_specs=[whole(blocks.shape), wide, wide, wide]
        + [per_item((MARKS, span)), per_item((MARKS, PAIR))],
        out_specs=[wide, wide, whole((8, width))],
        compiler_params=params(),
        name="land_back",
    )(blocks, gq, gk, gv, member_t, inv)


def partner_of(index, bit):
    return index + bit - 2 * bit * lax.rem(index // bit, 2)


class Loads:
    def __init__(self, sources, slots, sems):
        self.count = slots.shape[0]
        self.views = [slots.at[i % self.count, : src.shape[0]] for i, src in enumerate(sources)]
        self.copies = [
            pltpu.make_async_copy(src, view, sems.at[i % self.count])
            for i, (src, view) in enumerate(zip(sources, self.views))
        ]
        for copy in self.copies[: self.count]:
            copy.start()

    def get(self, i):
        self.copies[i].wait()
        return self.views[i]

    def release(self, i):
        if i + self.count < len(self.copies):
            self.copies[i + self.count].start()


ORDERS = ((2, 1, 3, 0), (3, 2, 1, 0), (1, 3, 2, 0))


class Scatter:
    def __init__(self, base, buffer, landings, send, recv, mine, devices):
        self.buffer, self.landings, self.mine = buffer, landings, mine
        self.stage = 0
        self.copies = []
        for stage in range(4):
            row = []
            for color, order in enumerate(ORDERS):
                dim = order[stage]
                k = (base * 3 + color) * 4 + stage
                row.append(
                    pltpu.make_async_remote_copy(
                        src_ref=self.part(color, stage, 1 - mine[dim]),
                        dst_ref=landings[stage].at[color],
                        send_sem=send.at[k],
                        recv_sem=recv.at[k],
                        device_id=devices[dim],
                        device_id_type=MESH,
                    )
                )
            self.copies.append(row)

    def part(self, color, stage, index):
        order = ORDERS[color]
        place = [slice(None)] * 4
        for dim in order[:stage]:
            place[dim] = self.mine[dim]
        place[order[stage]] = index
        return self.buffer.at[(color, *place)]

    def start(self):
        for copy in self.copies[0]:
            copy.start()

    def advance(self):
        stage = self.stage
        self.stage += 1
        for color, order in enumerate(ORDERS):
            self.copies[stage][color].wait()
            kept = self.part(color, stage, self.mine[order[stage]])
            kept[...] = kept[...] + self.landings[stage][color]
            if stage < 3:
                self.copies[stage + 1][color].start()

    def store(self, out):
        for color in range(3):
            out[color] = self.buffer[(color, *self.mine)]


def grads_kernel(
    r2_ref, act_ref, hid_ref, u_ref, r1_ref, x_ref, gq_ref, gk_ref, gv_ref, tok_ref,
    wq_ref, wk_ref, wv_ref, sums_ref, late_ref, bsum_ref, taps_ref,
    vo_ref, down_ref, up_ref, qk_ref, gt_ref, total_ref,
    slots, sa_h, sa_l, sb_h, sb_l, p_big, p_pair, r_down, r_up, r_vo, r_qk, *scratch
):
    lands = [scratch[4 * g : 4 * g + 4] for g in range(4)]
    held, caught, load_sem, core_send, core_recv, send, recv, sum_send, sum_recv = scratch[16:]
    me, dp = lax.axis_index("seq"), lax.axis_index("dp")
    core, z = lax.rem(me, 2), me // 2
    mine = (z // 2, lax.rem(z, 2), dp // 2, lax.rem(dp, 2))
    partner = {"seq": partner_of(me, 1)}
    devices = (
        {"seq": partner_of(me, 4)},
        {"seq": partner_of(me, 2)},
        {"dp": partner_of(dp, 2)},
        {"dp": partner_of(dp, 1)},
    )
    width = tok_ref.shape[1]
    ff = act_ref.shape[1]
    tiles = [pl.ds(c, width) for c in range(0, ff, width)]
    loads = Loads(
        [gv_ref, tok_ref, r1_ref, x_ref, r2_ref]
        + [act_ref.at[:, t] for t in tiles]
        + [hid_ref]
        + [u_ref.at[:, t] for t in tiles]
        + [gq_ref, gk_ref, tok_ref, gv_ref, wv_ref, gq_ref, wq_ref, gk_ref, wk_ref],
        slots,
        load_sem,
    )
    residual = pltpu.make_async_copy(r1_ref, gt_ref, load_sem.at[slots.shape[0]])
    residual.start()
    barrier = pltpu.get_barrier_semaphore()
    for device in (partner, *devices):
        pl.semaphore_signal(barrier, inc=1, device_id=device, device_id_type=MESH)
    pl.semaphore_wait(barrier, 5)

    def halfway(step):
        return pltpu.make_async_remote_copy(
            src_ref=held.at[step], dst_ref=caught.at[step],
            send_sem=sum_send.at[step], recv_sem=sum_recv.at[step],
            device_id=(partner, *devices)[step], device_id_type=MESH,
        )

    held[0] = jnp.zeros(held.shape[1:], f32)
    held[0, 0:8, :] = sums_ref[...]
    held[0, 8:16, :] = late_ref[...]
    for i, t in enumerate(range(0, ff, width)):
        held[0, 16 + i : 17 + i, :] = bsum_ref[:, t : t + width]
    held[0, 24:40, : 2 * PAIR] = taps_ref[...]
    step_of = [0]
    halfway(0).start()

    def sums_on():
        step = step_of[0]
        if step < 5:
            step_of[0] += 1
            halfway(step).wait()
            added = held[step] + caught[step]
            if step < 4:
                held[step + 1] = added
                halfway(step + 1).start()
            else:
                total_ref[...] = added

    def turn(view, hi_ref, lo_ref):
        for c in range(0, view.shape[0], 2 * PAIR):
            rows = slice(c, c + 2 * PAIR)
            hi, lo = split(jnp.transpose(view[rows, :]))
            hi_ref[:, rows] = hi
            lo_ref[:, rows] = lo

    def core_copy(k, src, dst):
        return pltpu.make_async_remote_copy(
            src_ref=src, dst_ref=dst, send_sem=core_send.at[k], recv_sem=core_recv.at[k],
            device_id=partner, device_id_type=MESH,
        )

    apart = [core, 1 - core]
    sa = (sa_h, sa_l)
    sb = (sb_h, sb_l)

    def times(s, t):
        return dots((s[0][...], s[1][...]), split(t), 1, 0)

    def pair_job(first, second, t_first, t_second):
        half = width // 2
        for c in range(2):
            lanes = slice(c * half, (c + 1) * half)
            a = times(first, t_first[:, lanes])
            b = times(second, t_second[:, lanes])
            for i in range(2):
                block = slice(i * 192, (i + 1) * 192)
                both = jnp.concatenate([a[:, block], b[:, block]], axis=1)
                for j in range(8):
                    for color in range(3):
                        p_pair[apart[j % 2], color, j // 4, j // 2 % 2, c, i] = both[
                            j * 96 : (j + 1) * 96, color * PAIR : (color + 1) * PAIR
                        ]

    def down_job(slot, t):
        for color in range(3):
            g = times(sa, t[:, color * 256 : (color + 1) * 256])
            for j in range(8):
                for side in range(2):
                    p_big[slot, apart[j % 2], color, j // 4, j // 2 % 2, side * 96 : side * 96 + 96] = g[
                        j * 96 : (j + 1) * 96, side * PAIR : (side + 1) * PAIR
                    ]

    def up_job(slot, t):
        half = width // 2
        for parity in range(2):
            g = times(sa, t[:, parity * half : (parity + 1) * half])
            for i in range(4):
                for color in range(3):
                    p_big[slot, apart[parity], color, i // 2, i % 2] = g[
                        i * 192 : (i + 1) * 192, color * PAIR : (color + 1) * PAIR
                    ]

    groups = [
        Scatter(g, buffer, lands[g], send, recv, mine, devices)
        for g, buffer in enumerate((r_vo, r_down, r_up, r_qk))
    ]
    vo, down, up, qk = groups

    turn(loads.get(0), sa_h, sa_l)
    loads.release(0)
    turn(loads.get(2), sb_h, sb_l)
    loads.release(2)
    pair_job(sa, sb, loads.get(1), loads.get(3))
    loads.release(1)
    loads.release(3)
    vo_copy = core_copy(0, p_pair.at[1], r_vo)
    vo_copy.start()
    turn(loads.get(4), sa_h, sa_l)
    loads.release(4)

    big = []
    for i in range(4):
        big.append((r_down.at[:, :, :, i // 2, i % 2], i % 2))
    for i in range(4):
        big.append((r_up.at[:, i // 2, i % 2], i % 2))
    copies = [
        core_copy(1 + i, p_big.at[slot, 1], place) for i, (place, slot) in enumerate(big)
    ]

    def absorb(i):
        place, slot = big[i]
        copies[i].wait()
        place[...] = place[...] + p_big[slot, 0]

    for i in range(8):
        if i == 4:
            turn(loads.get(9), sa_h, sa_l)
            loads.release(9)
        at = 5 + i + (i >= 4)
        (down_job if i < 4 else up_job)(i % 2, loads.get(at))
        loads.release(at)
        copies[i].start()
        sums_on()
        if i == 0:
            vo_copy.wait()
            r_vo[...] = r_vo[...] + p_pair[0]
            vo.start()
        else:
            absorb(i - 1)
        if i == 4:
            down.start()
        if i in (3, 4, 5, 6):
            vo.advance()
    vo.store(vo_ref)
    turn(loads.get(14), sa_h, sa_l)
    loads.release(14)
    turn(loads.get(15), sb_h, sb_l)
    loads.release(15)
    absorb(7)
    up.start()
    tokens = loads.get(16)
    pair_job(sa, sb, tokens, tokens)
    loads.release(16)
    qk_copy = core_copy(9, p_pair.at[1], r_qk)
    qk_copy.start()
    down.advance()

    def token_job(x, w):
        for c in range(0, width, 2 * PAIR):
            rows = slice(c, c + 2 * PAIR)
            hi, lo = split(w[rows, :])
            sa_h[rows, :width] = hi
            sa_l[rows, :width] = lo
        for c in range(0, x.shape[0], 2 * PAIR):
            rows = slice(c, c + 2 * PAIR)
            y = dots(split(x[rows, :]), (sa_h[:, :width], sa_l[:, :width]), 1, 1)
            gt_ref[rows, :] += y

    residual.wait()
    for i in range(3):
        token_job(loads.get(17 + 2 * i), loads.get(18 + 2 * i))
        loads.release(17 + 2 * i)
        loads.release(18 + 2 * i)
        if i == 0:
            qk_copy.wait()
            r_qk[...] = r_qk[...] + p_pair[0]
            qk.start()
        if i == 1:
            down.advance()
        if i == 2:
            up.advance()
            down.advance()
    for group in (qk, up, down, qk, up, qk, up, qk):
        group.advance()
    down.store(down_ref)
    up.store(up_ref)
    qk.store(qk_ref)


def grads_call(r2, act, hidden, u, r1, x, gq, gk, gv, tokens, wq, wk, wv, sums, late, bsum, taps):
    rows, width = tokens.shape
    big, small = (2 * 96, PAIR), (96, PAIR)
    any_space = pl.BlockSpec(memory_space=pl.ANY)
    vmem = pl.BlockSpec(memory_space=VM)

    def lands(block):
        return [VM((3,) + (2,) * (3 - stage) + block, f32) for stage in range(4)]

    dma = pltpu.SemaphoreType.DMA
    return pl.pallas_call(
        grads_kernel,
        out_shape=[
            jax.ShapeDtypeStruct((3,) + small, f32),
            jax.ShapeDtypeStruct((3,) + big, f32),
            jax.ShapeDtypeStruct((3,) + big, f32),
            jax.ShapeDtypeStruct((3,) + small, f32),
            jax.ShapeDtypeStruct((rows, width), f32),
            jax.ShapeDtypeStruct((40, width), f32),
        ],
        in_specs=[any_space] * 13 + [vmem] * 4,
        out_specs=[vmem] * 6,
        scratch_shapes=[
            VM((3, rows, width), f32),
            VM((width, rows), bf16),
            VM((width, rows), bf16),
            VM((width, rows), bf16),
            VM((width, rows), bf16),
            VM((2, 2, 3, 2, 2) + big, f32),
            VM((2, 3, 2, 2, 2, 2) + small, f32),
            VM((3, 2, 2, 2, 2) + big, f32),
            VM((3, 2, 2, 2, 2) + big, f32),
            VM((3, 2, 2, 2, 2) + small, f32),
            VM((3, 2, 2, 2, 2) + small, f32),
        ]
        + lands(small) + lands(big) + lands(big) + lands(small)
        + [
            VM((5, 40, width), f32),
            VM((5, 40, width), f32),
            dma((4,)),
            dma((10,)),
            dma((10,)),
            dma((48,)),
            dma((48,)),
            dma((5,)),
            dma((5,)),
        ],
        compiler_params=params(collective_id=4, has_side_effects=True),
        name="grads",
    )(r2, act, hidden, u, r1, x, gq, gk, gv, tokens, wq, wk, wv, sums, late, bsum, taps)


def swap(x, axis, offset):
    count = lax.axis_size(axis)
    return lax.ppermute(x, axis, [(i, i ^ offset) for i in range(count)])


def both_sides(x, margin):
    return jnp.stack([x[:, :margin], x[:, -margin:]])


def bit_of(axis, bit):
    return lax.axis_index(axis) // bit % 2


def halve_rows(x, bit):
    blocks, rows, columns = x.shape
    y = x.reshape(blocks // 2, 2, rows, columns)
    mine = bit_of("seq", bit)
    keep = lax.dynamic_index_in_dim(y, mine, 1, False)
    send = lax.dynamic_index_in_dim(y, 1 - mine, 1, False)
    return keep + swap(send, "seq", bit)


def halve_columns(x, bits, bit):
    mine = bit_of("dp", bit)
    columns = x.shape[2]
    groups = 2 ** bits.index(bit)
    size = columns // (2 * groups)

    def pick(which):
        parts = [
            lax.dynamic_slice_in_dim(x, 2 * g * size + which * size, size, 2)
            for g in range(groups)
        ]
        return parts[0] if groups == 1 else jnp.concatenate(parts, axis=2)

    return pick(mine) + swap(pick(1 - mine), "dp", bit)


def powers(axis):
    count = lax.axis_size(axis)
    return [2**i for i in range(count.bit_length() - 1)]


def scatter_sum(x, order):
    seq_bits, dp_bits = powers("seq"), powers("dp")[::-1]
    count = lax.axis_size("seq")
    x = x.reshape(count, x.shape[0] // count, x.shape[1])
    x = halve_rows(x, seq_bits.pop(0))
    for axis in order:
        if axis == "z" and seq_bits:
            x = halve_rows(x, seq_bits.pop(0))
        elif axis in "xy" and dp_bits:
            half = len(powers("dp")) // 2
            low = [b for b in dp_bits if b < 2**half]
            high = [b for b in dp_bits if b >= 2**half]
            chosen = (low if axis == "x" else high) or dp_bits
            x = halve_columns(x, dp_bits, chosen[0])
            dp_bits.remove(chosen[0])
    while seq_bits:
        x = halve_rows(x, seq_bits.pop(0))
    while dp_bits:
        x = halve_columns(x, dp_bits, dp_bits[0])
        dp_bits.pop(0)
    return x[0]


def sum_everywhere(x):
    for axis in ("seq", "dp"):
        for bit in powers(axis):
            x = x + swap(x, axis, bit)
    return x


def rounded_pair(w):
    hi = lax.reduce_precision(w, 8, 7)
    return hi.astype(bf16), (w - hi).astype(bf16)


def product(a, b, ca, cb):
    return lax.dot_general(a, b, (((ca,), (cb,)), ((), ())), precision=HIGH)


def on_device(
    tokens,
    lengths,
    keep,
    w_query,
    b_query,
    w_key,
    w_value,
    b_value,
    conv_weight,
    w_out,
    b_out,
    gain_one,
    shift_one,
    w_up,
    b_up,
    w_down,
    b_down,
    gain_two,
    shift_two,
    cotangent,
):
    items, span, width = tokens.shape
    heads, taps = conv_weight.shape
    head_size = width // heads
    margin = taps // 2
    factor = head_size ** (-0.25)
    pairs = heads // 2
    n = lax.axis_size("seq")
    per = -(-items * pairs // n)
    chunk_rows = per * MARKS + 8
    position = lax.axis_index("seq") * span + jnp.arange(span, dtype=jnp.int32)
    inside = position[None, :] < lengths[:, None]
    usable = (inside & (keep > 0)).astype(f32)
    use_row, use_col = usable[:, None, :], usable[:, :, None]
    segment = jnp.where(inside, position[None, :] * MARKS // lengths[:, None], MARKS)
    marks = jnp.arange(MARKS, dtype=jnp.int32)
    member_t = (segment[:, None, :] == marks[None, :, None]).astype(f32) * use_row
    rows = tokens.reshape(items * span, width)
    taps_forward = jnp.pad(conv_weight, ((0, 4), (0, 2 * PAIR - taps)))
    taps_backward = jnp.pad(conv_weight[:, ::-1], ((0, 4), (0, 2 * PAIR - taps)))

    queries, key_rows, values, land_q, land_k, inverse_divisor = project_call(
        tokens, member_t, w_query, w_key, w_value, jnp.stack([b_query, b_value]), n, factor
    )
    k1, w3, top, chunks = scores_call(
        queries, key_rows, values, land_q, land_k, use_row, n, per, pairs, chunk_rows
    )
    use_sides = both_sides(use_col, margin)
    kernel_two, z, owned_q, owned_k, context, mixed, vhalos = exchange_call(
        chunks, land_q, land_k, both_sides(values, margin) * use_sides, n, per, pairs
    )
    attn_input = mix_call(mixed, k1, values, use_col, vhalos, taps_forward, per, pairs, margin)

    vectors = jnp.stack(
        [b_out, gain_one, shift_one, b_down, gain_two, shift_two, b_out, b_out]
    )
    x = attn_input.reshape(items * span, width)
    output, act, u, r2, hidden, r1, og, row_sums, up_sums = rows_call(
        x,
        rows,
        cotangent.reshape(items * span, width),
        rounded_pair(w_out),
        rounded_pair(w_up),
        rounded_pair(w_down),
        vectors,
        b_up[None, :],
    )
    og = og.reshape(items, span, width)
    grad_queries, chunks = one_back_call(mixed, k1, og, queries, land_k, per, pairs)
    grad_context, own_q, own_k, ghalos = exchange_back_call(
        chunks, both_sides(og, margin), context, kernel_two, z, owned_q, owned_k, n, chunk_rows
    )
    gv_conv, grad_taps = conv_back_call(
        og, ghalos, values, vhalos, use_col, taps_backward, pairs, margin
    )
    grad_values, grad_keys, chunks = three_back_call(
        grad_context, mixed, w3, top, values, key_rows, gv_conv, land_q, per, pairs
    )
    land_grads = land_exchange_call(chunks, own_q, own_k, n)
    grad_queries, grad_keys, late_sums = land_back_call(
        land_grads, grad_queries, grad_keys, grad_values, member_t, inverse_divisor,
        per, pairs, factor,
    )
    grad_queries = grad_queries.reshape(items * span, width)
    grad_keys = grad_keys.reshape(items * span, width)
    grad_values = grad_values.reshape(items * span, width)
    ff = w_up.shape[1]
    if (n, lax.axis_size("dp"), width, ff) == (8, 4, 768, 3072):
        vo, down, up, qk, grad_tokens, totals = grads_call(
            r2, act, hidden, u, r1, x, grad_queries, grad_keys, grad_values, rows,
            w_query, w_key, w_value, row_sums, late_sums, up_sums, grad_taps,
        )
        vo, qk = (jnp.transpose(both, (0, 2, 1)).reshape(2, -1, both.shape[1]) for both in (vo, qk))
        grad_w_value, grad_w_out = vo[0], vo[1]
        grad_w_query, grad_w_key = qk[0], qk[1]
        down = down.reshape(3, 2, -1, PAIR)
        grad_w_down = jnp.transpose(down, (0, 1, 3, 2)).reshape(-1, down.shape[2])
        grad_w_up = jnp.transpose(up, (1, 0, 2)).reshape(up.shape[1], -1)
    else:
        grad_w_down = scatter_sum(product(r2, act, 0, 0), "yxzz").T
        grad_w_up = scatter_sum(product(u, hidden, 0, 0), "xzyz").T
        grad_w_out = scatter_sum(product(r1, x, 0, 0), "zyxz").T
        grad_w_value = scatter_sum(product(grad_values, rows, 0, 0), "zyxz").T
        grad_w_query = scatter_sum(product(grad_queries, rows, 0, 0), "yxzz").T
        grad_w_key = scatter_sum(product(grad_keys, rows, 0, 0), "xzyz").T
        grad_tokens = (
            r1
            + product(grad_values, w_value, 1, 1)
            + product(grad_queries, w_query, 1, 1)
            + product(grad_keys, w_key, 1, 1)
        )
        taps_rows = jnp.pad(grad_taps, ((0, 0), (0, width - grad_taps.shape[1])))
        up_rows = jnp.pad(up_sums.reshape(-1, width), ((0, 8 - ff // width), (0, 0)))
        totals = sum_everywhere(jnp.concatenate([row_sums, late_sums, up_rows, taps_rows]))
    row_sums, late = totals[:8], totals[8:16]
    up_sums = totals[16 : 16 + ff // width].reshape(ff)
    grad_conv = totals[24 : 24 + heads, PAIR - 1 : PAIR - 1 + taps]
    return (
        output.reshape(tokens.shape),
        grad_tokens.reshape(tokens.shape),
        grad_w_query,
        late[0],
        grad_w_key,
        grad_w_value,
        late[1],
        grad_conv,
        grad_w_out,
        row_sums[5],
        row_sums[3],
        row_sums[4],
        grad_w_up,
        up_sums,
        grad_w_down,
        row_sums[2],
        row_sums[0],
        row_sums[1],
    )


def solution(mesh):
    rows = P("dp", "seq", None)
    block = P("dp", "seq")
    in_specs = (rows, P("dp"), block) + (P(),) * 16 + (rows,)
    out_specs = (
        rows, rows, block, P(), block, block, P(), P(), block,
        P(), P(), P(), block, P(), block, P(), P(), P(),
    )
    return jax.shard_map(
        on_device, mesh=mesh, in_specs=in_specs, out_specs=out_specs, check_vma=False
    )
```

```python
import functools

import jax
import jax.numpy as jnp
from jax import lax
from jax.experimental import pallas as pl
from jax.experimental.pallas import tpu as pltpu
from jax.sharding import PartitionSpec as P

MARKS = 64
NEWTON = 6
PAIR = 128
HIGH = lax.Precision.HIGH
epsilon = 1e-05
f32 = jnp.float32
bf16 = jnp.bfloat16
VM = pltpu.VMEM
LIMIT = 66 * 1024 * 1024


def split(x):
    hi = x.astype(bf16)
    return hi, (x - hi.astype(f32)).astype(bf16)


def dg(a, b, ca, cb):
    return lax.dot_general(a, b, (((ca,), (cb,)), ((), ())), preferred_element_type=f32)


def dots(a, b, ca, cb):
    return dg(a[0], b[0], ca, cb) + dg(a[0], b[1], ca, cb) + dg(a[1], b[0], ca, cb)


def dot3(a, b, ca=1, cb=0):
    return dots(split(a), split(b), ca, cb)


def lane_low(shape):
    return lax.broadcasted_iota(jnp.int32, shape, len(shape) - 1) < PAIR // 2


def spread(compact):
    low = lane_low(compact.shape)
    zero = jnp.zeros_like(compact)
    return jnp.concatenate([jnp.where(low, compact, zero), jnp.where(low, zero, compact)], axis=0)


def compacted(block):
    half = block.shape[0] // 2
    return jnp.where(lane_low((half, block.shape[1])), block[:half], block[half:])


def row_of(column):
    return jnp.transpose(jnp.broadcast_to(column, (PAIR, PAIR)))[0:1, :]


def column_of(row):
    return jnp.transpose(jnp.broadcast_to(row, (PAIR, PAIR)))


def diagonal_mask():
    rows = lax.broadcasted_iota(jnp.int32, (PAIR, PAIR), 0) < PAIR // 2
    return rows == lane_low((PAIR, PAIR))


def block_sum(x):
    halves = x.reshape(2, x.shape[0] // 2, x.shape[1])
    total = jnp.sum(halves, axis=1, keepdims=True)
    return jnp.broadcast_to(total, halves.shape).reshape(x.shape)


def block_max(x):
    halves = x.reshape(2, x.shape[0] // 2, x.shape[1])
    total = jnp.max(halves, axis=1, keepdims=True)
    return jnp.broadcast_to(total, halves.shape).reshape(x.shape)


def params(**more):
    return pltpu.CompilerParams(vmem_limit_bytes=LIMIT, **more)


def whole(shape):
    return pl.BlockSpec(shape, lambda *_: (0,) * len(shape))


def per_item(shape):
    return pl.BlockSpec((1,) + shape, lambda i, *_: (i,) + (0,) * len(shape))


class Seat:
    def __init__(self, n):
        self.n, self.nz = n, n // 2
        self.me = lax.axis_index("seq")
        self.core = lax.rem(self.me, 2)
        self.z = self.me // 2
        self.owner = self.core * self.nz + self.z
        self.partner = self.me + 1 - 2 * self.core
        self.extra = lax.rem(self.me + 2 * self.core - 1 + n, n)

    def ahead(self, j):
        return lax.rem(self.z + j, self.nz)

    def behind(self, j):
        return lax.rem(self.z - j + self.nz, self.nz)

    def at(self, z):
        return 2 * z + self.core

    def hello(self, edges, more=()):
        others = [self.partner] + [self.at(self.ahead(j)) for j in range(1, self.nz)]
        if edges:
            others.append(self.extra)
        others = [{"seq": other} for other in others] + list(more)
        barrier = pltpu.get_barrier_semaphore()
        for other in others:
            pl.semaphore_signal(barrier, inc=1, device_id=other, device_id_type=MESH)
        pl.semaphore_wait(barrier, len(others))


MESH = pl.DeviceIdType.MESH


def remote(src, dst, send, recv, device):
    return pltpu.make_async_remote_copy(
        src_ref=src, dst_ref=dst, send_sem=send, recv_sem=recv,
        device_id={"seq": device}, device_id_type=MESH,
    )


class Reduce:
    def __init__(self, seat, chunks, first, acc, second, send, recv):
        self.seat, self.chunks, self.first, self.acc, self.second = seat, chunks, first, acc, second
        self.send, self.recv = send, recv
        self.across = remote(chunks.at[1 - seat.core], first, send.at[0], recv.at[0], seat.partner)
        self.along = [
            remote(
                acc.at[seat.ahead(j)], second.at[j - 1], send.at[j], recv.at[j],
                seat.at(seat.ahead(j)),
            )
            for j in range(1, seat.nz)
        ]

    def start(self):
        self.across.start()

    def middle(self, merge):
        self.across.wait()
        for z in range(self.seat.nz):
            self.acc[z] = merge([self.chunks.at[self.seat.core, z], self.first.at[z]])
        for copy in self.along:
            copy.start()

    def finish(self, merge):
        for copy in self.along:
            copy.wait()
        refs = [self.acc.at[self.seat.z]] + [self.second.at[j] for j in range(self.seat.nz - 1)]
        return merge(refs)

    @staticmethod
    def scratch(n, shape):
        nz = n // 2
        return [
            VM((nz,) + shape, f32),
            VM((nz,) + shape, f32),
            VM((nz - 1,) + shape, f32),
            pltpu.SemaphoreType.DMA((nz,)),
            pltpu.SemaphoreType.DMA((nz,)),
        ]


class Gather:
    def __init__(self, seat, out, send, recv):
        own = out.at[seat.core, seat.z]
        self.along = [
            remote(own, own, send.at[j], recv.at[j], seat.at(seat.ahead(j)))
            for j in range(1, seat.nz)
        ]
        self.across = [remote(own, own, send.at[0], recv.at[0], seat.partner)]
        for j in range(1, seat.nz):
            block = out.at[seat.core, seat.behind(j)]
            k = seat.nz + j
            self.across.append(remote(block, block, send.at[k], recv.at[k], seat.partner))

    def start(self):
        for copy in self.along:
            copy.start()
        self.across[0].start()

    def forward(self):
        for copy, onward in zip(self.along, self.across[1:]):
            copy.wait_recv()
            onward.start()

    def finish(self):
        for copy in self.along:
            copy.wait_send()
        for copy in self.across:
            copy.wait()

    @staticmethod
    def scratch(n):
        return [pltpu.SemaphoreType.DMA((n,)), pltpu.SemaphoreType.DMA((n,))]


class Edges:
    def __init__(self, seat, sides, halos, send, recv):
        self.seat, self.halos = seat, halos
        core = seat.core
        self.copies = [
            remote(sides.at[1 - core], halos.at[core], send.at[0], recv.at[0], seat.partner),
            remote(sides.at[core], halos.at[1 - core], send.at[1], recv.at[1], seat.extra),
        ]

    def start(self):
        for copy in self.copies:
            copy.start()

    def finish(self, out):
        for copy in self.copies:
            copy.wait()
        seat = self.seat
        inner = (jnp.where(seat.me > 0, 1.0, 0.0), jnp.where(seat.me < seat.n - 1, 1.0, 0.0))
        for side in range(2):
            out[side] = self.halos[side] * inner[side]

    @staticmethod
    def scratch(shape):
        return [VM(shape, f32), pltpu.SemaphoreType.DMA((2,)), pltpu.SemaphoreType.DMA((2,))]


def add_all(refs):
    return functools.reduce(lambda x, y: x + y, [r[...] for r in refs])


def partner_of(index, bit):
    return index + bit - 2 * bit * lax.rem(index // bit, 2)


class Loads:
    def __init__(self, sources, slots, sems):
        self.count = slots.shape[0]
        self.views, self.copies = [], []
        for i, src in enumerate(sources):
            slot = i % self.count
            view = slots.at[slot, : src.shape[-2]]
            self.views.append(view)
            if len(src.shape) == 2:
                self.copies.append([pltpu.make_async_copy(src, view, sems.at[slot, 0])])
                continue
            size = src.shape[2]
            self.copies.append(
                [
                    pltpu.make_async_copy(
                        src.at[j], view.at[:, j * size : (j + 1) * size], sems.at[slot, j]
                    )
                    for j in range(src.shape[0])
                ]
            )
        for i in range(min(self.count, len(sources))):
            self.begin(i)

    def begin(self, i):
        for copy in self.copies[i]:
            copy.start()

    def get(self, i):
        for copy in self.copies[i]:
            copy.wait()
        return self.views[i]

    def release(self, i):
        if i + self.count < len(self.copies):
            self.begin(i + self.count)


def halved(view, into):
    rows, columns = into.shape[1:]
    for r in range(0, rows, 2 * PAIR):
        part = slice(r, r + 2 * PAIR)
        into[0, part, :], into[1, part, :] = split(view[part, :])
    return into


ALL_LINKS = ((2, 3, 1, 0), (3, 2, 1, 0), (1, 3, 2, 0))
EVEN = ((2, 1, 3, 0), (3, 2, 1, 0), (1, 3, 2, 0))


class Links:
    def __init__(self):
        me, dp = lax.axis_index("seq"), lax.axis_index("dp")
        z = me // 2
        self.core = lax.rem(me, 2)
        self.mine = (z // 2, lax.rem(z, 2), dp // 2, lax.rem(dp, 2))
        self.partner = {"seq": partner_of(me, 1)}
        self.devices = (
            {"seq": partner_of(me, 4)},
            {"seq": partner_of(me, 2)},
            {"dp": partner_of(dp, 2)},
            {"dp": partner_of(dp, 1)},
        )
        self.apart = (self.core, 1 - self.core)

    def copy(self, k, src, dst, send, recv):
        return pltpu.make_async_remote_copy(
            src_ref=src, dst_ref=dst, send_sem=send.at[k], recv_sem=recv.at[k],
            device_id=self.partner, device_id_type=MESH,
        )


class Scatter:
    def __init__(self, base, links, buffers, send, recv, first=0, orders=ALL_LINKS):
        self.orders = orders
        self.links, self.buffers, self.first, self.stage = links, buffers, first, first
        self.copies = {}
        for stage in range(first, first + len(buffers) - 1):
            for color, order in enumerate(self.orders):
                dim = order[stage]
                k = (base * 3 + color) * 4 + stage
                self.copies[stage, color] = pltpu.make_async_remote_copy(
                    src_ref=self.part(color, stage, 1 - links.mine[dim]),
                    dst_ref=buffers[stage - first + 1].at[color],
                    send_sem=send.at[k],
                    recv_sem=recv.at[k],
                    device_id=links.devices[dim],
                    device_id_type=MESH,
                )

    def part(self, color, stage, index):
        order = self.orders[color]
        left = [dim for dim in range(4) if dim not in order[:stage]]
        place = [index if dim == order[stage] else slice(None) for dim in left]
        return self.buffers[stage - self.first].at[(color, *place)]

    def start(self):
        for color in range(3):
            self.copies[self.stage, color].start()

    def advance(self):
        stage = self.stage
        self.stage += 1
        for color, order in enumerate(self.orders):
            self.copies[stage, color].wait()
            landed = self.buffers[stage - self.first + 1].at[color]
            landed[...] = landed[...] + self.part(color, stage, self.links.mine[order[stage]])[...]
            if (stage + 1, color) in self.copies:
                self.copies[stage + 1, color].start()


def times(s, t, lanes):
    return dots((s[0], s[1]), split(t[:, lanes]), 1, 0)


BIG = (192, PAIR)
SMALL = (96, PAIR)


def landing(block, stage):
    return (3,) + (2,) * (3 - stage) + block


class Tiles:
    def __init__(self, links, down, s, t, buffer, scratch):
        self.links, self.down = links, down
        s_slots, self.s, t_slots, self.p_big, s_sem, t_sem, send, recv = scratch
        self.s_loads = Loads([s], s_slots, s_sem)
        self.t_loads = Loads([t.at[i] for i in range(4)], t_slots, t_sem)
        self.places, self.copies = [], []
        for i in range(4):
            at = (slice(None),) * (3 if down else 1) + (i // 2, i % 2)
            self.places.append(buffer.at[at])
            self.copies.append(links.copy(i, self.p_big.at[i % 2, 1], self.places[i], send, recv))

    def compute(self, i):
        if i == 0:
            halved(self.s_loads.get(0), self.s)
        t, slot, apart = self.t_loads.get(i), i % 2, self.links.apart
        for third in range(3):
            g = times(self.s, t, slice(third * 256, (third + 1) * 256))
            for side in range(2):
                lanes = slice(side * PAIR, (side + 1) * PAIR)
                if self.down:
                    for j in range(8):
                        at = (slot, apart[j % 2], third, j // 4, j // 2 % 2)
                        self.p_big[(*at, slice(side * 96, side * 96 + 96))] = g[j * 96 : (j + 1) * 96, lanes]
                else:
                    parity, color = divmod(2 * third + side, 3)
                    for j in range(4):
                        at = (slot, apart[parity], color, j // 2, j % 2)
                        self.p_big[at] = g[j * 192 : (j + 1) * 192, lanes]
        self.t_loads.release(i)
        self.copies[i].start()

    def absorb(self, i):
        self.copies[i].wait()
        place = self.places[i]
        place[...] = place[...] + self.p_big[i % 2, 0]

    @staticmethod
    def scratch(rows, width):
        dma = pltpu.SemaphoreType.DMA
        return [
            VM((1, width, rows), f32),
            VM((2, width, rows), bf16),
            VM((2, rows, width), f32),
            VM((2, 2, 3, 2, 2) + BIG, f32),
            dma((1, 4)),
            dma((2, 1)),
            dma((4,)),
            dma((4,)),
        ]


def project_kernel(n, items, factor, tok_ref, mem_ref, wq_ref, wk_ref, wv_ref, vec_ref,
                   q_out, k_out, v_out, lq_ref, lk_ref, inv_ref,
                   q_ref, k_ref, v_ref, tok_h, tok_l, halves, w_s, w_sem, out_sem,
                   sums, land, *scratch):
    seat = Seat(n)
    rows = items * MARKS // n
    width = tok_ref.shape[2]
    reduce = Reduce(seat, sums, *scratch[:5])
    gather = Gather(seat, land, *scratch[5:])
    fetches = [
        pltpu.make_async_copy(ref, w_s.at[i], w_sem.at[i])
        for i, ref in enumerate((wq_ref, wk_ref, wv_ref))
    ]
    for fetch in fetches:
        fetch.start()
    stores = [
        pltpu.make_async_copy(src, dst, out_sem.at[i])
        for i, (src, dst) in enumerate(
            ((q_ref, q_out), (k_ref, k_out), (v_ref, v_out))
        )
    ]
    seat.hello(False)
    for item in range(items):
        member = mem_ref[item].astype(bf16)
        hi, lo = split(tok_ref[item])
        tok_h[item], tok_l[item] = hi, lo
        total = dg(member, hi, 1, 0) + dg(member, lo, 1, 0)
        count = jnp.sum(mem_ref[item], axis=1, keepdims=True)
        for part in range(MARKS // rows):
            c = item * (MARKS // rows) + part
            piece = slice(part * rows, (part + 1) * rows)
            sums[c // seat.nz, c % seat.nz, :, :width] = total[piece]
            sums[c // seat.nz, c % seat.nz, :, width:] = jnp.broadcast_to(
                count[piece], (rows, PAIR)
            )
    reduce.start()
    b_query, b_value = vec_ref[0:1, :], vec_ref[1:2, :]
    for place in range(3):
        fetches[place].wait()
        hi, lo = split(w_s[place])
        halves[2 * place], halves[2 * place + 1] = hi, lo

    def project(place, out_ref, bias, scale):
        def lap(item, _):
            x = (tok_h[item], tok_l[item])
            y = dots(x, (halves[2 * place], halves[2 * place + 1]), 1, 0)
            y = y if bias is None else y + bias
            out_ref[item] = y if scale is None else y * scale
            return 0

        lax.fori_loop(0, items, lap, 0)

    project(0, q_ref, b_query, factor)
    stores[0].start()
    reduce.middle(add_all)
    project(1, k_ref, None, factor)
    stores[1].start()
    land[seat.core, seat.z] = reduce.finish(add_all)
    gather.start()
    project(2, v_ref, b_value, None)
    stores[2].start()
    gather.forward()
    gather.finish()
    whole_land = land[...].reshape(items * MARKS, width + PAIR)
    divisor = jnp.maximum(whole_land[:, width:], 1.0)
    inv_ref[...] = (1.0 / divisor).reshape(items, MARKS, PAIR)
    filled = whole_land[:, width : width + 1] / divisor[:, 0:1]
    x = split(whole_land[:, :width] / divisor[:, 0:1])
    lq = (dots(x, (halves[0], halves[1]), 1, 0) + filled * b_query) * factor
    lk = dots(x, (halves[2], halves[3]), 1, 0) * factor
    lq_ref[...] = lq.reshape(items, MARKS, width)
    lk_ref[...] = lk.reshape(items, MARKS, width)
    for store in stores:
        store.wait()


def project_call(tokens, member_t, w_query, w_key, w_value, vectors, n, factor):
    items, span, width = tokens.shape
    rows = items * MARKS // n
    big = jax.ShapeDtypeStruct((items, span, width), f32)
    small = jax.ShapeDtypeStruct((items, MARKS, width), f32)
    vmem, any_space = pl.BlockSpec(memory_space=VM), pl.BlockSpec(memory_space=pl.ANY)
    return pl.pallas_call(
        functools.partial(project_kernel, n, items, factor),
        out_shape=[big, big, big, small, small, jax.ShapeDtypeStruct((items, MARKS, PAIR), f32)],
        in_specs=[vmem] * 2 + [any_space] * 3 + [vmem],
        out_specs=[any_space] * 3 + [vmem] * 3,
        scratch_shapes=[VM((items, span, width), f32)] * 3
        + [VM((items, span, width), bf16)] * 2
        + [
            VM((6, width, width), bf16),
            VM((3, width, width), f32),
            pltpu.SemaphoreType.DMA((3,)),
            pltpu.SemaphoreType.DMA((3,)),
            VM((2, n // 2, rows, width + PAIR), f32),
            VM((2, n // 2, rows, width + PAIR), f32),
        ]
        + Reduce.scratch(n, (rows, width + PAIR))
        + Gather.scratch(n),
        compiler_params=params(collective_id=0, has_side_effects=True),
        name="project",
    )(tokens, member_t, w_query, w_key, w_value, vectors)


def scores_kernel(per, pairs, q_ref, k_ref, v_ref, lq_ref, lk_ref, use_ref, k1_ref, w3_ref, top_ref, chunk):
    item = pl.program_id(0)
    stats = per * MARKS

    @pl.when(item == 0)
    def _():
        chunk[...] = jnp.zeros_like(chunk)

    use = use_ref[0]
    for p in range(pairs):
        lanes = slice(p * PAIR, (p + 1) * PAIR)
        q = q_ref[0, :, lanes]
        s1 = dot3(spread(lk_ref[0, :, lanes]), q, 1, 1)
        e1 = jnp.exp(s1 - block_max(s1))
        k1_ref[0, lanes, :] = e1 / block_sum(e1)
        s3 = dot3(spread(lq_ref[0, :, lanes]), k_ref[0, :, lanes], 1, 1)
        masked = jnp.where(use > 0, s3, -1e30)
        top = jnp.max(masked, axis=1, keepdims=True)
        w3 = jnp.exp(masked - top) * use
        w3_ref[0, lanes, :] = w3
        total = jnp.sum(w3, axis=1, keepdims=True)
        weighted = compacted(dot3(w3, v_ref[0, :, lanes]))
        top_row = row_of(top)
        top_ref[0, p : p + 1, :] = top_row
        g = item * pairs + p
        owner, place = g // per, g % per
        chunk[owner, pl.ds(pl.multiple_of(place * MARKS, MARKS), MARKS), :] = weighted
        chunk[owner, pl.ds(stats + 2 * place, 1), :] = top_row
        chunk[owner, pl.ds(stats + 2 * place + 1, 1), :] = row_of(total)


def scores_call(q, k, v, lq, lk, use_row, n, per, pairs, chunk_rows):
    items, span, width = q.shape
    return pl.pallas_call(
        functools.partial(scores_kernel, per, pairs),
        out_shape=[
            jax.ShapeDtypeStruct((items, width, span), f32),
            jax.ShapeDtypeStruct((items, width, span), f32),
            jax.ShapeDtypeStruct((items, 8, PAIR), f32),
            jax.ShapeDtypeStruct((n, chunk_rows, PAIR), f32),
        ],
        grid=(items,),
        in_specs=[per_item((span, width))] * 3
        + [per_item((MARKS, width))] * 2
        + [per_item((1, span))],
        out_specs=[per_item((width, span))] * 2
        + [per_item((8, PAIR)), whole((n, chunk_rows, PAIR))],
        compiler_params=params(),
        name="scores",
    )(q, k, v, lq, lk, use_row)


def owned_land(seat, per, pairs, ref, into):
    for place in range(per):
        g = lax.rem(seat.owner * per + place, ref.shape[0] * pairs)
        item, p = g // pairs, lax.rem(g, pairs)
        into[place] = ref[item, :, pl.ds(pl.multiple_of(p * PAIR, PAIR), PAIR)]


def newton_step(a, z, eye):
    pr = dot3(a, z)
    n1 = 7.0 * eye - pr
    n2 = 15.0 * eye - dot3(pr, n1)
    n3 = 13.0 * eye - dot3(pr, n2)
    return pr, n1, n2, n3


def unit():
    rows = lax.broadcasted_iota(jnp.int32, (PAIR, PAIR), 0)
    return (rows == lax.broadcasted_iota(jnp.int32, (PAIR, PAIR), 1)).astype(f32)


def head_total(x):
    return block_sum(jnp.sum(x, axis=1, keepdims=True))


def merged(per, refs):
    stats = per * MARKS
    weights, rest = [], []
    for place in range(per):
        tops = [r[stats + 2 * place : stats + 2 * place + 1, :] for r in refs]
        largest = functools.reduce(jnp.maximum, tops)
        total = jnp.zeros_like(largest)
        weighted = jnp.zeros((MARKS, PAIR), f32)
        for r, top in zip(refs, tops):
            scale = jnp.exp(top - largest)
            total = total + scale * r[stats + 2 * place + 1 : stats + 2 * place + 2, :]
            scales = compacted(column_of(scale))
            weighted = weighted + scales * r[place * MARKS : (place + 1) * MARKS, :]
        weights.append(weighted)
        rest += [largest, total]
    filler = jnp.zeros((refs[0].shape[0] - stats - 2 * per, PAIR), f32)
    return jnp.concatenate(weights + rest + [filler], axis=0)


def exchange_kernel(n, per, pairs, chunk_ref, lq_ref, lk_ref, side_ref,
                    a_ref, z_ref, lqo_ref, lko_ref, ctx_ref, out_ref, halo_ref, mine, *scratch):
    seat = Seat(n)
    merge = functools.partial(merged, per)
    reduce = Reduce(seat, chunk_ref, *scratch[:5])
    gather = Gather(seat, out_ref, *scratch[5:7])
    edges = Edges(seat, side_ref, *scratch[7:])
    seat.hello(True)
    reduce.start()
    edges.start()
    owned_land(seat, per, pairs, lq_ref, lqo_ref)
    owned_land(seat, per, pairs, lk_ref, lko_ref)
    diagonal = diagonal_mask()
    eye = unit()
    for place in range(per):
        s2 = dot3(spread(lqo_ref[place]), spread(lko_ref[place]), 1, 1)
        s2 = jnp.where(diagonal, s2, -1e30)
        e2 = jnp.exp(s2 - jnp.max(s2, axis=1, keepdims=True))
        e2 = jnp.where(diagonal, e2, 0.0)
        a = e2 / jnp.sum(e2, axis=1, keepdims=True)
        a_ref[place] = a
        z_ref[0, place] = jnp.transpose(a) / head_total(a * a)
    reduce.middle(merge)

    def lap(step, _):
        for place in range(per):
            z = z_ref[step, place]
            _, _, _, n3 = newton_step(a_ref[place], z, eye)
            z_ref[step + 1, place] = 0.25 * dot3(z, n3)
        return 0

    lax.fori_loop(0, NEWTON, lap, 0)
    mine[...] = reduce.finish(merge)
    stats = per * MARKS
    block = out_ref.at[seat.core, seat.z]
    block[stats:, :] = mine[stats:, :]
    for place in range(per):
        rows = slice(place * MARKS, (place + 1) * MARKS)
        total = mine[stats + 2 * place + 1 : stats + 2 * place + 2, :]
        context = mine[rows, :] / compacted(column_of(total))
        ctx_ref[place] = context
        block[rows, :] = compacted(dot3(z_ref[NEWTON, place], spread(context)))
    gather.start()
    edges.finish(halo_ref)
    gather.forward()
    gather.finish()


def exchange_call(chunks, lq, lk, sides, n, per, pairs):
    rows = chunks.shape[1]
    small = jax.ShapeDtypeStruct((per, MARKS, PAIR), f32)
    blocks = (2, n // 2, rows, PAIR)
    out = pl.pallas_call(
        functools.partial(exchange_kernel, n, per, pairs),
        out_shape=[
            jax.ShapeDtypeStruct((per, PAIR, PAIR), f32),
            jax.ShapeDtypeStruct((NEWTON + 1, per, PAIR, PAIR), f32),
            small,
            small,
            small,
            jax.ShapeDtypeStruct(blocks, f32),
            jax.ShapeDtypeStruct(sides.shape, f32),
        ],
        in_specs=[pl.BlockSpec(memory_space=VM)] * 4,
        out_specs=[pl.BlockSpec(memory_space=VM)] * 7,
        scratch_shapes=[VM((rows, PAIR), f32)]
        + Reduce.scratch(n, (rows, PAIR))
        + Gather.scratch(n)
        + Edges.scratch(sides.shape),
        compiler_params=params(collective_id=1, has_side_effects=True),
        name="exchange",
    )(chunks.reshape(blocks), lq, lk, sides)
    return list(out[:5]) + [out[5].reshape(n, rows, PAIR), out[6]]


def toeplitz(taps_row, rows):
    wide = jnp.broadcast_to(taps_row, (rows, 2 * PAIR))
    return pltpu.roll(wide, 0, 1, stride=1, stride_axis=0)


def keep_taps(taps_ref, into, heads):
    for h in range(heads):
        hi, lo = split(toeplitz(taps_ref[h : h + 1, :], PAIR))
        into[0, h] = hi
        into[1, h] = lo


def keep_window(win, left, middle, right, margin, span):
    for rows, part in (
        (slice(0, margin), left),
        (slice(margin, margin + span), middle),
        (slice(margin + span, 2 * margin + span), right),
    ):
        hi, lo = split(part)
        win[0, rows, :] = hi
        win[1, rows, :] = lo


def convolve(taps, win, p, block, window):
    lanes = slice(p * PAIR, (p + 1) * PAIR)
    rows = slice(block * PAIR, block * PAIR + window)
    v = (win[0, rows, lanes], win[1, rows, lanes])
    halves = []
    for h in (2 * p, 2 * p + 1):
        t = (taps[0, h, :, :window], taps[1, h, :, :window])
        halves.append(dots(t, v, 1, 0))
    return jnp.where(lane_low((PAIR, PAIR)), halves[0], halves[1])


def owned_by(g, per):
    return g // per, g % per


def mix_kernel(per, pairs, margin, held, k1_ref, v_ref, use_ref, left_ref, right_ref, taps_ref, out_ref, taps, win):
    item = pl.program_id(0)
    span = v_ref.shape[1]
    window = PAIR + 2 * margin

    @pl.when(item == 0)
    def _():
        keep_taps(taps_ref, taps, 2 * pairs)

    keep_window(win, left_ref[0, 0], v_ref[0] * use_ref[0], right_ref[0, 0], margin, span)
    for p in range(pairs):
        lanes = slice(p * PAIR, (p + 1) * PAIR)
        slot, place = owned_by(item * pairs + p, per)
        mixed = held[slot, pl.ds(pl.multiple_of(place * MARKS, MARKS), MARKS), :]
        nystrom = dot3(k1_ref[0, lanes, :], spread(mixed), 0, 0)
        for block in range(span // PAIR):
            rows = slice(block * PAIR, (block + 1) * PAIR)
            out_ref[0, rows, lanes] = nystrom[rows] + convolve(taps, win, p, block, window)


def halo_specs(margin, width):
    return [
        pl.BlockSpec((1, 1, margin, width), lambda i, side=side: (side, i, 0, 0))
        for side in range(2)
    ]


def mix_call(blocks, k1, v, use_col, halos, taps, per, pairs, margin):
    items, span, width = v.shape
    return pl.pallas_call(
        functools.partial(mix_kernel, per, pairs, margin),
        out_shape=jax.ShapeDtypeStruct((items, span, width), f32),
        grid=(items,),
        in_specs=[whole(blocks.shape)]
        + [per_item((width, span)), per_item((span, width)), per_item((span, 1))]
        + halo_specs(margin, width)
        + [whole(taps.shape)],
        out_specs=per_item((span, width)),
        scratch_shapes=[
            VM((2, 2 * pairs, PAIR, 2 * PAIR), bf16),
            VM((2, span + 2 * margin, width), bf16),
        ],
        compiler_params=params(),
        name="mix",
    )(blocks, k1, v, use_col, halos, halos, taps)


def erf(x):
    x = jnp.clip(x, -3.832506856900711, 3.832506856900711)
    s = x * x
    a = 0.00022905065861350646
    for c in (0.0034082910107109506, 0.050955695062380861, 0.18520832239976145, 1.128379143519084):
        a = a * s + c
    b = -1.1791602954361697e-7
    for c in (
        0.000023547966471313185,
        0.0010179625278914885,
        0.014070470171167667,
        0.11098505178285362,
        0.49746925110067538,
        1.0,
    ):
        b = b * s + c
    return x * a / b


def normalize(x):
    center = x - jnp.mean(x, axis=-1, keepdims=True)
    inv_root = lax.rsqrt(jnp.mean(center * center, axis=-1, keepdims=True) + epsilon)
    return center * inv_root, inv_root


def norm_back(grad, scaled, inv_root):
    first = jnp.mean(grad, axis=-1, keepdims=True)
    second = jnp.mean(grad * scaled, axis=-1, keepdims=True)
    return inv_root * (grad - first - scaled * second)


def rows_kernel(
    x_ref, tok_ref, cot_ref, vec_ref, bup_ref, wo_ref, wu_ref, wd_ref,
    out_ref, act_ref, u_ref, r2t_ref, h1t_ref, r1t_ref, r1_ref, og_ref, sums_ref, bsum_ref,
    slope, wo_h, wo_l, wu_h, wu_l, wd_h, wd_l, staged, sems,
):
    step = pl.program_id(0)
    width = tok_ref.shape[1]
    ff = wu_ref.shape[1]
    tiles = [slice(c, c + width) for c in range(0, ff, width)]

    @pl.when(step == 0)
    def _():
        sums_ref[...] = jnp.zeros_like(sums_ref)
        bsum_ref[...] = jnp.zeros_like(bsum_ref)
        jobs = [(wo_ref, slice(None), slice(None), wo_h, wo_l)]
        jobs += [(wu_ref, slice(None), c, wu_h, wu_l) for c in tiles]
        jobs += [(wd_ref, c, slice(None), wd_h, wd_l) for c in tiles]
        depth, pieces = sems.shape
        size = width // pieces

        def load(i):
            w, r, c, _, _ = jobs[i]
            start = r.start or 0
            return [
                pltpu.make_async_copy(
                    w.at[pl.ds(start + k * size, size), c],
                    staged.at[i % depth, pl.ds(k * size, size)],
                    sems.at[i % depth, k],
                )
                for k in range(pieces)
            ]

        loads = [load(i) for i in range(len(jobs))]
        for copies in loads[:depth]:
            for copy in copies:
                copy.start()
        for i, (_, r, c, hi_ref, lo_ref) in enumerate(jobs):
            for copy in loads[i]:
                copy.wait()
            hi, lo = split(staged[i % depth])
            hi_ref[r, c] = hi
            lo_ref[r, c] = lo
            if i + depth < len(jobs):
                for copy in loads[i + depth]:
                    copy.start()

    b_out, gain_one, shift_one = vec_ref[0:1, :], vec_ref[1:2, :], vec_ref[2:3, :]
    b_down, gain_two, shift_two = vec_ref[3:4, :], vec_ref[4:5, :], vec_ref[5:6, :]
    wo = (wo_h[...], wo_l[...])
    attention = dots(split(x_ref[...]), wo, 1, 0) + b_out
    scaled_one, root_one = normalize(tok_ref[...] + attention)
    hidden = scaled_one * gain_one + shift_one
    h1t_ref[0] = jnp.transpose(hidden)
    hs = split(hidden)
    down = b_down
    for i, c in enumerate(tiles):
        pre = dots(hs, (wu_h[:, c], wu_l[:, c]), 1, 0) + bup_ref[:, c]
        phi = 0.5 + 0.5 * erf(pre * 0.7071067811865476)
        slope[:, c] = phi + pre * (0.3989422804014327 * jnp.exp(-0.5 * pre * pre))
        act = pre * phi
        act_ref[i] = act
        act = split(act)
        down = down + dots(act, (wd_h[c, :], wd_l[c, :]), 1, 0)
    scaled_two, root_two = normalize(hidden + down)
    out_ref[...] = scaled_two * gain_two + shift_two
    cot = cot_ref[...]
    r2 = norm_back(cot * gain_two, scaled_two, root_two)
    r2t_ref[0] = jnp.transpose(r2)
    rs = split(r2)
    grad_hidden = r2
    for i, c in enumerate(tiles):
        u = dots(rs, (wd_h[c, :], wd_l[c, :]), 1, 1) * slope[:, c]
        halves = split(u)
        u_ref[i] = u
        bsum_ref[:, c] += jnp.sum(u, axis=0, keepdims=True)
        grad_hidden = grad_hidden + dots(halves, (wu_h[:, c], wu_l[:, c]), 1, 1)
    r1 = norm_back(grad_hidden * gain_one, scaled_one, root_one)
    r1_ref[...] = r1
    r1t_ref[0] = jnp.transpose(r1)
    og_ref[...] = dots(split(r1), wo, 1, 1)
    for row, value in enumerate(
        (cot * scaled_two, cot, r2, grad_hidden * scaled_one, grad_hidden, r1)
    ):
        sums_ref[row : row + 1, :] += jnp.sum(value, axis=0, keepdims=True)


def rows_call(x, tokens, cotangent, w_out, w_up, w_down, vectors, b_up):
    rows, width = tokens.shape
    ff = w_up.shape[1]
    tile = 256
    count = ff // width
    wide = pl.BlockSpec((tile, width), lambda i: (i, 0))
    any_space = pl.BlockSpec(memory_space=pl.ANY)

    def fixed(shape):
        return pl.BlockSpec(shape, lambda i: (0, 0))

    narrow = jax.ShapeDtypeStruct((rows, width), f32)
    broad = jax.ShapeDtypeStruct((count, rows, width), f32)
    tall = jax.ShapeDtypeStruct((rows // tile, width, tile), f32)
    return pl.pallas_call(
        rows_kernel,
        out_shape=[narrow]
        + [broad] * 2
        + [tall] * 3
        + [narrow, narrow, jax.ShapeDtypeStruct((8, width), f32), jax.ShapeDtypeStruct((1, ff), f32)],
        grid=(rows // tile,),
        in_specs=[wide] * 3 + [fixed(vectors.shape), fixed(b_up.shape)] + [any_space] * 3,
        out_specs=[wide]
        + [pl.BlockSpec((count, tile, width), lambda i: (0, i, 0))] * 2
        + [pl.BlockSpec((1, width, tile), lambda i: (i, 0, 0))] * 3
        + [wide, wide, fixed((8, width)), fixed((1, ff))],
        scratch_shapes=[VM((tile, ff), f32)]
        + [VM((width, width), bf16)] * 2
        + [VM((width, ff), bf16)] * 2
        + [VM((ff, width), bf16)] * 2
        + [VM((2, width, width), f32), pltpu.SemaphoreType.DMA((2, 6))],
        compiler_params=params(),
        name="rows",
    )(x, tokens, cotangent, vectors, b_up, w_out, w_up, w_down)


def one_back_kernel(per, pairs, held, k1_ref, og_ref, q_ref, lk_ref, gq_ref, chunk):
    item = pl.program_id(0)

    @pl.when(item == 0)
    def _():
        chunk[...] = jnp.zeros_like(chunk)

    for p in range(pairs):
        lanes = slice(p * PAIR, (p + 1) * PAIR)
        owner, place = owned_by(item * pairs + p, per)
        mixed = spread(held[owner, pl.ds(pl.multiple_of(place * MARKS, MARKS), MARKS), :])
        k1 = k1_ref[0, lanes, :]
        og = split(og_ref[0, :, lanes])
        part_mixed = compacted(dots(split(k1), og, 1, 0))
        grad = dots(split(mixed), og, 1, 1)
        scores = k1 * (grad - block_sum(k1 * grad))
        ss = split(scores)
        gq_ref[0, :, lanes] = dots(ss, split(spread(lk_ref[0, :, lanes])), 0, 0)
        part_key = compacted(dots(ss, split(q_ref[0, :, lanes]), 1, 0))
        chunk[owner, pl.ds(pl.multiple_of(place * 2 * MARKS, 2 * MARKS), MARKS), :] = part_mixed
        chunk[owner, pl.ds(pl.multiple_of(place * 2 * MARKS + MARKS, MARKS), MARKS), :] = part_key


def one_back_call(blocks, k1, og, q, lk, per, pairs):
    items, span, width = q.shape
    out = (blocks.shape[0], 2 * per * MARKS, PAIR)
    wide = per_item((span, width))
    return pl.pallas_call(
        functools.partial(one_back_kernel, per, pairs),
        out_shape=[
            jax.ShapeDtypeStruct((items, span, width), f32),
            jax.ShapeDtypeStruct(out, f32),
        ],
        grid=(items,),
        in_specs=[whole(blocks.shape), per_item((width, span)), wide, wide]
        + [per_item((MARKS, width))],
        out_specs=[wide, whole(out)],
        compiler_params=params(),
        name="one_back",
    )(blocks, k1, og, q, lk)


class ConvBack:
    def __init__(self, pairs, margin, og, ghalo, v, vhalo, use, taps_ref, gv, gtaps, scratch):
        self.pairs, self.margin, self.ghalo, self.vhalo = pairs, margin, ghalo, vhalo
        self.og, self.v, self.use, self.gv, self.gtaps = og, v, use, gv, gtaps
        self.taps_ref = taps_ref
        self.taps, self.gwin, self.vwin, self.acc = scratch
        self.span = v.shape[1]
        self.window = PAIR + 2 * margin

    def begin(self):
        keep_taps(self.taps_ref, self.taps, 2 * self.pairs)
        self.acc[...] = jnp.zeros_like(self.acc)

    def item(self, item):
        margin, window, gwin, vwin = self.margin, self.window, self.gwin, self.vwin
        use = self.use[item]
        keep_window(gwin, self.ghalo[0, item], self.og[item], self.ghalo[1, item], margin, self.span)
        values = self.v[item] * use
        keep_window(vwin, self.vhalo[0, item], values, self.vhalo[1, item], margin, self.span)
        for p in range(self.pairs):
            lanes = slice(p * PAIR, (p + 1) * PAIR)
            for block in range(self.span // PAIR):
                rows = slice(block * PAIR, (block + 1) * PAIR)
                self.gv[item, rows, lanes] = convolve(self.taps, gwin, p, block, window) * use[rows]
                inner = slice(margin + block * PAIR, margin + (block + 1) * PAIR)
                outer = slice(block * PAIR, block * PAIR + window)
                v = (vwin[0, outer, lanes], vwin[1, outer, lanes])
                low = lane_low((PAIR, PAIR))
                hi, lo = gwin[0, inner, lanes], gwin[1, inner, lanes]
                zero = jnp.zeros_like(hi)
                first = (jnp.where(low, hi, zero), jnp.where(low, lo, zero))
                second = (jnp.where(low, zero, hi), jnp.where(low, zero, lo))
                self.acc[2 * p] += dots(first, v, 1, 1)
                self.acc[2 * p + 1] += dots(second, v, 1, 1)

    def end(self):
        rows = lax.broadcasted_iota(jnp.int32, (PAIR, PAIR), 0)
        flip = (rows + lax.broadcasted_iota(jnp.int32, (PAIR, PAIR), 1) == PAIR - 1).astype(bf16)
        for h in range(2 * self.pairs):
            c = self.acc[h]
            c = jnp.concatenate([c, jnp.zeros((PAIR, 2 * PAIR - self.window), f32)], axis=1)
            hi = c.astype(bf16)
            rest = c - hi.astype(f32)
            mid = rest.astype(bf16)
            low = (rest - mid.astype(f32)).astype(bf16)
            c = dg(flip, hi, 1, 0) + dg(flip, mid, 1, 0) + dg(flip, low, 1, 0)
            c = pltpu.roll(c, 0, 1, stride=1, stride_axis=0)
            self.gtaps[h : h + 1, :] = jnp.sum(c, axis=0, keepdims=True)

    @staticmethod
    def scratch(pairs, margin, span, width):
        return [
            VM((2, 2 * pairs, PAIR, 2 * PAIR), bf16),
            VM((2, span + 2 * margin, width), bf16),
            VM((2, span + 2 * margin, width), bf16),
            VM((2 * pairs, PAIR, PAIR + 2 * margin), f32),
        ]


def exchange_back_kernel(n, per, fused, *refs):
    refs = list(refs)
    chunk_ref, side_ref, ctx_ref, a_ref, z_ref, lq_ref, lk_ref = refs[:7]
    r2_ref, act_ref = refs[7:9] if fused else [None] * 2
    refs = refs[9:] if fused else refs[7:]
    out_ref, gq_ref, gk_ref, halo_ref = refs[:4]
    part_ref = refs[4] if fused else None
    gm, gz, ga, *scratch = refs[5:] if fused else refs[4:]
    seat = Seat(n)
    reduce = Reduce(seat, chunk_ref, *scratch[:5])
    gather = Gather(seat, out_ref, *scratch[5:7])
    edges = Edges(seat, side_ref, *scratch[7:10])
    if fused:
        links = Links()
        whole_ref, send, recv = scratch[10:13]
        tiles = Tiles(links, True, r2_ref, act_ref, whole_ref, scratch[13:])
        scatter = Scatter(0, links, [whole_ref, part_ref], send, recv)
        seat.hello(True, links.devices[2:])
    else:
        seat.hello(True)
    reduce.start()
    edges.start()
    reduce.middle(add_all)
    if fused:
        tiles.compute(0)
        tiles.compute(1)
        tiles.absorb(0)
        tiles.compute(2)
        tiles.absorb(1)
    diagonal = diagonal_mask()
    eye = unit()
    stats = per * MARKS
    gm[...] = reduce.finish(add_all)
    block = out_ref.at[seat.core, seat.z]
    block[stats:, :] = jnp.zeros((block.shape[0] - stats, PAIR), f32)
    for place in range(per):
        mixed = spread(gm[place * 2 * MARKS : place * 2 * MARKS + MARKS, :])
        context = spread(ctx_ref[place])
        grad = dot3(jnp.transpose(z_ref[NEWTON, place]), mixed)
        block[place * MARKS : (place + 1) * MARKS, :] = compacted(grad)
        dot = jnp.sum(grad * context, axis=1, keepdims=True)
        block[stats + place : stats + place + 1, :] = row_of(dot)
        gz[place] = jnp.where(diagonal, dot3(mixed, context, 1, 1), 0.0)
        ga[place] = jnp.zeros((PAIR, PAIR), f32)
    gather.start()

    def lap(back, _):
        step = NEWTON - 1 - back
        for place in range(per):
            a, z, g = a_ref[place], z_ref[step, place], 0.25 * gz[place]
            pr, n1, n2, n3 = newton_step(a, z, eye)
            back_three = dot3(jnp.transpose(z), g)
            turned = jnp.transpose(pr)
            back_two = -dot3(turned, back_three)
            back_one = -dot3(turned, back_two)
            grad = -dot3(back_three, n2, 1, 1) - dot3(back_two, n1, 1, 1) - back_one
            ga[place] += dot3(grad, z, 1, 1)
            gz[place] = dot3(g, n3, 1, 1) + dot3(jnp.transpose(a), grad)
        return 0

    if fused:
        tiles.compute(3)
        tiles.absorb(2)
        tiles.absorb(3)
        scatter.start()
        gather.forward()
        lax.fori_loop(0, NEWTON, lap, 0)
    else:
        lax.fori_loop(0, NEWTON - 1, lap, 0)
        gather.forward()
        lax.fori_loop(NEWTON - 1, NEWTON, lap, 0)
    for place in range(per):
        a, g = a_ref[place], jnp.transpose(gz[place])
        norm = head_total(a * a)
        slope = -head_total(g * a) / (norm * norm)
        grad = ga[place] + g / norm + 2.0 * slope * a
        scores = a * (grad - jnp.sum(a * grad, axis=1, keepdims=True))
        gq_ref[place] = compacted(dot3(scores, spread(lk_ref[place])))
        gk_ref[place] = gm[place * 2 * MARKS + MARKS : (place + 1) * 2 * MARKS, :] + compacted(
            dot3(jnp.transpose(scores), spread(lq_ref[place]))
        )
    edges.finish(halo_ref)
    gather.finish()
    if fused:
        scatter.advance()


def exchange_back_call(chunks, sides, ctx, a, z, lq, lk, n, rows, r2=None, act=None):
    per = ctx.shape[0]
    small = jax.ShapeDtypeStruct(ctx.shape, f32)
    chunk = chunks.shape[1:]
    blocks = (2, n // 2, rows, PAIR)
    fused = r2 is not None
    more_in, more_shapes, more_scratch = (), [], []
    if fused:
        more_in = (r2, act)
        more_shapes = [jax.ShapeDtypeStruct(landing(BIG, 0), f32)]
        more_scratch = [VM(landing(BIG, -1), f32)] + [pltpu.SemaphoreType.DMA((12,))] * 2
        more_scratch += Tiles.scratch(*act.shape[1:])
    out = pl.pallas_call(
        functools.partial(exchange_back_kernel, n, per, fused),
        out_shape=[
            jax.ShapeDtypeStruct(blocks, f32),
            small,
            small,
            jax.ShapeDtypeStruct(sides.shape, f32),
        ]
        + more_shapes,
        in_specs=[pl.BlockSpec(memory_space=VM)] * 7
        + [pl.BlockSpec(memory_space=pl.ANY)] * len(more_in),
        out_specs=[pl.BlockSpec(memory_space=VM)] * (4 + len(more_shapes)),
        scratch_shapes=[VM(chunk, f32)]
        + [VM((per, PAIR, PAIR), f32)] * 2
        + Reduce.scratch(n, chunk)
        + Gather.scratch(n)
        + Edges.scratch(sides.shape)
        + more_scratch,
        compiler_params=params(collective_id=2, has_side_effects=True),
        name="exchange_back",
    )(chunks.reshape((2, n // 2) + chunk), sides, ctx, a, z, lq, lk, *more_in)
    return [out[0].reshape(n, rows, PAIR)] + list(out[1:])


def keep_both(value, lanes, out_ref, turned_ref):
    out_ref[0, :, lanes] = value
    turned_ref[0, lanes, :] = jnp.transpose(value)


def both_specs(items, span, width):
    shapes = [(items, span, width), (items, width, span)]
    shapes = [jax.ShapeDtypeStruct(shape, f32) for shape in shapes]
    return shapes, [per_item((span, width)), per_item((width, span))]


def three_back_kernel(per, pairs, held, stat, w3_ref, top_ref, v_ref, k_ref, lq_ref,
                      gk_ref, gv_ref, chunk):
    item = pl.program_id(0)
    stats = per * MARKS

    @pl.when(item == 0)
    def _():
        chunk[...] = jnp.zeros_like(chunk)

    for p in range(pairs):
        lanes = slice(p * PAIR, (p + 1) * PAIR)
        owner, place = owned_by(item * pairs + p, per)
        grad = split(spread(held[owner, pl.ds(pl.multiple_of(place * MARKS, MARKS), MARKS), :]))
        row_dot = column_of(held[owner, pl.ds(stats + place, 1), :])
        largest = stat[owner, pl.ds(stats + 2 * place, 1), :]
        total = stat[owner, pl.ds(stats + 2 * place + 1, 1), :]
        scale = column_of(jnp.exp(top_ref[0, p : p + 1, :] - largest) / total)
        k3 = w3_ref[0, lanes, :] * scale[:, 0:1]
        gk3 = dots(grad, split(v_ref[0, :, lanes]), 1, 1)
        scores = split(k3 * (gk3 - row_dot[:, 0:1]))
        gv_ref[0, :, lanes] = dots(split(k3), grad, 0, 0)
        gk_ref[0, :, lanes] = dots(scores, split(spread(lq_ref[0, :, lanes])), 0, 0)
        part = compacted(dots(scores, split(k_ref[0, :, lanes]), 1, 0))
        chunk[owner, pl.ds(pl.multiple_of(place * MARKS, MARKS), MARKS), :] = part


def three_back_call(grads, blocks, w3, top, v, k, lq, per, pairs):
    items, span, width = v.shape
    out = (blocks.shape[0], per * MARKS, PAIR)
    wide = per_item((span, width))
    shape = jax.ShapeDtypeStruct((items, span, width), f32)
    return pl.pallas_call(
        functools.partial(three_back_kernel, per, pairs),
        out_shape=[shape, shape, jax.ShapeDtypeStruct(out, f32)],
        grid=(items,),
        in_specs=[whole(blocks.shape)] * 2
        + [per_item((width, span)), per_item((8, PAIR)), wide, wide]
        + [per_item((MARKS, width))],
        out_specs=[wide, wide, whole(out)],
        compiler_params=params(),
        name="three_back",
    )(grads, blocks, w3, top, v, k, lq)


def land_exchange_kernel(n, per, pairs, margin, fused, *refs):
    refs = list(refs)
    chunk_ref, q_ref, k_ref = refs[:3]
    convolution, refs = refs[3:9], refs[9:]
    if fused:
        in_down, hid_ref, u_ref, out_ref, gv_ref, gtaps_ref, down_ref, part_ref, *scratch = refs
    else:
        out_ref, gv_ref, gtaps_ref, *scratch = refs
    conv = ConvBack(pairs, margin, *convolution, gv_ref, gtaps_ref, scratch[:4])
    scratch = scratch[4:]

    def conv_lap(item, _):
        conv.item(item)
        return 0

    seat = Seat(n)
    reduce = Reduce(seat, chunk_ref, *scratch[:5])
    gather = Gather(seat, out_ref, *scratch[5:7])
    if fused:
        links = Links()
        second, third, whole_ref, send, recv = scratch[7:12]
        down = Scatter(0, links, [in_down, second, third, down_ref], send, recv, 1)
        up = Scatter(1, links, [whole_ref, part_ref], send, recv)
        tiles = Tiles(links, False, hid_ref, u_ref, whole_ref, scratch[12:])
        seat.hello(False, links.devices[2:])
    else:
        seat.hello(False)
    reduce.start()
    reduce.middle(add_all)
    if fused:
        down.start()
        tiles.compute(0)
    half = per * MARKS
    block = out_ref.at[seat.core, seat.z]
    block[half:, :] = k_ref[...]
    block[:half, :] = q_ref[...] + reduce.finish(add_all)
    gather.start()
    if fused:
        tiles.compute(1)
        tiles.absorb(0)
        down.advance()
        tiles.compute(2)
        tiles.absorb(1)
        tiles.compute(3)
        tiles.absorb(2)
        down.advance()
    conv.begin()
    items = gv_ref.shape[0]
    if fused:
        tiles.absorb(3)
        up.start()
    lax.fori_loop(0, items // 2, conv_lap, 0)
    gather.forward()
    lax.fori_loop(items // 2, items, conv_lap, 0)
    conv.end()
    gather.finish()
    if fused:
        down.advance()
        up.advance()


def land_exchange_call(chunks, own_q, own_k, convolution, n, pairs, margin, in_down=None, hidden=None, u=None):
    per = own_q.shape[0]
    half = per * MARKS
    blocks = (2, n // 2, 2 * half, PAIR)
    fused = in_down is not None
    conv_shapes = [convolution[0].shape, (-(-2 * pairs // 8) * 8, 2 * PAIR)]
    vmem = pl.BlockSpec(memory_space=VM)
    more_in, more_specs, more_shapes, more_scratch = (), [], [], []
    if fused:
        more_in = (in_down, hidden, u)
        more_specs = [vmem] + [pl.BlockSpec(memory_space=pl.ANY)] * 2
        more_shapes = [landing(BIG, 3), landing(BIG, 0)]
        more_scratch = [VM(landing(BIG, stage), f32) for stage in (1, 2, -1)]
        more_scratch += [pltpu.SemaphoreType.DMA((24,))] * 2
        more_scratch += Tiles.scratch(*u.shape[1:])
    out = pl.pallas_call(
        functools.partial(land_exchange_kernel, n, per, pairs, margin, fused),
        out_shape=[jax.ShapeDtypeStruct(shape, f32) for shape in [blocks, *conv_shapes] + more_shapes],
        in_specs=[vmem] * 9 + more_specs,
        out_specs=[vmem] * (3 + len(more_shapes)),
        scratch_shapes=ConvBack.scratch(pairs, margin, *convolution[0].shape[1:])
        + Reduce.scratch(n, (half, PAIR)) + Gather.scratch(n) + more_scratch,
        compiler_params=params(collective_id=3, has_side_effects=True),
        name="land_exchange",
    )(
        chunks.reshape(2, n // 2, half, PAIR),
        own_q.reshape(half, PAIR),
        own_k.reshape(half, PAIR),
        *convolution,
        *more_in,
    )
    return [out[0].reshape(n, 2 * half, PAIR)] + list(out[1:])


def land_back_kernel(per, pairs, factor, held, gq_ref, gk_ref, gv_ref, gvc_ref, mem_ref, inv_ref, *outs):
    sums_ref = outs[6]
    item = pl.program_id(0)
    half = per * MARKS

    @pl.when(item == 0)
    def _():
        sums_ref[...] = jnp.zeros_like(sums_ref)

    member = mem_ref[0].astype(bf16)
    inv = inv_ref[0]
    for p in range(pairs):
        lanes = slice(p * PAIR, (p + 1) * PAIR)
        slot, place = owned_by(item * pairs + p, per)
        for ref, out, base in ((gq_ref, outs[:2], 0), (gk_ref, outs[2:4], half)):
            grad = held[slot, pl.ds(pl.multiple_of(base + place * MARKS, MARKS), MARKS), :]
            hi, lo = split(grad * inv)
            landed = dg(member, hi, 0, 0) + dg(member, lo, 0, 0)
            total = (ref[0, :, lanes] + landed) * factor
            keep_both(total, lanes, *out)
            if base == 0:
                sums_ref[0:1, lanes] += jnp.sum(total, axis=0, keepdims=True)
        total = gv_ref[0, :, lanes] + gvc_ref[0, :, lanes]
        keep_both(total, lanes, *outs[4:6])
        sums_ref[1:2, lanes] += jnp.sum(total, axis=0, keepdims=True)


def land_back_call(blocks, gq, gk, gv, gv_conv, member_t, inv, per, pairs, factor):
    items, span, width = gq.shape
    wide = per_item((span, width))
    shapes, specs = both_specs(items, span, width)
    out = pl.pallas_call(
        functools.partial(land_back_kernel, per, pairs, factor),
        out_shape=shapes * 3 + [jax.ShapeDtypeStruct((8, width), f32)],
        grid=(items,),
        in_specs=[whole(blocks.shape)] + [wide] * 4
        + [per_item((MARKS, span)), per_item((MARKS, PAIR))],
        out_specs=specs * 3 + [whole((8, width))],
        compiler_params=params(),
        name="land_back",
    )(blocks, gq, gk, gv, gv_conv, member_t, inv)
    return out[:2], out[2:4], out[4:6], out[6]


def grads_kernel(
    r1t_ref, x_ref, gqt_ref, gkt_ref, gvt_ref, tok_ref, gq_ref, gk_ref, gv_ref, wq_ref, wk_ref, wv_ref, r1_ref,
    in_up, sums_ref, late_ref, bsum_ref, taps_ref,
    vo_ref, up_ref, qk_ref, gt_ref, total_ref,
    s_slots, s_first, s_second, t_slots, w_s, p_pair, *scratch
):
    vo_bufs, qk_bufs, up_bufs = list(scratch[:4]), list(scratch[4:8]), list(scratch[8:10])
    held, caught, load_sem, s_sem, t_sem, core_send, core_recv, send, recv, sum_send, sum_recv = scratch[10:]
    links = Links()
    width = tok_ref.shape[1]
    ff = bsum_ref.shape[1]
    s_loads = Loads([gvt_ref, r1t_ref, gqt_ref, gkt_ref], s_slots, s_sem)
    t_loads = Loads(
        [tok_ref, x_ref, gv_ref, wv_ref, gq_ref, wq_ref, gk_ref, wk_ref], t_slots, t_sem
    )
    residual = pltpu.make_async_copy(r1_ref, gt_ref, load_sem.at[0])
    residual.start()
    barrier = pltpu.get_barrier_semaphore()
    for device in (links.partner, *links.devices):
        pl.semaphore_signal(barrier, inc=1, device_id=device, device_id_type=MESH)
    pl.semaphore_wait(barrier, 5)
    up = Scatter(0, links, [in_up, *up_bufs, up_ref], send, recv, 1, EVEN)
    vo = Scatter(1, links, [*vo_bufs, vo_ref], send, recv, orders=EVEN)
    qk = Scatter(2, links, [*qk_bufs, qk_ref], send, recv, orders=EVEN)
    up.start()

    def halfway(step):
        return pltpu.make_async_remote_copy(
            src_ref=held.at[step], dst_ref=caught.at[step],
            send_sem=sum_send.at[step], recv_sem=sum_recv.at[step],
            device_id=(links.partner, *links.devices)[step], device_id_type=MESH,
        )

    held[0] = jnp.zeros(held.shape[1:], f32)
    held[0, 0:8, :] = sums_ref[...]
    held[0, 8:16, :] = late_ref[...]
    for i, t in enumerate(range(0, ff, width)):
        held[0, 16 + i : 17 + i, :] = bsum_ref[:, t : t + width]
    held[0, 24:40, : 2 * PAIR] = taps_ref[...]
    halfway(0).start()

    def sums_on(step):
        halfway(step).wait()
        added = held[step] + caught[step]
        if step < 4:
            held[step + 1] = added
            halfway(step + 1).start()
        else:
            total_ref[...] = added

    def pair_job(first, second, t_first, t_second):
        half = PAIR // 2
        for which, (s, t) in enumerate(((first, t_first), (second, t_second))):
            for third in range(3):
                g = times(s, t, slice(third * 256, (third + 1) * 256))
                for unit in range(4):
                    block, k = divmod(4 * third + unit, 3)
                    color, side = divmod(3 * which + k, 2)
                    lanes = slice(side * half, (side + 1) * half)
                    for j in range(8):
                        at = (links.apart[j % 2], color, j // 4, j // 2 % 2, block // 2, block % 2)
                        p_pair[(*at, slice(None), lanes)] = g[
                            j * 96 : (j + 1) * 96, unit * half : (unit + 1) * half
                        ]

    def absorb(copy, buffer):
        copy.wait()
        buffer[...] = buffer[...] + p_pair[0]

    def token_job(i):
        x, w = t_loads.get(2 + 2 * i), t_loads.get(3 + 2 * i)
        halved(w, w_s)
        for c in range(0, gt_ref.shape[0], 2 * PAIR):
            rows = slice(c, c + 2 * PAIR)
            gt_ref[rows, :] += dots(split(x[rows, :]), (w_s[0], w_s[1]), 1, 1)
        t_loads.release(2 + 2 * i)
        t_loads.release(3 + 2 * i)

    tokens = t_loads.get(0)
    halved(s_loads.get(0), s_first)
    s_loads.release(0)
    halved(s_loads.get(1), s_second)
    s_loads.release(1)
    pair_job(s_first, s_second, tokens, t_loads.get(1))
    t_loads.release(1)
    vo_copy = links.copy(0, p_pair.at[1], vo_bufs[0], core_send, core_recv)
    vo_copy.start()
    sums_on(0)
    up.advance()
    residual.wait()
    token_job(0)
    absorb(vo_copy, vo_bufs[0])
    vo.start()
    halved(s_loads.get(2), s_first)
    halved(s_loads.get(3), s_second)
    pair_job(s_first, s_second, tokens, tokens)
    t_loads.release(0)
    qk_copy = links.copy(1, p_pair.at[1], qk_bufs[0], core_send, core_recv)
    qk_copy.start()
    vo.advance()
    up.advance()
    sums_on(1)
    token_job(1)
    absorb(qk_copy, qk_bufs[0])
    qk.start()
    vo.advance()
    sums_on(2)
    token_job(2)
    up.advance()
    qk.advance()
    vo.advance()
    sums_on(3)
    qk.advance()
    sums_on(4)
    vo.advance()
    qk.advance()
    qk.advance()


def grads_call(arrays, r1, in_up, sums):
    rows, width = r1.shape
    any_space = pl.BlockSpec(memory_space=pl.ANY)
    vmem = pl.BlockSpec(memory_space=VM)
    dma = pltpu.SemaphoreType.DMA
    out_shapes = [
        landing(SMALL, 3), landing(BIG, 3), landing(SMALL, 3), (rows, width), (40, width),
    ]
    return pl.pallas_call(
        grads_kernel,
        out_shape=[jax.ShapeDtypeStruct(shape, f32) for shape in out_shapes],
        in_specs=[any_space] * (len(arrays) + 1) + [vmem] * (1 + len(sums)),
        out_specs=[vmem] * 5,
        scratch_shapes=[
            VM((2, width, rows), f32),
            VM((2, width, rows), bf16),
            VM((2, width, rows), bf16),
            VM((4, rows, width), f32),
            VM((2, width, width), bf16),
            VM((2, 3, 2, 2, 2, 2) + SMALL, f32),
        ]
        + [VM(landing(SMALL, stage), f32) for stage in (-1, 0, 1, 2)] * 2
        + [VM(landing(BIG, stage), f32) for stage in (1, 2)]
        + [VM((5, 40, width), f32)] * 2
        + [dma((1,)), dma((2, 4)), dma((4, 1)), dma((2,)), dma((2,))]
        + [dma((36,)), dma((36,)), dma((5,)), dma((5,))],
        compiler_params=params(collective_id=4, has_side_effects=True),
        name="grads",
    )(*arrays, r1, in_up, *sums)


def swap(x, axis, offset):
    count = lax.axis_size(axis)
    return lax.ppermute(x, axis, [(i, i ^ offset) for i in range(count)])


def both_sides(x, margin):
    return jnp.stack([x[:, :margin], x[:, -margin:]])


def bit_of(axis, bit):
    return lax.axis_index(axis) // bit % 2


def halve_rows(x, bit):
    blocks, rows, columns = x.shape
    y = x.reshape(blocks // 2, 2, rows, columns)
    mine = bit_of("seq", bit)
    keep = lax.dynamic_index_in_dim(y, mine, 1, False)
    send = lax.dynamic_index_in_dim(y, 1 - mine, 1, False)
    return keep + swap(send, "seq", bit)


def halve_columns(x, bits, bit):
    mine = bit_of("dp", bit)
    columns = x.shape[2]
    groups = 2 ** bits.index(bit)
    size = columns // (2 * groups)

    def pick(which):
        parts = [
            lax.dynamic_slice_in_dim(x, 2 * g * size + which * size, size, 2)
            for g in range(groups)
        ]
        return parts[0] if groups == 1 else jnp.concatenate(parts, axis=2)

    return pick(mine) + swap(pick(1 - mine), "dp", bit)


def powers(axis):
    count = lax.axis_size(axis)
    return [2**i for i in range(count.bit_length() - 1)]


def scatter_sum(x, order):
    seq_bits, dp_bits = powers("seq"), powers("dp")[::-1]
    count = lax.axis_size("seq")
    x = x.reshape(count, x.shape[0] // count, x.shape[1])
    x = halve_rows(x, seq_bits.pop(0))
    for axis in order:
        if axis == "z" and seq_bits:
            x = halve_rows(x, seq_bits.pop(0))
        elif axis in "xy" and dp_bits:
            half = len(powers("dp")) // 2
            low = [b for b in dp_bits if b < 2**half]
            high = [b for b in dp_bits if b >= 2**half]
            chosen = (low if axis == "x" else high) or dp_bits
            x = halve_columns(x, dp_bits, chosen[0])
            dp_bits.remove(chosen[0])
    while seq_bits:
        x = halve_rows(x, seq_bits.pop(0))
    while dp_bits:
        x = halve_columns(x, dp_bits, dp_bits[0])
        dp_bits.pop(0)
    return x[0]


def sum_everywhere(x):
    for axis in ("seq", "dp"):
        for bit in powers(axis):
            x = x + swap(x, axis, bit)
    return x


def product(a, b, ca, cb):
    return lax.dot_general(a, b, (((ca,), (cb,)), ((), ())), precision=HIGH)


def on_device(
    tokens,
    lengths,
    keep,
    w_query,
    b_query,
    w_key,
    w_value,
    b_value,
    conv_weight,
    w_out,
    b_out,
    gain_one,
    shift_one,
    w_up,
    b_up,
    w_down,
    b_down,
    gain_two,
    shift_two,
    cotangent,
):
    items, span, width = tokens.shape
    heads, taps = conv_weight.shape
    head_size = width // heads
    margin = taps // 2
    factor = head_size ** (-0.25)
    pairs = heads // 2
    n = lax.axis_size("seq")
    per = -(-items * pairs // n)
    chunk_rows = per * MARKS + 8
    position = lax.axis_index("seq") * span + jnp.arange(span, dtype=jnp.int32)
    inside = position[None, :] < lengths[:, None]
    usable = (inside & (keep > 0)).astype(f32)
    use_row, use_col = usable[:, None, :], usable[:, :, None]
    segment = jnp.where(inside, position[None, :] * MARKS // lengths[:, None], MARKS)
    marks = jnp.arange(MARKS, dtype=jnp.int32)
    member_t = (segment[:, None, :] == marks[None, :, None]).astype(f32) * use_row
    rows = tokens.reshape(items * span, width)
    taps_forward = jnp.pad(conv_weight, ((0, 4), (0, 2 * PAIR - taps)))
    taps_backward = jnp.pad(conv_weight[:, ::-1], ((0, 4), (0, 2 * PAIR - taps)))

    queries, key_rows, values, land_q, land_k, inverse_divisor = project_call(
        tokens, member_t, w_query, w_key, w_value, jnp.stack([b_query, b_value]), n, factor
    )
    k1, w3, top, chunks = scores_call(
        queries, key_rows, values, land_q, land_k, use_row, n, per, pairs, chunk_rows
    )
    use_sides = both_sides(use_col, margin)
    kernel_two, z, owned_q, owned_k, context, mixed, vhalos = exchange_call(
        chunks, land_q, land_k, both_sides(values, margin) * use_sides, n, per, pairs
    )
    x = mix_call(mixed, k1, values, use_col, vhalos, taps_forward, per, pairs, margin)

    def flat(array):
        return array.reshape(items * span, width)

    x = flat(x)
    vectors = jnp.stack([b_out, gain_one, shift_one, b_down, gain_two, shift_two])
    output, act, u, r2_t, hidden_t, r1_t, r1, og, row_sums, up_sums = rows_call(
        x, rows, cotangent.reshape(items * span, width), w_out, w_up, w_down, vectors, b_up[None, :]
    )
    og = og.reshape(items, span, width)
    grad_queries, chunks = one_back_call(mixed, k1, og, queries, land_k, per, pairs)
    ff = w_up.shape[1]
    fused = (n, lax.axis_size("dp"), width, ff) == (8, 4, 768, 3072)
    grad_context, own_q, own_k, ghalos, *down_part = exchange_back_call(
        chunks, both_sides(og, margin), context, kernel_two, z, owned_q, owned_k, n, chunk_rows,
        *((r2_t, act) if fused else ()),
    )
    grad_keys, grad_values, chunks = three_back_call(
        grad_context, mixed, w3, top, values, key_rows, land_q, per, pairs
    )
    land_grads, gv_conv, grad_taps, *ff_grads = land_exchange_call(
        chunks, own_q, own_k, (og, ghalos, values, vhalos, use_col, taps_backward), n, pairs, margin,
        *((*down_part, hidden_t, u) if fused else ()),
    )
    gq, gk, gv, late_sums = land_back_call(
        land_grads, grad_queries, grad_keys, grad_values, gv_conv,
        member_t, inverse_divisor, per, pairs, factor,
    )
    if fused:
        down, up_part = ff_grads
        vo, up, qk, grad_tokens, totals = grads_call(
            [r1_t, x, gq[1], gk[1], gv[1], rows, flat(gq[0]), flat(gk[0]), flat(gv[0])]
            + [w_query, w_key, w_value],
            r1,
            up_part,
            [row_sums, late_sums, up_sums, grad_taps],
        )
        vo, qk = (jnp.transpose(both, (0, 2, 1)).reshape(2, -1, both.shape[1]) for both in (vo, qk))
        grad_w_value, grad_w_out = vo[0], vo[1]
        grad_w_query, grad_w_key = qk[0], qk[1]
        down = down.reshape(3, 2, -1, PAIR)
        grad_w_down = jnp.transpose(down, (0, 1, 3, 2)).reshape(-1, down.shape[2])
        grad_w_up = jnp.transpose(up, (1, 0, 2)).reshape(up.shape[1], -1)
    else:
        def unturned(array):
            return flat(jnp.swapaxes(array, 1, 2))

        def untiled(array):
            return jnp.swapaxes(array, 0, 1).reshape(items * span, ff)

        gq, gk, gv = (flat(pair[0]) for pair in (gq, gk, gv))
        grad_w_down = scatter_sum(product(unturned(r2_t), untiled(act), 0, 0), "yxzz").T
        grad_w_up = scatter_sum(product(untiled(u), unturned(hidden_t), 0, 0), "xzyz").T
        grad_w_out = scatter_sum(product(r1, x, 0, 0), "zyxz").T
        grad_w_value = scatter_sum(product(gv, rows, 0, 0), "zyxz").T
        grad_w_query = scatter_sum(product(gq, rows, 0, 0), "yxzz").T
        grad_w_key = scatter_sum(product(gk, rows, 0, 0), "xzyz").T
        grad_tokens = (
            r1
            + product(gv, w_value, 1, 1)
            + product(gq, w_query, 1, 1)
            + product(gk, w_key, 1, 1)
        )
        taps_rows = jnp.pad(grad_taps, ((0, 0), (0, width - grad_taps.shape[1])))
        up_rows = jnp.pad(up_sums.reshape(-1, width), ((0, 8 - ff // width), (0, 0)))
        totals = sum_everywhere(jnp.concatenate([row_sums, late_sums, up_rows, taps_rows]))
    row_sums, late = totals[:8], totals[8:16]
    up_sums = totals[16 : 16 + ff // width].reshape(ff)
    grad_conv = totals[24 : 24 + heads, PAIR - 1 : PAIR - 1 + taps]
    return (
        output.reshape(tokens.shape),
        grad_tokens.reshape(tokens.shape),
        grad_w_query,
        late[0],
        grad_w_key,
        grad_w_value,
        late[1],
        grad_conv,
        grad_w_out,
        row_sums[5],
        row_sums[3],
        row_sums[4],
        grad_w_up,
        up_sums,
        grad_w_down,
        row_sums[2],
        row_sums[0],
        row_sums[1],
    )


def solution(mesh):
    rows = P("dp", "seq", None)
    block = P("dp", "seq")
    in_specs = (rows, P("dp"), block) + (P(),) * 16 + (rows,)
    out_specs = (
        rows, rows, block, P(), block, block, P(), P(), block,
        P(), P(), P(), block, P(), block, P(), P(), P(),
    )
    return jax.shard_map(
        on_device, mesh=mesh, in_specs=in_specs, out_specs=out_specs, check_vma=False
    )
```

```python
import functools

import jax
import jax.numpy as jnp
from jax import lax
from jax.experimental import pallas as pl
from jax.experimental.pallas import tpu as pltpu
from jax.sharding import PartitionSpec as P

MARKS = 64
NEWTON = 6
PAIR = 128
HIGH = lax.Precision.HIGH
epsilon = 1e-05
f32 = jnp.float32
bf16 = jnp.bfloat16
VM = pltpu.VMEM
LIMIT = 66 * 1024 * 1024


def split(x):
    hi = x.astype(bf16)
    return hi, (x - hi.astype(f32)).astype(bf16)


def dg(a, b, ca, cb):
    return lax.dot_general(a, b, (((ca,), (cb,)), ((), ())), preferred_element_type=f32)


def dots(a, b, ca, cb):
    return dg(a[0], b[0], ca, cb) + dg(a[0], b[1], ca, cb) + dg(a[1], b[0], ca, cb)


def dot3(a, b, ca=1, cb=0):
    return dots(split(a), split(b), ca, cb)


def lane_low(shape):
    return lax.broadcasted_iota(jnp.int32, shape, len(shape) - 1) < PAIR // 2


def spread(compact):
    low = lane_low(compact.shape)
    zero = jnp.zeros_like(compact)
    return jnp.concatenate([jnp.where(low, compact, zero), jnp.where(low, zero, compact)], axis=0)


def compacted(block):
    half = block.shape[0] // 2
    return jnp.where(lane_low((half, block.shape[1])), block[:half], block[half:])


def row_of(column):
    return jnp.transpose(jnp.broadcast_to(column, (PAIR, PAIR)))[0:1, :]


def column_of(row):
    return jnp.transpose(jnp.broadcast_to(row, (PAIR, PAIR)))


def diagonal_mask():
    rows = lax.broadcasted_iota(jnp.int32, (PAIR, PAIR), 0) < PAIR // 2
    return rows == lane_low((PAIR, PAIR))


def block_sum(x):
    halves = x.reshape(2, x.shape[0] // 2, x.shape[1])
    total = jnp.sum(halves, axis=1, keepdims=True)
    return jnp.broadcast_to(total, halves.shape).reshape(x.shape)


def block_max(x):
    halves = x.reshape(2, x.shape[0] // 2, x.shape[1])
    total = jnp.max(halves, axis=1, keepdims=True)
    return jnp.broadcast_to(total, halves.shape).reshape(x.shape)


def params(**more):
    return pltpu.CompilerParams(vmem_limit_bytes=LIMIT, **more)


def whole(shape):
    return pl.BlockSpec(shape, lambda *_: (0,) * len(shape))


def per_item(shape):
    return pl.BlockSpec((1,) + shape, lambda i, *_: (i,) + (0,) * len(shape))


class Seat:
    def __init__(self, n):
        self.n, self.nz = n, n // 2
        self.me = lax.axis_index("seq")
        self.core = lax.rem(self.me, 2)
        self.z = self.me // 2
        self.owner = self.core * self.nz + self.z
        self.partner = self.me + 1 - 2 * self.core
        self.extra = lax.rem(self.me + 2 * self.core - 1 + n, n)

    def ahead(self, j):
        return lax.rem(self.z + j, self.nz)

    def behind(self, j):
        return lax.rem(self.z - j + self.nz, self.nz)

    def at(self, z):
        return 2 * z + self.core

    def hello(self, edges, more=()):
        others = [self.partner] + [self.at(self.ahead(j)) for j in range(1, self.nz)]
        if edges:
            others.append(self.extra)
        others = [{"seq": other} for other in others] + list(more)
        barrier = pltpu.get_barrier_semaphore()
        for other in others:
            pl.semaphore_signal(barrier, inc=1, device_id=other, device_id_type=MESH)
        pl.semaphore_wait(barrier, len(others))


MESH = pl.DeviceIdType.MESH


def remote(src, dst, send, recv, device):
    return pltpu.make_async_remote_copy(
        src_ref=src, dst_ref=dst, send_sem=send, recv_sem=recv,
        device_id={"seq": device}, device_id_type=MESH,
    )


class Reduce:
    def __init__(self, seat, chunks, first, acc, second, send, recv):
        self.seat, self.chunks, self.first, self.acc, self.second = seat, chunks, first, acc, second
        self.send, self.recv = send, recv
        self.across = remote(chunks.at[1 - seat.core], first, send.at[0], recv.at[0], seat.partner)
        self.along = [
            remote(
                acc.at[seat.ahead(j)], second.at[j - 1], send.at[j], recv.at[j],
                seat.at(seat.ahead(j)),
            )
            for j in range(1, seat.nz)
        ]

    def start(self):
        self.across.start()

    def middle(self, merge):
        self.across.wait()
        for z in range(self.seat.nz):
            self.acc[z] = merge([self.chunks.at[self.seat.core, z], self.first.at[z]])
        for copy in self.along:
            copy.start()

    def finish(self, merge):
        for copy in self.along:
            copy.wait()
        refs = [self.acc.at[self.seat.z]] + [self.second.at[j] for j in range(self.seat.nz - 1)]
        return merge(refs)

    @staticmethod
    def scratch(n, shape):
        nz = n // 2
        return [
            VM((nz,) + shape, f32),
            VM((nz,) + shape, f32),
            VM((nz - 1,) + shape, f32),
            pltpu.SemaphoreType.DMA((nz,)),
            pltpu.SemaphoreType.DMA((nz,)),
        ]


class Gather:
    def __init__(self, seat, out, send, recv):
        own = out.at[seat.core, seat.z]
        self.along = [
            remote(own, own, send.at[j], recv.at[j], seat.at(seat.ahead(j)))
            for j in range(1, seat.nz)
        ]
        self.across = [remote(own, own, send.at[0], recv.at[0], seat.partner)]
        for j in range(1, seat.nz):
            block = out.at[seat.core, seat.behind(j)]
            k = seat.nz + j
            self.across.append(remote(block, block, send.at[k], recv.at[k], seat.partner))

    def start(self):
        for copy in self.along:
            copy.start()
        self.across[0].start()

    def forward(self):
        for copy, onward in zip(self.along, self.across[1:]):
            copy.wait_recv()
            onward.start()

    def finish(self):
        for copy in self.along:
            copy.wait_send()
        for copy in self.across:
            copy.wait()

    @staticmethod
    def scratch(n):
        return [pltpu.SemaphoreType.DMA((n,)), pltpu.SemaphoreType.DMA((n,))]


class Edges:
    def __init__(self, seat, sides, halos, send, recv):
        self.seat, self.halos = seat, halos
        core = seat.core
        self.copies = [
            remote(sides.at[1 - core], halos.at[core], send.at[0], recv.at[0], seat.partner),
            remote(sides.at[core], halos.at[1 - core], send.at[1], recv.at[1], seat.extra),
        ]

    def start(self):
        for copy in self.copies:
            copy.start()

    def finish(self, out):
        for copy in self.copies:
            copy.wait()
        seat = self.seat
        inner = (jnp.where(seat.me > 0, 1.0, 0.0), jnp.where(seat.me < seat.n - 1, 1.0, 0.0))
        for side in range(2):
            out[side] = self.halos[side] * inner[side]

    @staticmethod
    def scratch(shape):
        return [VM(shape, f32), pltpu.SemaphoreType.DMA((2,)), pltpu.SemaphoreType.DMA((2,))]


def add_all(refs):
    return functools.reduce(lambda x, y: x + y, [r[...] for r in refs])


def partner_of(index, bit):
    return index + bit - 2 * bit * lax.rem(index // bit, 2)


class Loads:
    def __init__(self, sources, slots, sems):
        self.count = slots.shape[0]
        self.views, self.copies = [], []
        for i, src in enumerate(sources):
            slot = i % self.count
            view = slots.at[slot, : src.shape[-2]]
            self.views.append(view)
            if len(src.shape) == 2:
                self.copies.append([pltpu.make_async_copy(src, view, sems.at[slot, 0])])
                continue
            size = src.shape[2]
            self.copies.append(
                [
                    pltpu.make_async_copy(
                        src.at[j], view.at[:, j * size : (j + 1) * size], sems.at[slot, j]
                    )
                    for j in range(src.shape[0])
                ]
            )
        for i in range(min(self.count, len(sources))):
            self.begin(i)

    def begin(self, i):
        for copy in self.copies[i]:
            copy.start()

    def get(self, i):
        for copy in self.copies[i]:
            copy.wait()
        return self.views[i]

    def release(self, i):
        if i + self.count < len(self.copies):
            self.begin(i + self.count)


def halved(view, into):
    size = 64

    def lap(k, _):
        part = pl.ds(pl.multiple_of(k * size, size), size)
        into[0, part, :], into[1, part, :] = split(view[part, :])
        return 0

    lax.fori_loop(0, into.shape[1] // size, lap, 0)
    return into


ALL_LINKS = ((2, 3, 1, 0), (3, 2, 1, 0), (1, 3, 2, 0))
EVEN = ((2, 1, 3, 0), (3, 2, 1, 0), (1, 3, 2, 0))


class Links:
    def __init__(self):
        me, dp = lax.axis_index("seq"), lax.axis_index("dp")
        z = me // 2
        self.core = lax.rem(me, 2)
        self.mine = (z // 2, lax.rem(z, 2), dp // 2, lax.rem(dp, 2))
        self.partner = {"seq": partner_of(me, 1)}
        self.devices = (
            {"seq": partner_of(me, 4)},
            {"seq": partner_of(me, 2)},
            {"dp": partner_of(dp, 2)},
            {"dp": partner_of(dp, 1)},
        )
        self.apart = (self.core, 1 - self.core)

    def copy(self, k, src, dst, send, recv):
        return pltpu.make_async_remote_copy(
            src_ref=src, dst_ref=dst, send_sem=send.at[k], recv_sem=recv.at[k],
            device_id=self.partner, device_id_type=MESH,
        )


class Scatter:
    def __init__(self, base, links, buffers, send, recv, first=0, orders=ALL_LINKS):
        self.orders = orders
        self.links, self.buffers, self.first, self.stage = links, buffers, first, first
        self.copies = {}
        for stage in range(first, first + len(buffers) - 1):
            for color, order in enumerate(self.orders):
                dim = order[stage]
                k = (base * 3 + color) * 4 + stage
                self.copies[stage, color] = pltpu.make_async_remote_copy(
                    src_ref=self.part(color, stage, 1 - links.mine[dim]),
                    dst_ref=buffers[stage - first + 1].at[color],
                    send_sem=send.at[k],
                    recv_sem=recv.at[k],
                    device_id=links.devices[dim],
                    device_id_type=MESH,
                )

    def part(self, color, stage, index):
        order = self.orders[color]
        left = [dim for dim in range(4) if dim not in order[:stage]]
        place = [index if dim == order[stage] else slice(None) for dim in left]
        return self.buffers[stage - self.first].at[(color, *place)]

    def start(self):
        for color in range(3):
            self.copies[self.stage, color].start()

    def advance(self):
        stage = self.stage
        self.stage += 1
        for color, order in enumerate(self.orders):
            self.copies[stage, color].wait()
            landed = self.buffers[stage - self.first + 1].at[color]
            landed[...] = landed[...] + self.part(color, stage, self.links.mine[order[stage]])[...]
            if (stage + 1, color) in self.copies:
                self.copies[stage + 1, color].start()


def times(s, t, lanes):
    return dots((s[0], s[1]), split(t[:, lanes]), 1, 0)


BIG = (192, PAIR)
SMALL = (96, PAIR)


def landing(block, stage):
    return (3,) + (2,) * (3 - stage) + block


class Tiles:
    def __init__(self, links, down, s, t, buffer, scratch):
        self.links, self.down = links, down
        s_slots, self.s, t_slots, self.p_big, s_sem, t_sem, send, recv = scratch
        self.s_loads = Loads([s], s_slots, s_sem)
        self.t_loads = Loads([t.at[i] for i in range(4)], t_slots, t_sem)
        self.places, self.copies = [], []
        for i in range(4):
            at = (slice(None),) * (3 if down else 1) + (i // 2, i % 2)
            self.places.append(buffer.at[at])
            self.copies.append(links.copy(i, self.p_big.at[i % 2, 1], self.places[i], send, recv))

    def compute(self, i):
        if i == 0:
            halved(self.s_loads.get(0), self.s)
        t, slot, apart = self.t_loads.get(i), i % 2, self.links.apart
        core = self.links.core

        def lap(third, _):
            g = times(self.s, t, pl.ds(pl.multiple_of(third * 256, 256), 256))
            for side in range(2):
                lanes = slice(side * PAIR, (side + 1) * PAIR)
                if self.down:
                    for j in range(8):
                        at = (slot, apart[j % 2], third, j // 4, j // 2 % 2)
                        self.p_big[(*at, slice(side * 96, side * 96 + 96))] = g[j * 96 : (j + 1) * 96, lanes]
                else:
                    block = 2 * third + side
                    parity, color = block // 3, lax.rem(block, 3)
                    half = core + parity * (1 - 2 * core)
                    for j in range(4):
                        self.p_big[slot, half, color, j // 2, j % 2] = g[j * 192 : (j + 1) * 192, lanes]
            return 0

        lax.fori_loop(0, 3, lap, 0)
        self.t_loads.release(i)
        self.copies[i].start()

    def absorb(self, i):
        self.copies[i].wait()
        place = self.places[i]
        place[...] = place[...] + self.p_big[i % 2, 0]

    @staticmethod
    def scratch(rows, width):
        dma = pltpu.SemaphoreType.DMA
        return [
            VM((1, width, rows), f32),
            VM((2, width, rows), bf16),
            VM((2, rows, width), f32),
            VM((2, 2, 3, 2, 2) + BIG, f32),
            dma((1, 4)),
            dma((2, 1)),
            dma((4,)),
            dma((4,)),
        ]


def project_kernel(n, items, factor, tok_ref, mem_ref, wq_ref, wk_ref, wv_ref, vec_ref,
                   q_out, k_out, v_out, lq_ref, lk_ref, inv_ref,
                   q_ref, k_ref, v_ref, tok_h, tok_l, halves, w_s, w_sem, out_sem,
                   sums, land, *scratch):
    seat = Seat(n)
    rows = items * MARKS // n
    width = tok_ref.shape[2]
    reduce = Reduce(seat, sums, *scratch[:5])
    gather = Gather(seat, land, *scratch[5:])
    fetches = [
        pltpu.make_async_copy(ref, w_s.at[i], w_sem.at[i])
        for i, ref in enumerate((wq_ref, wk_ref, wv_ref))
    ]
    for fetch in fetches:
        fetch.start()
    stores = [
        pltpu.make_async_copy(src, dst, out_sem.at[i])
        for i, (src, dst) in enumerate(
            ((q_ref, q_out), (k_ref, k_out), (v_ref, v_out))
        )
    ]
    seat.hello(False)
    for item in range(items):
        member = mem_ref[item].astype(bf16)
        hi, lo = split(tok_ref[item])
        tok_h[item], tok_l[item] = hi, lo
        total = dg(member, hi, 1, 0) + dg(member, lo, 1, 0)
        count = jnp.sum(mem_ref[item], axis=1, keepdims=True)
        for part in range(MARKS // rows):
            c = item * (MARKS // rows) + part
            piece = slice(part * rows, (part + 1) * rows)
            sums[c // seat.nz, c % seat.nz, :, :width] = total[piece]
            sums[c // seat.nz, c % seat.nz, :, width:] = jnp.broadcast_to(
                count[piece], (rows, PAIR)
            )
    reduce.start()
    b_query, b_value = vec_ref[0:1, :], vec_ref[1:2, :]
    for place in range(3):
        fetches[place].wait()
        halved(w_s.at[place], halves.at[2 * place : 2 * place + 2])

    def project(place, out_ref, bias, scale):
        def lap(item, _):
            x = (tok_h[item], tok_l[item])
            y = dots(x, (halves[2 * place], halves[2 * place + 1]), 1, 0)
            y = y if bias is None else y + bias
            out_ref[item] = y if scale is None else y * scale
            return 0

        lax.fori_loop(0, items, lap, 0)

    project(0, q_ref, b_query, factor)
    stores[0].start()
    reduce.middle(add_all)
    project(1, k_ref, None, factor)
    stores[1].start()
    land[seat.core, seat.z] = reduce.finish(add_all)
    gather.start()
    project(2, v_ref, b_value, None)
    stores[2].start()
    gather.forward()
    gather.finish()
    whole_land = land[...].reshape(items * MARKS, width + PAIR)
    divisor = jnp.maximum(whole_land[:, width:], 1.0)
    inv_ref[...] = (1.0 / divisor).reshape(items, MARKS, PAIR)
    filled = whole_land[:, width : width + 1] / divisor[:, 0:1]
    x = split(whole_land[:, :width] / divisor[:, 0:1])
    lq = (dots(x, (halves[0], halves[1]), 1, 0) + filled * b_query) * factor
    lk = dots(x, (halves[2], halves[3]), 1, 0) * factor
    lq_ref[...] = lq.reshape(items, MARKS, width)
    lk_ref[...] = lk.reshape(items, MARKS, width)
    for store in stores:
        store.wait()


def project_call(tokens, member_t, w_query, w_key, w_value, vectors, n, factor):
    items, span, width = tokens.shape
    rows = items * MARKS // n
    big = jax.ShapeDtypeStruct((items, span, width), f32)
    small = jax.ShapeDtypeStruct((items, MARKS, width), f32)
    vmem, any_space = pl.BlockSpec(memory_space=VM), pl.BlockSpec(memory_space=pl.ANY)
    return pl.pallas_call(
        functools.partial(project_kernel, n, items, factor),
        out_shape=[big, big, big, small, small, jax.ShapeDtypeStruct((items, MARKS, PAIR), f32)],
        in_specs=[vmem] * 2 + [any_space] * 3 + [vmem],
        out_specs=[any_space] * 3 + [vmem] * 3,
        scratch_shapes=[VM((items, span, width), f32)] * 3
        + [VM((items, span, width), bf16)] * 2
        + [
            VM((6, width, width), bf16),
            VM((3, width, width), f32),
            pltpu.SemaphoreType.DMA((3,)),
            pltpu.SemaphoreType.DMA((3,)),
            VM((2, n // 2, rows, width + PAIR), f32),
            VM((2, n // 2, rows, width + PAIR), f32),
        ]
        + Reduce.scratch(n, (rows, width + PAIR))
        + Gather.scratch(n),
        compiler_params=params(collective_id=0, has_side_effects=True),
        name="project",
    )(tokens, member_t, w_query, w_key, w_value, vectors)


def scores_kernel(per, pairs, q_ref, k_ref, v_ref, lq_ref, lk_ref, use_ref, k1_ref, w3_ref, top_ref, chunk):
    item = pl.program_id(0)
    stats = per * MARKS

    @pl.when(item == 0)
    def _():
        chunk[...] = jnp.zeros_like(chunk)

    use = use_ref[0]
    for p in range(pairs):
        lanes = slice(p * PAIR, (p + 1) * PAIR)
        q = q_ref[0, :, lanes]
        s1 = dot3(spread(lk_ref[0, :, lanes]), q, 1, 1)
        e1 = jnp.exp(s1 - block_max(s1))
        k1_ref[0, lanes, :] = e1 / block_sum(e1)
        s3 = dot3(spread(lq_ref[0, :, lanes]), k_ref[0, :, lanes], 1, 1)
        masked = jnp.where(use > 0, s3, -1e30)
        top = jnp.max(masked, axis=1, keepdims=True)
        w3 = jnp.exp(masked - top) * use
        w3_ref[0, lanes, :] = w3
        total = jnp.sum(w3, axis=1, keepdims=True)
        weighted = compacted(dot3(w3, v_ref[0, :, lanes]))
        top_row = row_of(top)
        top_ref[0, p : p + 1, :] = top_row
        g = item * pairs + p
        owner, place = g // per, g % per
        chunk[owner, pl.ds(pl.multiple_of(place * MARKS, MARKS), MARKS), :] = weighted
        chunk[owner, pl.ds(stats + 2 * place, 1), :] = top_row
        chunk[owner, pl.ds(stats + 2 * place + 1, 1), :] = row_of(total)


def scores_call(q, k, v, lq, lk, use_row, n, per, pairs, chunk_rows):
    items, span, width = q.shape
    return pl.pallas_call(
        functools.partial(scores_kernel, per, pairs),
        out_shape=[
            jax.ShapeDtypeStruct((items, width, span), f32),
            jax.ShapeDtypeStruct((items, width, span), f32),
            jax.ShapeDtypeStruct((items, 8, PAIR), f32),
            jax.ShapeDtypeStruct((n, chunk_rows, PAIR), f32),
        ],
        grid=(items,),
        in_specs=[per_item((span, width))] * 3
        + [per_item((MARKS, width))] * 2
        + [per_item((1, span))],
        out_specs=[per_item((width, span))] * 2
        + [per_item((8, PAIR)), whole((n, chunk_rows, PAIR))],
        compiler_params=params(),
        name="scores",
    )(q, k, v, lq, lk, use_row)


def owned_land(seat, per, pairs, ref, into):
    for place in range(per):
        g = lax.rem(seat.owner * per + place, ref.shape[0] * pairs)
        item, p = g // pairs, lax.rem(g, pairs)
        into[place] = ref[item, :, pl.ds(pl.multiple_of(p * PAIR, PAIR), PAIR)]


def newton_step(a, z, eye):
    pr = dot3(a, z)
    n1 = 7.0 * eye - pr
    n2 = 15.0 * eye - dot3(pr, n1)
    n3 = 13.0 * eye - dot3(pr, n2)
    return pr, n1, n2, n3


def unit():
    rows = lax.broadcasted_iota(jnp.int32, (PAIR, PAIR), 0)
    return (rows == lax.broadcasted_iota(jnp.int32, (PAIR, PAIR), 1)).astype(f32)


def head_total(x):
    return block_sum(jnp.sum(x, axis=1, keepdims=True))


def merged(per, refs):
    stats = per * MARKS
    weights, rest = [], []
    for place in range(per):
        tops = [r[stats + 2 * place : stats + 2 * place + 1, :] for r in refs]
        largest = functools.reduce(jnp.maximum, tops)
        total = jnp.zeros_like(largest)
        weighted = jnp.zeros((MARKS, PAIR), f32)
        for r, top in zip(refs, tops):
            scale = jnp.exp(top - largest)
            total = total + scale * r[stats + 2 * place + 1 : stats + 2 * place + 2, :]
            scales = compacted(column_of(scale))
            weighted = weighted + scales * r[place * MARKS : (place + 1) * MARKS, :]
        weights.append(weighted)
        rest += [largest, total]
    filler = jnp.zeros((refs[0].shape[0] - stats - 2 * per, PAIR), f32)
    return jnp.concatenate(weights + rest + [filler], axis=0)


def exchange_kernel(n, per, pairs, chunk_ref, lq_ref, lk_ref, side_ref,
                    a_ref, z_ref, lqo_ref, lko_ref, ctx_ref, out_ref, halo_ref, mine, *scratch):
    seat = Seat(n)
    merge = functools.partial(merged, per)
    reduce = Reduce(seat, chunk_ref, *scratch[:5])
    gather = Gather(seat, out_ref, *scratch[5:7])
    edges = Edges(seat, side_ref, *scratch[7:])
    seat.hello(True)
    reduce.start()
    edges.start()
    owned_land(seat, per, pairs, lq_ref, lqo_ref)
    owned_land(seat, per, pairs, lk_ref, lko_ref)
    diagonal = diagonal_mask()
    eye = unit()
    for place in range(per):
        s2 = dot3(spread(lqo_ref[place]), spread(lko_ref[place]), 1, 1)
        s2 = jnp.where(diagonal, s2, -1e30)
        e2 = jnp.exp(s2 - jnp.max(s2, axis=1, keepdims=True))
        e2 = jnp.where(diagonal, e2, 0.0)
        a = e2 / jnp.sum(e2, axis=1, keepdims=True)
        a_ref[place] = a
        z_ref[0, place] = jnp.transpose(a) / head_total(a * a)
    reduce.middle(merge)

    def lap(step, _):
        for place in range(per):
            z = z_ref[step, place]
            _, _, _, n3 = newton_step(a_ref[place], z, eye)
            z_ref[step + 1, place] = 0.25 * dot3(z, n3)
        return 0

    lax.fori_loop(0, NEWTON, lap, 0)
    mine[...] = reduce.finish(merge)
    stats = per * MARKS
    block = out_ref.at[seat.core, seat.z]
    block[stats:, :] = mine[stats:, :]
    for place in range(per):
        rows = slice(place * MARKS, (place + 1) * MARKS)
        total = mine[stats + 2 * place + 1 : stats + 2 * place + 2, :]
        context = mine[rows, :] / compacted(column_of(total))
        ctx_ref[place] = context
        block[rows, :] = compacted(dot3(z_ref[NEWTON, place], spread(context)))
    gather.start()
    edges.finish(halo_ref)
    gather.forward()
    gather.finish()


def exchange_call(chunks, lq, lk, sides, n, per, pairs):
    rows = chunks.shape[1]
    small = jax.ShapeDtypeStruct((per, MARKS, PAIR), f32)
    blocks = (2, n // 2, rows, PAIR)
    out = pl.pallas_call(
        functools.partial(exchange_kernel, n, per, pairs),
        out_shape=[
            jax.ShapeDtypeStruct((per, PAIR, PAIR), f32),
            jax.ShapeDtypeStruct((NEWTON + 1, per, PAIR, PAIR), f32),
            small,
            small,
            small,
            jax.ShapeDtypeStruct(blocks, f32),
            jax.ShapeDtypeStruct(sides.shape, f32),
        ],
        in_specs=[pl.BlockSpec(memory_space=VM)] * 4,
        out_specs=[pl.BlockSpec(memory_space=VM)] * 7,
        scratch_shapes=[VM((rows, PAIR), f32)]
        + Reduce.scratch(n, (rows, PAIR))
        + Gather.scratch(n)
        + Edges.scratch(sides.shape),
        compiler_params=params(collective_id=1, has_side_effects=True),
        name="exchange",
    )(chunks.reshape(blocks), lq, lk, sides)
    return list(out[:5]) + [out[5].reshape(n, rows, PAIR), out[6]]


def toeplitz(taps_row, rows):
    wide = jnp.broadcast_to(taps_row, (rows, 2 * PAIR))
    return pltpu.roll(wide, 0, 1, stride=1, stride_axis=0)


def keep_taps(taps_ref, into, heads):
    for h in range(heads):
        hi, lo = split(toeplitz(taps_ref[h : h + 1, :], PAIR))
        into[0, h] = hi
        into[1, h] = lo


def keep_window(win, left, middle, right, margin, span):
    for rows, part in (
        (slice(0, margin), left),
        (slice(margin, margin + span), middle),
        (slice(margin + span, 2 * margin + span), right),
    ):
        hi, lo = split(part)
        win[0, rows, :] = hi
        win[1, rows, :] = lo


def convolve(taps, win, p, block, window):
    lanes = slice(p * PAIR, (p + 1) * PAIR)
    rows = slice(block * PAIR, block * PAIR + window)
    v = (win[0, rows, lanes], win[1, rows, lanes])
    halves = []
    for h in (2 * p, 2 * p + 1):
        t = (taps[0, h, :, :window], taps[1, h, :, :window])
        halves.append(dots(t, v, 1, 0))
    return jnp.where(lane_low((PAIR, PAIR)), halves[0], halves[1])


def owned_by(g, per):
    return g // per, g % per


def mix_kernel(per, pairs, margin, held, k1_ref, v_ref, use_ref, left_ref, right_ref, taps_ref, out_ref, taps, win):
    item = pl.program_id(0)
    span = v_ref.shape[1]
    window = PAIR + 2 * margin

    @pl.when(item == 0)
    def _():
        keep_taps(taps_ref, taps, 2 * pairs)

    keep_window(win, left_ref[0, 0], v_ref[0] * use_ref[0], right_ref[0, 0], margin, span)
    for p in range(pairs):
        lanes = slice(p * PAIR, (p + 1) * PAIR)
        slot, place = owned_by(item * pairs + p, per)
        mixed = held[slot, pl.ds(pl.multiple_of(place * MARKS, MARKS), MARKS), :]
        nystrom = dot3(k1_ref[0, lanes, :], spread(mixed), 0, 0)
        for block in range(span // PAIR):
            rows = slice(block * PAIR, (block + 1) * PAIR)
            out_ref[0, rows, lanes] = nystrom[rows] + convolve(taps, win, p, block, window)


def halo_specs(margin, width):
    return [
        pl.BlockSpec((1, 1, margin, width), lambda i, side=side: (side, i, 0, 0))
        for side in range(2)
    ]


def mix_call(blocks, k1, v, use_col, halos, taps, per, pairs, margin):
    items, span, width = v.shape
    return pl.pallas_call(
        functools.partial(mix_kernel, per, pairs, margin),
        out_shape=jax.ShapeDtypeStruct((items, span, width), f32),
        grid=(items,),
        in_specs=[whole(blocks.shape)]
        + [per_item((width, span)), per_item((span, width)), per_item((span, 1))]
        + halo_specs(margin, width)
        + [whole(taps.shape)],
        out_specs=per_item((span, width)),
        scratch_shapes=[
            VM((2, 2 * pairs, PAIR, 2 * PAIR), bf16),
            VM((2, span + 2 * margin, width), bf16),
        ],
        compiler_params=params(),
        name="mix",
    )(blocks, k1, v, use_col, halos, halos, taps)


def erf(x):
    x = jnp.clip(x, -3.832506856900711, 3.832506856900711)
    s = x * x
    a = 0.00022905065861350646
    for c in (0.0034082910107109506, 0.050955695062380861, 0.18520832239976145, 1.128379143519084):
        a = a * s + c
    b = -1.1791602954361697e-7
    for c in (
        0.000023547966471313185,
        0.0010179625278914885,
        0.014070470171167667,
        0.11098505178285362,
        0.49746925110067538,
        1.0,
    ):
        b = b * s + c
    return x * a / b


def normalize(x):
    center = x - jnp.mean(x, axis=-1, keepdims=True)
    inv_root = lax.rsqrt(jnp.mean(center * center, axis=-1, keepdims=True) + epsilon)
    return center * inv_root, inv_root


def norm_back(grad, scaled, inv_root):
    first = jnp.mean(grad, axis=-1, keepdims=True)
    second = jnp.mean(grad * scaled, axis=-1, keepdims=True)
    return inv_root * (grad - first - scaled * second)


def rows_kernel(
    x_ref, tok_ref, cot_ref, vec_ref, bup_ref, wo_ref, wu_ref, wd_ref,
    out_ref, act_ref, u_ref, r2t_ref, h1t_ref, r1t_ref, r1_ref, og_ref, sums_ref, bsum_ref,
    slope, wo_h, wo_l, wu_h, wu_l, wd_h, wd_l, staged, sems,
):
    step = pl.program_id(0)
    width = tok_ref.shape[1]
    ff = wu_ref.shape[1]
    tiles = [slice(c, c + width) for c in range(0, ff, width)]

    @pl.when(step == 0)
    def _():
        sums_ref[...] = jnp.zeros_like(sums_ref)
        bsum_ref[...] = jnp.zeros_like(bsum_ref)
        jobs = [(wo_ref, slice(None), slice(None), wo_h, wo_l)]
        jobs += [(wu_ref, slice(None), c, wu_h, wu_l) for c in tiles]
        jobs += [(wd_ref, c, slice(None), wd_h, wd_l) for c in tiles]
        depth, pieces = sems.shape
        size = width // pieces

        def load(i):
            w, r, c, _, _ = jobs[i]
            start = r.start or 0
            return [
                pltpu.make_async_copy(
                    w.at[pl.ds(start + k * size, size), c],
                    staged.at[i % depth, pl.ds(k * size, size)],
                    sems.at[i % depth, k],
                )
                for k in range(pieces)
            ]

        loads = [load(i) for i in range(len(jobs))]
        for copies in loads[:depth]:
            for copy in copies:
                copy.start()
        for i, (_, r, c, hi_ref, lo_ref) in enumerate(jobs):
            for copy in loads[i]:
                copy.wait()
            base = r.start or 0

            def lap(k, _, i=i, c=c, base=base, hi_ref=hi_ref, lo_ref=lo_ref):
                start = pl.multiple_of(k * 64, 64)
                hi, lo = split(staged[i % depth, pl.ds(start, 64), :])
                hi_ref[pl.ds(base + start, 64), c] = hi
                lo_ref[pl.ds(base + start, 64), c] = lo
                return 0

            lax.fori_loop(0, width // 64, lap, 0)
            if i + depth < len(jobs):
                for copy in loads[i + depth]:
                    copy.start()

    b_out, gain_one, shift_one = vec_ref[0:1, :], vec_ref[1:2, :], vec_ref[2:3, :]
    b_down, gain_two, shift_two = vec_ref[3:4, :], vec_ref[4:5, :], vec_ref[5:6, :]
    wo = (wo_h[...], wo_l[...])
    attention = dots(split(x_ref[...]), wo, 1, 0) + b_out
    scaled_one, root_one = normalize(tok_ref[...] + attention)
    hidden = scaled_one * gain_one + shift_one
    h1t_ref[0] = jnp.transpose(hidden)
    hs = split(hidden)
    down = b_down
    for i, c in enumerate(tiles):
        pre = dots(hs, (wu_h[:, c], wu_l[:, c]), 1, 0) + bup_ref[:, c]
        phi = 0.5 + 0.5 * erf(pre * 0.7071067811865476)
        slope[:, c] = phi + pre * (0.3989422804014327 * jnp.exp(-0.5 * pre * pre))
        act = pre * phi
        act_ref[i] = act
        act = split(act)
        down = down + dots(act, (wd_h[c, :], wd_l[c, :]), 1, 0)
    scaled_two, root_two = normalize(hidden + down)
    out_ref[...] = scaled_two * gain_two + shift_two
    cot = cot_ref[...]
    r2 = norm_back(cot * gain_two, scaled_two, root_two)
    r2t_ref[0] = jnp.transpose(r2)
    rs = split(r2)
    grad_hidden = r2
    for i, c in enumerate(tiles):
        u = dots(rs, (wd_h[c, :], wd_l[c, :]), 1, 1) * slope[:, c]
        halves = split(u)
        u_ref[i] = u
        bsum_ref[:, c] += jnp.sum(u, axis=0, keepdims=True)
        grad_hidden = grad_hidden + dots(halves, (wu_h[:, c], wu_l[:, c]), 1, 1)
    r1 = norm_back(grad_hidden * gain_one, scaled_one, root_one)
    r1_ref[...] = r1
    r1t_ref[0] = jnp.transpose(r1)
    og_ref[...] = dots(split(r1), wo, 1, 1)
    for row, value in enumerate(
        (cot * scaled_two, cot, r2, grad_hidden * scaled_one, grad_hidden, r1)
    ):
        sums_ref[row : row + 1, :] += jnp.sum(value, axis=0, keepdims=True)


def rows_call(x, tokens, cotangent, w_out, w_up, w_down, vectors, b_up):
    rows, width = tokens.shape
    ff = w_up.shape[1]
    tile = 256
    count = ff // width
    wide = pl.BlockSpec((tile, width), lambda i: (i, 0))
    any_space = pl.BlockSpec(memory_space=pl.ANY)

    def fixed(shape):
        return pl.BlockSpec(shape, lambda i: (0, 0))

    narrow = jax.ShapeDtypeStruct((rows, width), f32)
    broad = jax.ShapeDtypeStruct((count, rows, width), f32)
    tall = jax.ShapeDtypeStruct((rows // tile, width, tile), f32)
    return pl.pallas_call(
        rows_kernel,
        out_shape=[narrow]
        + [broad] * 2
        + [tall] * 3
        + [narrow, narrow, jax.ShapeDtypeStruct((8, width), f32), jax.ShapeDtypeStruct((1, ff), f32)],
        grid=(rows // tile,),
        in_specs=[wide] * 3 + [fixed(vectors.shape), fixed(b_up.shape)] + [any_space] * 3,
        out_specs=[wide]
        + [pl.BlockSpec((count, tile, width), lambda i: (0, i, 0))] * 2
        + [pl.BlockSpec((1, width, tile), lambda i: (i, 0, 0))] * 3
        + [wide, wide, fixed((8, width)), fixed((1, ff))],
        scratch_shapes=[VM((tile, ff), f32)]
        + [VM((width, width), bf16)] * 2
        + [VM((width, ff), bf16)] * 2
        + [VM((ff, width), bf16)] * 2
        + [VM((2, width, width), f32), pltpu.SemaphoreType.DMA((2, 6))],
        compiler_params=params(),
        name="rows",
    )(x, tokens, cotangent, vectors, b_up, w_out, w_up, w_down)


def one_back_kernel(per, pairs, held, k1_ref, og_ref, q_ref, lk_ref, gq_ref, chunk):
    item = pl.program_id(0)

    @pl.when(item == 0)
    def _():
        chunk[...] = jnp.zeros_like(chunk)

    for p in range(pairs):
        lanes = slice(p * PAIR, (p + 1) * PAIR)
        owner, place = owned_by(item * pairs + p, per)
        mixed = spread(held[owner, pl.ds(pl.multiple_of(place * MARKS, MARKS), MARKS), :])
        k1 = k1_ref[0, lanes, :]
        og = split(og_ref[0, :, lanes])
        part_mixed = compacted(dots(split(k1), og, 1, 0))
        grad = dots(split(mixed), og, 1, 1)
        scores = k1 * (grad - block_sum(k1 * grad))
        ss = split(scores)
        gq_ref[0, :, lanes] = dots(ss, split(spread(lk_ref[0, :, lanes])), 0, 0)
        part_key = compacted(dots(ss, split(q_ref[0, :, lanes]), 1, 0))
        chunk[owner, pl.ds(pl.multiple_of(place * 2 * MARKS, 2 * MARKS), MARKS), :] = part_mixed
        chunk[owner, pl.ds(pl.multiple_of(place * 2 * MARKS + MARKS, MARKS), MARKS), :] = part_key


def one_back_call(blocks, k1, og, q, lk, per, pairs):
    items, span, width = q.shape
    out = (blocks.shape[0], 2 * per * MARKS, PAIR)
    wide = per_item((span, width))
    return pl.pallas_call(
        functools.partial(one_back_kernel, per, pairs),
        out_shape=[
            jax.ShapeDtypeStruct((items, span, width), f32),
            jax.ShapeDtypeStruct(out, f32),
        ],
        grid=(items,),
        in_specs=[whole(blocks.shape), per_item((width, span)), wide, wide]
        + [per_item((MARKS, width))],
        out_specs=[wide, whole(out)],
        compiler_params=params(),
        name="one_back",
    )(blocks, k1, og, q, lk)


class ConvBack:
    def __init__(self, pairs, margin, og, ghalo, v, vhalo, use, taps_ref, gv, gtaps, scratch):
        self.pairs, self.margin, self.ghalo, self.vhalo = pairs, margin, ghalo, vhalo
        self.og, self.v, self.use, self.gv, self.gtaps = og, v, use, gv, gtaps
        self.taps_ref = taps_ref
        self.taps, self.gwin, self.vwin, self.acc = scratch
        self.span = v.shape[1]
        self.window = PAIR + 2 * margin

    def begin(self):
        keep_taps(self.taps_ref, self.taps, 2 * self.pairs)
        self.acc[...] = jnp.zeros_like(self.acc)

    def item(self, item):
        margin, window, gwin, vwin = self.margin, self.window, self.gwin, self.vwin
        use = self.use[item]
        keep_window(gwin, self.ghalo[0, item], self.og[item], self.ghalo[1, item], margin, self.span)
        values = self.v[item] * use
        keep_window(vwin, self.vhalo[0, item], values, self.vhalo[1, item], margin, self.span)
        for p in range(self.pairs):
            lanes = slice(p * PAIR, (p + 1) * PAIR)
            for block in range(self.span // PAIR):
                rows = slice(block * PAIR, (block + 1) * PAIR)
                self.gv[item, rows, lanes] = convolve(self.taps, gwin, p, block, window) * use[rows]
                inner = slice(margin + block * PAIR, margin + (block + 1) * PAIR)
                outer = slice(block * PAIR, block * PAIR + window)
                v = (vwin[0, outer, lanes], vwin[1, outer, lanes])
                low = lane_low((PAIR, PAIR))
                hi, lo = gwin[0, inner, lanes], gwin[1, inner, lanes]
                zero = jnp.zeros_like(hi)
                first = (jnp.where(low, hi, zero), jnp.where(low, lo, zero))
                second = (jnp.where(low, zero, hi), jnp.where(low, zero, lo))
                self.acc[2 * p] += dots(first, v, 1, 1)
                self.acc[2 * p + 1] += dots(second, v, 1, 1)

    def end(self):
        rows = lax.broadcasted_iota(jnp.int32, (PAIR, PAIR), 0)
        flip = (rows + lax.broadcasted_iota(jnp.int32, (PAIR, PAIR), 1) == PAIR - 1).astype(bf16)
        for h in range(2 * self.pairs):
            c = self.acc[h]
            c = jnp.concatenate([c, jnp.zeros((PAIR, 2 * PAIR - self.window), f32)], axis=1)
            hi = c.astype(bf16)
            rest = c - hi.astype(f32)
            mid = rest.astype(bf16)
            low = (rest - mid.astype(f32)).astype(bf16)
            c = dg(flip, hi, 1, 0) + dg(flip, mid, 1, 0) + dg(flip, low, 1, 0)
            c = pltpu.roll(c, 0, 1, stride=1, stride_axis=0)
            self.gtaps[h : h + 1, :] = jnp.sum(c, axis=0, keepdims=True)

    @staticmethod
    def scratch(pairs, margin, span, width):
        return [
            VM((2, 2 * pairs, PAIR, 2 * PAIR), bf16),
            VM((2, span + 2 * margin, width), bf16),
            VM((2, span + 2 * margin, width), bf16),
            VM((2 * pairs, PAIR, PAIR + 2 * margin), f32),
        ]


def exchange_back_kernel(n, per, fused, *refs):
    refs = list(refs)
    chunk_ref, side_ref, ctx_ref, a_ref, z_ref, lq_ref, lk_ref = refs[:7]
    r2_ref, act_ref = refs[7:9] if fused else [None] * 2
    refs = refs[9:] if fused else refs[7:]
    out_ref, gq_ref, gk_ref, halo_ref = refs[:4]
    part_ref = refs[4] if fused else None
    gm, gz, ga, *scratch = refs[5:] if fused else refs[4:]
    seat = Seat(n)
    reduce = Reduce(seat, chunk_ref, *scratch[:5])
    gather = Gather(seat, out_ref, *scratch[5:7])
    edges = Edges(seat, side_ref, *scratch[7:10])
    if fused:
        links = Links()
        whole_ref, send, recv = scratch[10:13]
        tiles = Tiles(links, True, r2_ref, act_ref, whole_ref, scratch[13:])
        scatter = Scatter(0, links, [whole_ref, part_ref], send, recv)
        seat.hello(True, links.devices[2:])
    else:
        seat.hello(True)
    reduce.start()
    edges.start()
    reduce.middle(add_all)
    if fused:
        tiles.compute(0)
        tiles.compute(1)
        tiles.absorb(0)
        tiles.compute(2)
        tiles.absorb(1)
    diagonal = diagonal_mask()
    eye = unit()
    stats = per * MARKS
    gm[...] = reduce.finish(add_all)
    block = out_ref.at[seat.core, seat.z]
    block[stats:, :] = jnp.zeros((block.shape[0] - stats, PAIR), f32)
    for place in range(per):
        mixed = spread(gm[place * 2 * MARKS : place * 2 * MARKS + MARKS, :])
        context = spread(ctx_ref[place])
        grad = dot3(jnp.transpose(z_ref[NEWTON, place]), mixed)
        block[place * MARKS : (place + 1) * MARKS, :] = compacted(grad)
        dot = jnp.sum(grad * context, axis=1, keepdims=True)
        block[stats + place : stats + place + 1, :] = row_of(dot)
        gz[place] = jnp.where(diagonal, dot3(mixed, context, 1, 1), 0.0)
        ga[place] = jnp.zeros((PAIR, PAIR), f32)
    gather.start()

    def lap(back, _):
        step = NEWTON - 1 - back
        for place in range(per):
            a, z, g = a_ref[place], z_ref[step, place], 0.25 * gz[place]
            pr, n1, n2, n3 = newton_step(a, z, eye)
            back_three = dot3(jnp.transpose(z), g)
            turned = jnp.transpose(pr)
            back_two = -dot3(turned, back_three)
            back_one = -dot3(turned, back_two)
            grad = -dot3(back_three, n2, 1, 1) - dot3(back_two, n1, 1, 1) - back_one
            ga[place] += dot3(grad, z, 1, 1)
            gz[place] = dot3(g, n3, 1, 1) + dot3(jnp.transpose(a), grad)
        return 0

    if fused:
        tiles.compute(3)
        tiles.absorb(2)
        tiles.absorb(3)
        scatter.start()
        gather.forward()
        lax.fori_loop(0, NEWTON, lap, 0)
    else:
        lax.fori_loop(0, NEWTON - 1, lap, 0)
        gather.forward()
        lax.fori_loop(NEWTON - 1, NEWTON, lap, 0)
    for place in range(per):
        a, g = a_ref[place], jnp.transpose(gz[place])
        norm = head_total(a * a)
        slope = -head_total(g * a) / (norm * norm)
        grad = ga[place] + g / norm + 2.0 * slope * a
        scores = a * (grad - jnp.sum(a * grad, axis=1, keepdims=True))
        gq_ref[place] = compacted(dot3(scores, spread(lk_ref[place])))
        gk_ref[place] = gm[place * 2 * MARKS + MARKS : (place + 1) * 2 * MARKS, :] + compacted(
            dot3(jnp.transpose(scores), spread(lq_ref[place]))
        )
    edges.finish(halo_ref)
    gather.finish()
    if fused:
        scatter.advance()


def exchange_back_call(chunks, sides, ctx, a, z, lq, lk, n, rows, r2=None, act=None):
    per = ctx.shape[0]
    small = jax.ShapeDtypeStruct(ctx.shape, f32)
    chunk = chunks.shape[1:]
    blocks = (2, n // 2, rows, PAIR)
    fused = r2 is not None
    more_in, more_shapes, more_scratch = (), [], []
    if fused:
        more_in = (r2, act)
        more_shapes = [jax.ShapeDtypeStruct(landing(BIG, 0), f32)]
        more_scratch = [VM(landing(BIG, -1), f32)] + [pltpu.SemaphoreType.DMA((12,))] * 2
        more_scratch += Tiles.scratch(*act.shape[1:])
    out = pl.pallas_call(
        functools.partial(exchange_back_kernel, n, per, fused),
        out_shape=[
            jax.ShapeDtypeStruct(blocks, f32),
            small,
            small,
            jax.ShapeDtypeStruct(sides.shape, f32),
        ]
        + more_shapes,
        in_specs=[pl.BlockSpec(memory_space=VM)] * 7
        + [pl.BlockSpec(memory_space=pl.ANY)] * len(more_in),
        out_specs=[pl.BlockSpec(memory_space=VM)] * (4 + len(more_shapes)),
        scratch_shapes=[VM(chunk, f32)]
        + [VM((per, PAIR, PAIR), f32)] * 2
        + Reduce.scratch(n, chunk)
        + Gather.scratch(n)
        + Edges.scratch(sides.shape)
        + more_scratch,
        compiler_params=params(collective_id=2, has_side_effects=True),
        name="exchange_back",
    )(chunks.reshape((2, n // 2) + chunk), sides, ctx, a, z, lq, lk, *more_in)
    return [out[0].reshape(n, rows, PAIR)] + list(out[1:])


def keep_both(value, lanes, out_ref, turned_ref):
    out_ref[0, :, lanes] = value
    turned_ref[0, lanes, :] = jnp.transpose(value)


def both_specs(items, span, width):
    shapes = [(items, span, width), (items, width, span)]
    shapes = [jax.ShapeDtypeStruct(shape, f32) for shape in shapes]
    return shapes, [per_item((span, width)), per_item((width, span))]


def three_back_kernel(per, pairs, held, stat, w3_ref, top_ref, v_ref, k_ref, lq_ref,
                      gk_ref, gv_ref, chunk):
    item = pl.program_id(0)
    stats = per * MARKS

    @pl.when(item == 0)
    def _():
        chunk[...] = jnp.zeros_like(chunk)

    for p in range(pairs):
        lanes = slice(p * PAIR, (p + 1) * PAIR)
        owner, place = owned_by(item * pairs + p, per)
        grad = split(spread(held[owner, pl.ds(pl.multiple_of(place * MARKS, MARKS), MARKS), :]))
        row_dot = column_of(held[owner, pl.ds(stats + place, 1), :])
        largest = stat[owner, pl.ds(stats + 2 * place, 1), :]
        total = stat[owner, pl.ds(stats + 2 * place + 1, 1), :]
        scale = column_of(jnp.exp(top_ref[0, p : p + 1, :] - largest) / total)
        k3 = w3_ref[0, lanes, :] * scale[:, 0:1]
        gk3 = dots(grad, split(v_ref[0, :, lanes]), 1, 1)
        scores = split(k3 * (gk3 - row_dot[:, 0:1]))
        gv_ref[0, :, lanes] = dots(split(k3), grad, 0, 0)
        gk_ref[0, :, lanes] = dots(scores, split(spread(lq_ref[0, :, lanes])), 0, 0)
        part = compacted(dots(scores, split(k_ref[0, :, lanes]), 1, 0))
        chunk[owner, pl.ds(pl.multiple_of(place * MARKS, MARKS), MARKS), :] = part


def three_back_call(grads, blocks, w3, top, v, k, lq, per, pairs):
    items, span, width = v.shape
    out = (blocks.shape[0], per * MARKS, PAIR)
    wide = per_item((span, width))
    shape = jax.ShapeDtypeStruct((items, span, width), f32)
    return pl.pallas_call(
        functools.partial(three_back_kernel, per, pairs),
        out_shape=[shape, shape, jax.ShapeDtypeStruct(out, f32)],
        grid=(items,),
        in_specs=[whole(blocks.shape)] * 2
        + [per_item((width, span)), per_item((8, PAIR)), wide, wide]
        + [per_item((MARKS, width))],
        out_specs=[wide, wide, whole(out)],
        compiler_params=params(),
        name="three_back",
    )(grads, blocks, w3, top, v, k, lq)


def land_exchange_kernel(n, per, pairs, margin, fused, *refs):
    refs = list(refs)
    chunk_ref, q_ref, k_ref = refs[:3]
    convolution, refs = refs[3:9], refs[9:]
    if fused:
        in_down, hid_ref, u_ref, out_ref, gv_ref, gtaps_ref, down_ref, part_ref, *scratch = refs
    else:
        out_ref, gv_ref, gtaps_ref, *scratch = refs
    conv = ConvBack(pairs, margin, *convolution, gv_ref, gtaps_ref, scratch[:4])
    scratch = scratch[4:]

    def conv_lap(item, _):
        conv.item(item)
        return 0

    seat = Seat(n)
    reduce = Reduce(seat, chunk_ref, *scratch[:5])
    gather = Gather(seat, out_ref, *scratch[5:7])
    if fused:
        links = Links()
        second, third, whole_ref, send, recv = scratch[7:12]
        down = Scatter(0, links, [in_down, second, third, down_ref], send, recv, 1)
        up = Scatter(1, links, [whole_ref, part_ref], send, recv)
        tiles = Tiles(links, False, hid_ref, u_ref, whole_ref, scratch[12:])
        seat.hello(False, links.devices[2:])
    else:
        seat.hello(False)
    reduce.start()
    reduce.middle(add_all)
    if fused:
        down.start()
        tiles.compute(0)
    half = per * MARKS
    block = out_ref.at[seat.core, seat.z]
    block[half:, :] = k_ref[...]
    block[:half, :] = q_ref[...] + reduce.finish(add_all)
    gather.start()
    if fused:
        tiles.compute(1)
        tiles.absorb(0)
        down.advance()
        tiles.compute(2)
        tiles.absorb(1)
        tiles.compute(3)
        tiles.absorb(2)
        down.advance()
    conv.begin()
    items = gv_ref.shape[0]
    if fused:
        tiles.absorb(3)
        up.start()
    lax.fori_loop(0, items // 2, conv_lap, 0)
    gather.forward()
    lax.fori_loop(items // 2, items, conv_lap, 0)
    conv.end()
    gather.finish()
    if fused:
        down.advance()
        up.advance()


def land_exchange_call(chunks, own_q, own_k, convolution, n, pairs, margin, in_down=None, hidden=None, u=None):
    per = own_q.shape[0]
    half = per * MARKS
    blocks = (2, n // 2, 2 * half, PAIR)
    fused = in_down is not None
    conv_shapes = [convolution[0].shape, (-(-2 * pairs // 8) * 8, 2 * PAIR)]
    vmem = pl.BlockSpec(memory_space=VM)
    more_in, more_specs, more_shapes, more_scratch = (), [], [], []
    if fused:
        more_in = (in_down, hidden, u)
        more_specs = [vmem] + [pl.BlockSpec(memory_space=pl.ANY)] * 2
        more_shapes = [landing(BIG, 3), landing(BIG, 0)]
        more_scratch = [VM(landing(BIG, stage), f32) for stage in (1, 2, -1)]
        more_scratch += [pltpu.SemaphoreType.DMA((24,))] * 2
        more_scratch += Tiles.scratch(*u.shape[1:])
    out = pl.pallas_call(
        functools.partial(land_exchange_kernel, n, per, pairs, margin, fused),
        out_shape=[jax.ShapeDtypeStruct(shape, f32) for shape in [blocks, *conv_shapes] + more_shapes],
        in_specs=[vmem] * 9 + more_specs,
        out_specs=[vmem] * (3 + len(more_shapes)),
        scratch_shapes=ConvBack.scratch(pairs, margin, *convolution[0].shape[1:])
        + Reduce.scratch(n, (half, PAIR)) + Gather.scratch(n) + more_scratch,
        compiler_params=params(collective_id=3, has_side_effects=True),
        name="land_exchange",
    )(
        chunks.reshape(2, n // 2, half, PAIR),
        own_q.reshape(half, PAIR),
        own_k.reshape(half, PAIR),
        *convolution,
        *more_in,
    )
    return [out[0].reshape(n, 2 * half, PAIR)] + list(out[1:])


def land_back_kernel(per, pairs, factor, held, gq_ref, gk_ref, gv_ref, gvc_ref, mem_ref, inv_ref, *outs):
    sums_ref = outs[6]
    item = pl.program_id(0)
    half = per * MARKS

    @pl.when(item == 0)
    def _():
        sums_ref[...] = jnp.zeros_like(sums_ref)

    member = mem_ref[0].astype(bf16)
    inv = inv_ref[0]
    for p in range(pairs):
        lanes = slice(p * PAIR, (p + 1) * PAIR)
        slot, place = owned_by(item * pairs + p, per)
        for ref, out, base in ((gq_ref, outs[:2], 0), (gk_ref, outs[2:4], half)):
            grad = held[slot, pl.ds(pl.multiple_of(base + place * MARKS, MARKS), MARKS), :]
            hi, lo = split(grad * inv)
            landed = dg(member, hi, 0, 0) + dg(member, lo, 0, 0)
            total = (ref[0, :, lanes] + landed) * factor
            keep_both(total, lanes, *out)
            if base == 0:
                sums_ref[0:1, lanes] += jnp.sum(total, axis=0, keepdims=True)
        total = gv_ref[0, :, lanes] + gvc_ref[0, :, lanes]
        keep_both(total, lanes, *outs[4:6])
        sums_ref[1:2, lanes] += jnp.sum(total, axis=0, keepdims=True)


def land_back_call(blocks, gq, gk, gv, gv_conv, member_t, inv, per, pairs, factor):
    items, span, width = gq.shape
    wide = per_item((span, width))
    shapes, specs = both_specs(items, span, width)
    out = pl.pallas_call(
        functools.partial(land_back_kernel, per, pairs, factor),
        out_shape=shapes * 3 + [jax.ShapeDtypeStruct((8, width), f32)],
        grid=(items,),
        in_specs=[whole(blocks.shape)] + [wide] * 4
        + [per_item((MARKS, span)), per_item((MARKS, PAIR))],
        out_specs=specs * 3 + [whole((8, width))],
        compiler_params=params(),
        name="land_back",
    )(blocks, gq, gk, gv, gv_conv, member_t, inv)
    return out[:2], out[2:4], out[4:6], out[6]


def grads_kernel(
    r1t_ref, x_ref, gqt_ref, gkt_ref, gvt_ref, tok_ref, gq_ref, gk_ref, gv_ref, wq_ref, wk_ref, wv_ref, r1_ref,
    in_up, sums_ref, late_ref, bsum_ref, taps_ref,
    vo_ref, up_ref, qk_ref, gt_ref, total_ref,
    s_slots, s_first, s_second, t_slots, w_s, p_pair, *scratch
):
    vo_bufs, qk_bufs, up_bufs = list(scratch[:4]), list(scratch[4:8]), list(scratch[8:10])
    held, caught, load_sem, s_sem, t_sem, core_send, core_recv, send, recv, sum_send, sum_recv = scratch[10:]
    links = Links()
    width = tok_ref.shape[1]
    ff = bsum_ref.shape[1]
    s_loads = Loads([gvt_ref, r1t_ref, gqt_ref, gkt_ref], s_slots, s_sem)
    t_loads = Loads(
        [tok_ref, x_ref, gv_ref, wv_ref, gq_ref, wq_ref, gk_ref, wk_ref], t_slots, t_sem
    )
    residual = pltpu.make_async_copy(r1_ref, gt_ref, load_sem.at[0])
    residual.start()
    barrier = pltpu.get_barrier_semaphore()
    for device in (links.partner, *links.devices):
        pl.semaphore_signal(barrier, inc=1, device_id=device, device_id_type=MESH)
    pl.semaphore_wait(barrier, 5)
    up = Scatter(0, links, [in_up, *up_bufs, up_ref], send, recv, 1, EVEN)
    vo = Scatter(1, links, [*vo_bufs, vo_ref], send, recv, orders=EVEN)
    qk = Scatter(2, links, [*qk_bufs, qk_ref], send, recv, orders=EVEN)
    up.start()

    def halfway(step):
        return pltpu.make_async_remote_copy(
            src_ref=held.at[step], dst_ref=caught.at[step],
            send_sem=sum_send.at[step], recv_sem=sum_recv.at[step],
            device_id=(links.partner, *links.devices)[step], device_id_type=MESH,
        )

    held[0] = jnp.zeros(held.shape[1:], f32)
    held[0, 0:8, :] = sums_ref[...]
    held[0, 8:16, :] = late_ref[...]
    for i, t in enumerate(range(0, ff, width)):
        held[0, 16 + i : 17 + i, :] = bsum_ref[:, t : t + width]
    held[0, 24:40, : 2 * PAIR] = taps_ref[...]
    halfway(0).start()

    def sums_on(step):
        halfway(step).wait()
        added = held[step] + caught[step]
        if step < 4:
            held[step + 1] = added
            halfway(step + 1).start()
        else:
            total_ref[...] = added

    def pair_job(first, second, t_first, t_second):
        half = PAIR // 2
        for which, (s, t) in enumerate(((first, t_first), (second, t_second))):
            for third in range(3):
                g = times(s, t, slice(third * 256, (third + 1) * 256))
                for unit in range(4):
                    block, k = divmod(4 * third + unit, 3)
                    color, side = divmod(3 * which + k, 2)
                    lanes = slice(side * half, (side + 1) * half)
                    for j in range(8):
                        at = (links.apart[j % 2], color, j // 4, j // 2 % 2, block // 2, block % 2)
                        p_pair[(*at, slice(None), lanes)] = g[
                            j * 96 : (j + 1) * 96, unit * half : (unit + 1) * half
                        ]

    def absorb(copy, buffer):
        copy.wait()
        buffer[...] = buffer[...] + p_pair[0]

    def token_job(i):
        x, w = t_loads.get(2 + 2 * i), t_loads.get(3 + 2 * i)
        halved(w, w_s)

        def lap(c, _):
            rows = pl.ds(pl.multiple_of(c * 256, 256), 256)
            gt_ref[rows, :] += dots(split(x[rows, :]), (w_s[0], w_s[1]), 1, 1)
            return 0

        lax.fori_loop(0, gt_ref.shape[0] // 256, lap, 0)
        t_loads.release(2 + 2 * i)
        t_loads.release(3 + 2 * i)

    tokens = t_loads.get(0)
    halved(s_loads.get(0), s_first)
    s_loads.release(0)
    halved(s_loads.get(1), s_second)
    s_loads.release(1)
    pair_job(s_first, s_second, tokens, t_loads.get(1))
    t_loads.release(1)
    vo_copy = links.copy(0, p_pair.at[1], vo_bufs[0], core_send, core_recv)
    vo_copy.start()
    sums_on(0)
    up.advance()
    residual.wait()
    token_job(0)
    absorb(vo_copy, vo_bufs[0])
    vo.start()
    halved(s_loads.get(2), s_first)
    halved(s_loads.get(3), s_second)
    pair_job(s_first, s_second, tokens, tokens)
    t_loads.release(0)
    qk_copy = links.copy(1, p_pair.at[1], qk_bufs[0], core_send, core_recv)
    qk_copy.start()
    vo.advance()
    up.advance()
    sums_on(1)
    token_job(1)
    absorb(qk_copy, qk_bufs[0])
    qk.start()
    vo.advance()
    sums_on(2)
    token_job(2)
    up.advance()
    qk.advance()
    vo.advance()
    sums_on(3)
    qk.advance()
    sums_on(4)
    vo.advance()
    qk.advance()
    qk.advance()


def grads_call(arrays, r1, in_up, sums):
    rows, width = r1.shape
    any_space = pl.BlockSpec(memory_space=pl.ANY)
    vmem = pl.BlockSpec(memory_space=VM)
    dma = pltpu.SemaphoreType.DMA
    out_shapes = [
        landing(SMALL, 3), landing(BIG, 3), landing(SMALL, 3), (rows, width), (40, width),
    ]
    return pl.pallas_call(
        grads_kernel,
        out_shape=[jax.ShapeDtypeStruct(shape, f32) for shape in out_shapes],
        in_specs=[any_space] * (len(arrays) + 1) + [vmem] * (1 + len(sums)),
        out_specs=[vmem] * 5,
        scratch_shapes=[
            VM((2, width, rows), f32),
            VM((2, width, rows), bf16),
            VM((2, width, rows), bf16),
            VM((4, rows, width), f32),
            VM((2, width, width), bf16),
            VM((2, 3, 2, 2, 2, 2) + SMALL, f32),
        ]
        + [VM(landing(SMALL, stage), f32) for stage in (-1, 0, 1, 2)] * 2
        + [VM(landing(BIG, stage), f32) for stage in (1, 2)]
        + [VM((5, 40, width), f32)] * 2
        + [dma((1,)), dma((2, 4)), dma((4, 1)), dma((2,)), dma((2,))]
        + [dma((36,)), dma((36,)), dma((5,)), dma((5,))],
        compiler_params=params(collective_id=4, has_side_effects=True),
        name="grads",
    )(*arrays, r1, in_up, *sums)


def swap(x, axis, offset):
    count = lax.axis_size(axis)
    return lax.ppermute(x, axis, [(i, i ^ offset) for i in range(count)])


def both_sides(x, margin):
    return jnp.stack([x[:, :margin], x[:, -margin:]])


def bit_of(axis, bit):
    return lax.axis_index(axis) // bit % 2


def halve_rows(x, bit):
    blocks, rows, columns = x.shape
    y = x.reshape(blocks // 2, 2, rows, columns)
    mine = bit_of("seq", bit)
    keep = lax.dynamic_index_in_dim(y, mine, 1, False)
    send = lax.dynamic_index_in_dim(y, 1 - mine, 1, False)
    return keep + swap(send, "seq", bit)


def halve_columns(x, bits, bit):
    mine = bit_of("dp", bit)
    columns = x.shape[2]
    groups = 2 ** bits.index(bit)
    size = columns // (2 * groups)

    def pick(which):
        parts = [
            lax.dynamic_slice_in_dim(x, 2 * g * size + which * size, size, 2)
            for g in range(groups)
        ]
        return parts[0] if groups == 1 else jnp.concatenate(parts, axis=2)

    return pick(mine) + swap(pick(1 - mine), "dp", bit)


def powers(axis):
    count = lax.axis_size(axis)
    return [2**i for i in range(count.bit_length() - 1)]


def scatter_sum(x, order):
    seq_bits, dp_bits = powers("seq"), powers("dp")[::-1]
    count = lax.axis_size("seq")
    x = x.reshape(count, x.shape[0] // count, x.shape[1])
    x = halve_rows(x, seq_bits.pop(0))
    for axis in order:
        if axis == "z" and seq_bits:
            x = halve_rows(x, seq_bits.pop(0))
        elif axis in "xy" and dp_bits:
            half = len(powers("dp")) // 2
            low = [b for b in dp_bits if b < 2**half]
            high = [b for b in dp_bits if b >= 2**half]
            chosen = (low if axis == "x" else high) or dp_bits
            x = halve_columns(x, dp_bits, chosen[0])
            dp_bits.remove(chosen[0])
    while seq_bits:
        x = halve_rows(x, seq_bits.pop(0))
    while dp_bits:
        x = halve_columns(x, dp_bits, dp_bits[0])
        dp_bits.pop(0)
    return x[0]


def sum_everywhere(x):
    for axis in ("seq", "dp"):
        for bit in powers(axis):
            x = x + swap(x, axis, bit)
    return x


def product(a, b, ca, cb):
    return lax.dot_general(a, b, (((ca,), (cb,)), ((), ())), precision=HIGH)


def on_device(
    tokens,
    lengths,
    keep,
    w_query,
    b_query,
    w_key,
    w_value,
    b_value,
    conv_weight,
    w_out,
    b_out,
    gain_one,
    shift_one,
    w_up,
    b_up,
    w_down,
    b_down,
    gain_two,
    shift_two,
    cotangent,
):
    items, span, width = tokens.shape
    heads, taps = conv_weight.shape
    head_size = width // heads
    margin = taps // 2
    factor = head_size ** (-0.25)
    pairs = heads // 2
    n = lax.axis_size("seq")
    per = -(-items * pairs // n)
    chunk_rows = per * MARKS + 8
    position = lax.axis_index("seq") * span + jnp.arange(span, dtype=jnp.int32)
    inside = position[None, :] < lengths[:, None]
    usable = (inside & (keep > 0)).astype(f32)
    use_row, use_col = usable[:, None, :], usable[:, :, None]
    segment = jnp.where(inside, position[None, :] * MARKS // lengths[:, None], MARKS)
    marks = jnp.arange(MARKS, dtype=jnp.int32)
    member_t = (segment[:, None, :] == marks[None, :, None]).astype(f32) * use_row
    rows = tokens.reshape(items * span, width)
    taps_forward = jnp.pad(conv_weight, ((0, 4), (0, 2 * PAIR - taps)))
    taps_backward = jnp.pad(conv_weight[:, ::-1], ((0, 4), (0, 2 * PAIR - taps)))

    queries, key_rows, values, land_q, land_k, inverse_divisor = project_call(
        tokens, member_t, w_query, w_key, w_value, jnp.stack([b_query, b_value]), n, factor
    )
    k1, w3, top, chunks = scores_call(
        queries, key_rows, values, land_q, land_k, use_row, n, per, pairs, chunk_rows
    )
    use_sides = both_sides(use_col, margin)
    kernel_two, z, owned_q, owned_k, context, mixed, vhalos = exchange_call(
        chunks, land_q, land_k, both_sides(values, margin) * use_sides, n, per, pairs
    )
    x = mix_call(mixed, k1, values, use_col, vhalos, taps_forward, per, pairs, margin)

    def flat(array):
        return array.reshape(items * span, width)

    x = flat(x)
    vectors = jnp.stack([b_out, gain_one, shift_one, b_down, gain_two, shift_two])
    output, act, u, r2_t, hidden_t, r1_t, r1, og, row_sums, up_sums = rows_call(
        x, rows, cotangent.reshape(items * span, width), w_out, w_up, w_down, vectors, b_up[None, :]
    )
    og = og.reshape(items, span, width)
    grad_queries, chunks = one_back_call(mixed, k1, og, queries, land_k, per, pairs)
    ff = w_up.shape[1]
    fused = (n, lax.axis_size("dp"), width, ff) == (8, 4, 768, 3072)
    grad_context, own_q, own_k, ghalos, *down_part = exchange_back_call(
        chunks, both_sides(og, margin), context, kernel_two, z, owned_q, owned_k, n, chunk_rows,
        *((r2_t, act) if fused else ()),
    )
    grad_keys, grad_values, chunks = three_back_call(
        grad_context, mixed, w3, top, values, key_rows, land_q, per, pairs
    )
    land_grads, gv_conv, grad_taps, *ff_grads = land_exchange_call(
        chunks, own_q, own_k, (og, ghalos, values, vhalos, use_col, taps_backward), n, pairs, margin,
        *((*down_part, hidden_t, u) if fused else ()),
    )
    gq, gk, gv, late_sums = land_back_call(
        land_grads, grad_queries, grad_keys, grad_values, gv_conv,
        member_t, inverse_divisor, per, pairs, factor,
    )
    if fused:
        down, up_part = ff_grads
        vo, up, qk, grad_tokens, totals = grads_call(
            [r1_t, x, gq[1], gk[1], gv[1], rows, flat(gq[0]), flat(gk[0]), flat(gv[0])]
            + [w_query, w_key, w_value],
            r1,
            up_part,
            [row_sums, late_sums, up_sums, grad_taps],
        )
        vo, qk = (jnp.transpose(both, (0, 2, 1)).reshape(2, -1, both.shape[1]) for both in (vo, qk))
        grad_w_value, grad_w_out = vo[0], vo[1]
        grad_w_query, grad_w_key = qk[0], qk[1]
        down = down.reshape(3, 2, -1, PAIR)
        grad_w_down = jnp.transpose(down, (0, 1, 3, 2)).reshape(-1, down.shape[2])
        grad_w_up = jnp.transpose(up, (1, 0, 2)).reshape(up.shape[1], -1)
    else:
        def unturned(array):
            return flat(jnp.swapaxes(array, 1, 2))

        def untiled(array):
            return jnp.swapaxes(array, 0, 1).reshape(items * span, ff)

        gq, gk, gv = (flat(pair[0]) for pair in (gq, gk, gv))
        grad_w_down = scatter_sum(product(unturned(r2_t), untiled(act), 0, 0), "yxzz").T
        grad_w_up = scatter_sum(product(untiled(u), unturned(hidden_t), 0, 0), "xzyz").T
        grad_w_out = scatter_sum(product(r1, x, 0, 0), "zyxz").T
        grad_w_value = scatter_sum(product(gv, rows, 0, 0), "zyxz").T
        grad_w_query = scatter_sum(product(gq, rows, 0, 0), "yxzz").T
        grad_w_key = scatter_sum(product(gk, rows, 0, 0), "xzyz").T
        grad_tokens = (
            r1
            + product(gv, w_value, 1, 1)
            + product(gq, w_query, 1, 1)
            + product(gk, w_key, 1, 1)
        )
        taps_rows = jnp.pad(grad_taps, ((0, 0), (0, width - grad_taps.shape[1])))
        up_rows = jnp.pad(up_sums.reshape(-1, width), ((0, 8 - ff // width), (0, 0)))
        totals = sum_everywhere(jnp.concatenate([row_sums, late_sums, up_rows, taps_rows]))
    row_sums, late = totals[:8], totals[8:16]
    up_sums = totals[16 : 16 + ff // width].reshape(ff)
    grad_conv = totals[24 : 24 + heads, PAIR - 1 : PAIR - 1 + taps]
    return (
        output.reshape(tokens.shape),
        grad_tokens.reshape(tokens.shape),
        grad_w_query,
        late[0],
        grad_w_key,
        grad_w_value,
        late[1],
        grad_conv,
        grad_w_out,
        row_sums[5],
        row_sums[3],
        row_sums[4],
        grad_w_up,
        up_sums,
        grad_w_down,
        row_sums[2],
        row_sums[0],
        row_sums[1],
    )


def solution(mesh):
    rows = P("dp", "seq", None)
    block = P("dp", "seq")
    in_specs = (rows, P("dp"), block) + (P(),) * 16 + (rows,)
    out_specs = (
        rows, rows, block, P(), block, block, P(), P(), block,
        P(), P(), P(), block, P(), block, P(), P(), P(),
    )
    return jax.shard_map(
        on_device, mesh=mesh, in_specs=in_specs, out_specs=out_specs, check_vma=False
    )
```

```python
import functools

import jax
import jax.numpy as jnp
from jax import lax
from jax.experimental import pallas as pl
from jax.experimental.pallas import tpu as pltpu
from jax.sharding import PartitionSpec as P

MARKS = 64
NEWTON = 6
PAIR = 128
HIGH = lax.Precision.HIGH
epsilon = 1e-05
f32 = jnp.float32
bf16 = jnp.bfloat16
VM = pltpu.VMEM
LIMIT = 66 * 1024 * 1024


def split(x):
    hi = x.astype(bf16)
    return hi, (x - hi.astype(f32)).astype(bf16)


def dg(a, b, ca, cb):
    return lax.dot_general(a, b, (((ca,), (cb,)), ((), ())), preferred_element_type=f32)


def dots(a, b, ca, cb):
    return dg(a[0], b[0], ca, cb) + dg(a[0], b[1], ca, cb) + dg(a[1], b[0], ca, cb)


def dot3(a, b, ca=1, cb=0):
    return dots(split(a), split(b), ca, cb)


def lane_low(shape):
    return lax.broadcasted_iota(jnp.int32, shape, len(shape) - 1) < PAIR // 2


def spread(compact):
    low = lane_low(compact.shape)
    zero = jnp.zeros_like(compact)
    return jnp.concatenate([jnp.where(low, compact, zero), jnp.where(low, zero, compact)], axis=0)


def compacted(block):
    half = block.shape[0] // 2
    return jnp.where(lane_low((half, block.shape[1])), block[:half], block[half:])


def row_of(column):
    return jnp.transpose(jnp.broadcast_to(column, (PAIR, PAIR)))[0:1, :]


def column_of(row):
    return jnp.transpose(jnp.broadcast_to(row, (PAIR, PAIR)))


def diagonal_mask():
    rows = lax.broadcasted_iota(jnp.int32, (PAIR, PAIR), 0) < PAIR // 2
    return rows == lane_low((PAIR, PAIR))


def block_sum(x):
    halves = x.reshape(2, x.shape[0] // 2, x.shape[1])
    total = jnp.sum(halves, axis=1, keepdims=True)
    return jnp.broadcast_to(total, halves.shape).reshape(x.shape)


def block_max(x):
    halves = x.reshape(2, x.shape[0] // 2, x.shape[1])
    total = jnp.max(halves, axis=1, keepdims=True)
    return jnp.broadcast_to(total, halves.shape).reshape(x.shape)


def params(**more):
    return pltpu.CompilerParams(vmem_limit_bytes=LIMIT, **more)


def whole(shape):
    return pl.BlockSpec(shape, lambda *_: (0,) * len(shape))


def per_item(shape):
    return pl.BlockSpec((1,) + shape, lambda i, *_: (i,) + (0,) * len(shape))


class Seat:
    def __init__(self, n):
        self.n, self.nz = n, n // 2
        self.me = lax.axis_index("seq")
        self.core = lax.rem(self.me, 2)
        self.z = self.me // 2
        self.owner = self.core * self.nz + self.z
        self.partner = self.me + 1 - 2 * self.core
        self.extra = lax.rem(self.me + 2 * self.core - 1 + n, n)

    def ahead(self, j):
        return lax.rem(self.z + j, self.nz)

    def behind(self, j):
        return lax.rem(self.z - j + self.nz, self.nz)

    def at(self, z):
        return 2 * z + self.core

    def hello(self, edges, more=()):
        others = [self.partner] + [self.at(self.ahead(j)) for j in range(1, self.nz)]
        if edges:
            others.append(self.extra)
        others = [{"seq": other} for other in others] + list(more)
        barrier = pltpu.get_barrier_semaphore()
        for other in others:
            pl.semaphore_signal(barrier, inc=1, device_id=other, device_id_type=MESH)
        pl.semaphore_wait(barrier, len(others))


MESH = pl.DeviceIdType.MESH


def remote(src, dst, send, recv, device):
    return pltpu.make_async_remote_copy(
        src_ref=src, dst_ref=dst, send_sem=send, recv_sem=recv,
        device_id={"seq": device}, device_id_type=MESH,
    )


class Reduce:
    def __init__(self, seat, chunks, first, acc, second, send, recv):
        self.seat, self.chunks, self.first, self.acc, self.second = seat, chunks, first, acc, second
        self.send, self.recv = send, recv
        self.across = remote(chunks.at[1 - seat.core], first, send.at[0], recv.at[0], seat.partner)
        self.along = [
            remote(
                acc.at[seat.ahead(j)], second.at[j - 1], send.at[j], recv.at[j],
                seat.at(seat.ahead(j)),
            )
            for j in range(1, seat.nz)
        ]

    def start(self):
        self.across.start()

    def middle(self, merge):
        self.across.wait()
        for z in range(self.seat.nz):
            self.acc[z] = merge([self.chunks.at[self.seat.core, z], self.first.at[z]])
        for copy in self.along:
            copy.start()

    def finish(self, merge):
        for copy in self.along:
            copy.wait()
        refs = [self.acc.at[self.seat.z]] + [self.second.at[j] for j in range(self.seat.nz - 1)]
        return merge(refs)

    @staticmethod
    def scratch(n, shape):
        nz = n // 2
        return [
            VM((nz,) + shape, f32),
            VM((nz,) + shape, f32),
            VM((nz - 1,) + shape, f32),
            pltpu.SemaphoreType.DMA((nz,)),
            pltpu.SemaphoreType.DMA((nz,)),
        ]


class Gather:
    def __init__(self, seat, out, send, recv):
        own = out.at[seat.core, seat.z]
        self.along = [
            remote(own, own, send.at[j], recv.at[j], seat.at(seat.ahead(j)))
            for j in range(1, seat.nz)
        ]
        self.across = [remote(own, own, send.at[0], recv.at[0], seat.partner)]
        for j in range(1, seat.nz):
            block = out.at[seat.core, seat.behind(j)]
            k = seat.nz + j
            self.across.append(remote(block, block, send.at[k], recv.at[k], seat.partner))

    def start(self):
        for copy in self.along:
            copy.start()
        self.across[0].start()

    def forward(self):
        for copy, onward in zip(self.along, self.across[1:]):
            copy.wait_recv()
            onward.start()

    def finish(self):
        for copy in self.along:
            copy.wait_send()
        for copy in self.across:
            copy.wait()

    @staticmethod
    def scratch(n):
        return [pltpu.SemaphoreType.DMA((n,)), pltpu.SemaphoreType.DMA((n,))]


class Edges:
    def __init__(self, seat, sides, halos, send, recv):
        self.seat, self.halos = seat, halos
        core = seat.core
        self.copies = [
            remote(sides.at[1 - core], halos.at[core], send.at[0], recv.at[0], seat.partner),
            remote(sides.at[core], halos.at[1 - core], send.at[1], recv.at[1], seat.extra),
        ]

    def start(self):
        for copy in self.copies:
            copy.start()

    def finish(self, out):
        for copy in self.copies:
            copy.wait()
        seat = self.seat
        inner = (jnp.where(seat.me > 0, 1.0, 0.0), jnp.where(seat.me < seat.n - 1, 1.0, 0.0))
        for side in range(2):
            out[side] = self.halos[side] * inner[side]

    @staticmethod
    def scratch(shape):
        return [VM(shape, f32), pltpu.SemaphoreType.DMA((2,)), pltpu.SemaphoreType.DMA((2,))]


def add_all(refs):
    return functools.reduce(lambda x, y: x + y, [r[...] for r in refs])


def partner_of(index, bit):
    return index + bit - 2 * bit * lax.rem(index // bit, 2)


class Loads:
    def __init__(self, sources, slots, sems):
        self.count = slots.shape[0]
        self.views, self.copies = [], []
        for i, src in enumerate(sources):
            slot = i % self.count
            view = slots.at[slot, : src.shape[-2]]
            self.views.append(view)
            if len(src.shape) == 2:
                self.copies.append([pltpu.make_async_copy(src, view, sems.at[slot, 0])])
                continue
            size = src.shape[2]
            self.copies.append(
                [
                    pltpu.make_async_copy(
                        src.at[j], view.at[:, j * size : (j + 1) * size], sems.at[slot, j]
                    )
                    for j in range(src.shape[0])
                ]
            )
        for i in range(min(self.count, len(sources))):
            self.begin(i)

    def begin(self, i):
        for copy in self.copies[i]:
            copy.start()

    def get(self, i):
        for copy in self.copies[i]:
            copy.wait()
        return self.views[i]

    def release(self, i):
        if i + self.count < len(self.copies):
            self.begin(i + self.count)


def halved(view, into):
    size = 64

    def lap(k, _):
        part = pl.ds(pl.multiple_of(k * size, size), size)
        into[0, part, :], into[1, part, :] = split(view[part, :])
        return 0

    lax.fori_loop(0, into.shape[1] // size, lap, 0)
    return into


ALL_LINKS = ((2, 3, 1, 0), (3, 2, 1, 0), (1, 3, 2, 0))
EVEN = ((2, 1, 3, 0), (3, 2, 1, 0), (1, 3, 2, 0))


class Links:
    def __init__(self):
        me, dp = lax.axis_index("seq"), lax.axis_index("dp")
        z = me // 2
        self.core = lax.rem(me, 2)
        self.mine = (z // 2, lax.rem(z, 2), dp // 2, lax.rem(dp, 2))
        self.partner = {"seq": partner_of(me, 1)}
        self.devices = (
            {"seq": partner_of(me, 4)},
            {"seq": partner_of(me, 2)},
            {"dp": partner_of(dp, 2)},
            {"dp": partner_of(dp, 1)},
        )
        self.apart = (self.core, 1 - self.core)

    def copy(self, k, src, dst, send, recv):
        return pltpu.make_async_remote_copy(
            src_ref=src, dst_ref=dst, send_sem=send.at[k], recv_sem=recv.at[k],
            device_id=self.partner, device_id_type=MESH,
        )


class Scatter:
    def __init__(self, base, links, buffers, send, recv, first=0, orders=ALL_LINKS):
        self.orders = orders
        self.links, self.buffers, self.first, self.stage = links, buffers, first, first
        self.copies = {}
        for stage in range(first, first + len(buffers) - 1):
            for color, order in enumerate(self.orders):
                dim = order[stage]
                k = (base * 3 + color) * 4 + stage
                self.copies[stage, color] = pltpu.make_async_remote_copy(
                    src_ref=self.part(color, stage, 1 - links.mine[dim]),
                    dst_ref=buffers[stage - first + 1].at[color],
                    send_sem=send.at[k],
                    recv_sem=recv.at[k],
                    device_id=links.devices[dim],
                    device_id_type=MESH,
                )

    def part(self, color, stage, index):
        order = self.orders[color]
        left = [dim for dim in range(4) if dim not in order[:stage]]
        place = [index if dim == order[stage] else slice(None) for dim in left]
        return self.buffers[stage - self.first].at[(color, *place)]

    def start(self):
        for color in range(3):
            self.copies[self.stage, color].start()

    def advance(self):
        stage = self.stage
        self.stage += 1
        for color, order in enumerate(self.orders):
            self.copies[stage, color].wait()
            landed = self.buffers[stage - self.first + 1].at[color]
            landed[...] = landed[...] + self.part(color, stage, self.links.mine[order[stage]])[...]
            if (stage + 1, color) in self.copies:
                self.copies[stage + 1, color].start()


def times(s, t, lanes):
    return dots((s[0], s[1]), split(t[:, lanes]), 1, 0)


BIG = (192, PAIR)
SMALL = (96, PAIR)


def landing(block, stage):
    return (3,) + (2,) * (3 - stage) + block


class Tiles:
    def __init__(self, links, down, s, t, buffer, scratch):
        self.links, self.down = links, down
        s_slots, self.s, t_slots, self.p_big, s_sem, t_sem, send, recv = scratch
        self.s_loads = Loads([s], s_slots, s_sem)
        self.t_loads = Loads([t.at[i] for i in range(4)], t_slots, t_sem)
        self.places, self.copies = [], []
        for i in range(4):
            at = (slice(None),) * (3 if down else 1) + (i // 2, i % 2)
            self.places.append(buffer.at[at])
            self.copies.append(links.copy(i, self.p_big.at[i % 2, 1], self.places[i], send, recv))

    def compute(self, i):
        if i == 0:
            halved(self.s_loads.get(0), self.s)
        t, slot, apart = self.t_loads.get(i), i % 2, self.links.apart
        core = self.links.core

        def lap(third, _):
            g = times(self.s, t, pl.ds(pl.multiple_of(third * 256, 256), 256))
            for side in range(2):
                lanes = slice(side * PAIR, (side + 1) * PAIR)
                if self.down:
                    for j in range(8):
                        at = (slot, apart[j % 2], third, j // 4, j // 2 % 2)
                        self.p_big[(*at, slice(side * 96, side * 96 + 96))] = g[j * 96 : (j + 1) * 96, lanes]
                else:
                    block = 2 * third + side
                    parity, color = block // 3, lax.rem(block, 3)
                    half = core + parity * (1 - 2 * core)
                    for j in range(4):
                        self.p_big[slot, half, color, j // 2, j % 2] = g[j * 192 : (j + 1) * 192, lanes]
            return 0

        lax.fori_loop(0, 3, lap, 0)
        self.t_loads.release(i)
        self.copies[i].start()

    def absorb(self, i):
        self.copies[i].wait()
        place = self.places[i]
        place[...] = place[...] + self.p_big[i % 2, 0]

    @staticmethod
    def scratch(rows, width):
        dma = pltpu.SemaphoreType.DMA
        return [
            VM((1, width, rows), f32),
            VM((2, width, rows), bf16),
            VM((2, rows, width), f32),
            VM((2, 2, 3, 2, 2) + BIG, f32),
            dma((1, 4)),
            dma((2, 1)),
            dma((4,)),
            dma((4,)),
        ]


def project_kernel(n, items, factor, tok_ref, mem_ref, wq_ref, wk_ref, wv_ref, vec_ref,
                   q_out, k_out, v_out, lq_ref, lk_ref, inv_ref,
                   q_ref, k_ref, v_ref, tok_h, tok_l, halves, w_s, w_sem, out_sem,
                   sums, land, *scratch):
    seat = Seat(n)
    rows = items * MARKS // n
    width = tok_ref.shape[2]
    reduce = Reduce(seat, sums, *scratch[:5])
    gather = Gather(seat, land, *scratch[5:])
    fetches = [
        pltpu.make_async_copy(ref, w_s.at[i], w_sem.at[i])
        for i, ref in enumerate((wq_ref, wk_ref, wv_ref))
    ]
    for fetch in fetches:
        fetch.start()
    stores = [
        pltpu.make_async_copy(src, dst, out_sem.at[i])
        for i, (src, dst) in enumerate(
            ((q_ref, q_out), (k_ref, k_out), (v_ref, v_out))
        )
    ]
    seat.hello(False)
    for item in range(items):
        member = mem_ref[item].astype(bf16)
        hi, lo = split(tok_ref[item])
        tok_h[item], tok_l[item] = hi, lo
        total = dg(member, hi, 1, 0) + dg(member, lo, 1, 0)
        count = jnp.sum(mem_ref[item], axis=1, keepdims=True)
        for part in range(MARKS // rows):
            c = item * (MARKS // rows) + part
            piece = slice(part * rows, (part + 1) * rows)
            sums[c // seat.nz, c % seat.nz, :, :width] = total[piece]
            sums[c // seat.nz, c % seat.nz, :, width:] = jnp.broadcast_to(
                count[piece], (rows, PAIR)
            )
    reduce.start()
    b_query, b_value = vec_ref[0:1, :], vec_ref[1:2, :]
    for place in range(3):
        fetches[place].wait()
        halved(w_s.at[place], halves.at[2 * place : 2 * place + 2])

    def project(place, out_ref, bias, scale):
        def lap(item, _):
            x = (tok_h[item], tok_l[item])
            y = dots(x, (halves[2 * place], halves[2 * place + 1]), 1, 0)
            y = y if bias is None else y + bias
            out_ref[item] = y if scale is None else y * scale
            return 0

        lax.fori_loop(0, items, lap, 0)

    project(0, q_ref, b_query, factor)
    stores[0].start()
    reduce.middle(add_all)
    project(1, k_ref, None, factor)
    stores[1].start()
    land[seat.core, seat.z] = reduce.finish(add_all)
    gather.start()
    project(2, v_ref, b_value, None)
    stores[2].start()
    gather.forward()
    gather.finish()
    whole_land = land[...].reshape(items * MARKS, width + PAIR)
    divisor = jnp.maximum(whole_land[:, width:], 1.0)
    inv_ref[...] = (1.0 / divisor).reshape(items, MARKS, PAIR)
    filled = whole_land[:, width : width + 1] / divisor[:, 0:1]
    x = split(whole_land[:, :width] / divisor[:, 0:1])
    lq = (dots(x, (halves[0], halves[1]), 1, 0) + filled * b_query) * factor
    lk = dots(x, (halves[2], halves[3]), 1, 0) * factor
    lq_ref[...] = lq.reshape(items, MARKS, width)
    lk_ref[...] = lk.reshape(items, MARKS, width)
    for store in stores:
        store.wait()


def project_call(tokens, member_t, w_query, w_key, w_value, vectors, n, factor):
    items, span, width = tokens.shape
    rows = items * MARKS // n
    big = jax.ShapeDtypeStruct((items, span, width), f32)
    small = jax.ShapeDtypeStruct((items, MARKS, width), f32)
    vmem, any_space = pl.BlockSpec(memory_space=VM), pl.BlockSpec(memory_space=pl.ANY)
    return pl.pallas_call(
        functools.partial(project_kernel, n, items, factor),
        out_shape=[big, big, big, small, small, jax.ShapeDtypeStruct((items, MARKS, PAIR), f32)],
        in_specs=[vmem] * 2 + [any_space] * 3 + [vmem],
        out_specs=[any_space] * 3 + [vmem] * 3,
        scratch_shapes=[VM((items, span, width), f32)] * 3
        + [VM((items, span, width), bf16)] * 2
        + [
            VM((6, width, width), bf16),
            VM((3, width, width), f32),
            pltpu.SemaphoreType.DMA((3,)),
            pltpu.SemaphoreType.DMA((3,)),
            VM((2, n // 2, rows, width + PAIR), f32),
            VM((2, n // 2, rows, width + PAIR), f32),
        ]
        + Reduce.scratch(n, (rows, width + PAIR))
        + Gather.scratch(n),
        compiler_params=params(collective_id=0, has_side_effects=True),
        name="project",
    )(tokens, member_t, w_query, w_key, w_value, vectors)


def scores_kernel(per, pairs, q_ref, k_ref, v_ref, lq_ref, lk_ref, use_ref, k1_ref, w3_ref, top_ref, chunk):
    item = pl.program_id(0)
    stats = per * MARKS

    @pl.when(item == 0)
    def _():
        chunk[...] = jnp.zeros_like(chunk)

    use = use_ref[0]
    for p in range(pairs):
        lanes = slice(p * PAIR, (p + 1) * PAIR)
        q = q_ref[0, :, lanes]
        s1 = dot3(spread(lk_ref[0, :, lanes]), q, 1, 1)
        e1 = jnp.exp(s1 - block_max(s1))
        k1_ref[0, lanes, :] = e1 / block_sum(e1)
        s3 = dot3(spread(lq_ref[0, :, lanes]), k_ref[0, :, lanes], 1, 1)
        masked = jnp.where(use > 0, s3, -1e30)
        top = jnp.max(masked, axis=1, keepdims=True)
        w3 = jnp.exp(masked - top) * use
        w3_ref[0, lanes, :] = w3
        total = jnp.sum(w3, axis=1, keepdims=True)
        weighted = compacted(dot3(w3, v_ref[0, :, lanes]))
        top_row = row_of(top)
        top_ref[0, p : p + 1, :] = top_row
        g = item * pairs + p
        owner, place = g // per, g % per
        chunk[owner, pl.ds(pl.multiple_of(place * MARKS, MARKS), MARKS), :] = weighted
        chunk[owner, pl.ds(stats + 2 * place, 1), :] = top_row
        chunk[owner, pl.ds(stats + 2 * place + 1, 1), :] = row_of(total)


def scores_call(q, k, v, lq, lk, use_row, n, per, pairs, chunk_rows):
    items, span, width = q.shape
    return pl.pallas_call(
        functools.partial(scores_kernel, per, pairs),
        out_shape=[
            jax.ShapeDtypeStruct((items, width, span), f32),
            jax.ShapeDtypeStruct((items, width, span), f32),
            jax.ShapeDtypeStruct((items, 8, PAIR), f32),
            jax.ShapeDtypeStruct((n, chunk_rows, PAIR), f32),
        ],
        grid=(items,),
        in_specs=[per_item((span, width))] * 3
        + [per_item((MARKS, width))] * 2
        + [per_item((1, span))],
        out_specs=[per_item((width, span))] * 2
        + [per_item((8, PAIR)), whole((n, chunk_rows, PAIR))],
        compiler_params=params(),
        name="scores",
    )(q, k, v, lq, lk, use_row)


def owned_land(seat, per, pairs, ref, into):
    for place in range(per):
        g = lax.rem(seat.owner * per + place, ref.shape[0] * pairs)
        item, p = g // pairs, lax.rem(g, pairs)
        into[place] = ref[item, :, pl.ds(pl.multiple_of(p * PAIR, PAIR), PAIR)]


def newton_step(a, z, eye):
    pr = dot3(a, z)
    n1 = 7.0 * eye - pr
    n2 = 15.0 * eye - dot3(pr, n1)
    n3 = 13.0 * eye - dot3(pr, n2)
    return pr, n1, n2, n3


def unit():
    rows = lax.broadcasted_iota(jnp.int32, (PAIR, PAIR), 0)
    return (rows == lax.broadcasted_iota(jnp.int32, (PAIR, PAIR), 1)).astype(f32)


def head_total(x):
    return block_sum(jnp.sum(x, axis=1, keepdims=True))


def merged(per, refs):
    stats = per * MARKS
    weights, rest = [], []
    for place in range(per):
        tops = [r[stats + 2 * place : stats + 2 * place + 1, :] for r in refs]
        largest = functools.reduce(jnp.maximum, tops)
        total = jnp.zeros_like(largest)
        weighted = jnp.zeros((MARKS, PAIR), f32)
        for r, top in zip(refs, tops):
            scale = jnp.exp(top - largest)
            total = total + scale * r[stats + 2 * place + 1 : stats + 2 * place + 2, :]
            scales = compacted(column_of(scale))
            weighted = weighted + scales * r[place * MARKS : (place + 1) * MARKS, :]
        weights.append(weighted)
        rest += [largest, total]
    filler = jnp.zeros((refs[0].shape[0] - stats - 2 * per, PAIR), f32)
    return jnp.concatenate(weights + rest + [filler], axis=0)


def exchange_kernel(n, per, pairs, chunk_ref, lq_ref, lk_ref, side_ref,
                    a_ref, z_ref, lqo_ref, lko_ref, ctx_ref, out_ref, halo_ref, mine, *scratch):
    seat = Seat(n)
    merge = functools.partial(merged, per)
    reduce = Reduce(seat, chunk_ref, *scratch[:5])
    gather = Gather(seat, out_ref, *scratch[5:7])
    edges = Edges(seat, side_ref, *scratch[7:])
    seat.hello(True)
    reduce.start()
    edges.start()
    owned_land(seat, per, pairs, lq_ref, lqo_ref)
    owned_land(seat, per, pairs, lk_ref, lko_ref)
    diagonal = diagonal_mask()
    eye = unit()
    for place in range(per):
        s2 = dot3(spread(lqo_ref[place]), spread(lko_ref[place]), 1, 1)
        s2 = jnp.where(diagonal, s2, -1e30)
        e2 = jnp.exp(s2 - jnp.max(s2, axis=1, keepdims=True))
        e2 = jnp.where(diagonal, e2, 0.0)
        a = e2 / jnp.sum(e2, axis=1, keepdims=True)
        a_ref[place] = a
        z_ref[0, place] = jnp.transpose(a) / head_total(a * a)
    reduce.middle(merge)

    def lap(step, _):
        for place in range(per):
            z = z_ref[step, place]
            _, _, _, n3 = newton_step(a_ref[place], z, eye)
            z_ref[step + 1, place] = 0.25 * dot3(z, n3)
        return 0

    lax.fori_loop(0, NEWTON, lap, 0)
    mine[...] = reduce.finish(merge)
    stats = per * MARKS
    block = out_ref.at[seat.core, seat.z]
    block[stats:, :] = mine[stats:, :]
    for place in range(per):
        rows = slice(place * MARKS, (place + 1) * MARKS)
        total = mine[stats + 2 * place + 1 : stats + 2 * place + 2, :]
        context = mine[rows, :] / compacted(column_of(total))
        ctx_ref[place] = context
        block[rows, :] = compacted(dot3(z_ref[NEWTON, place], spread(context)))
    gather.start()
    edges.finish(halo_ref)
    gather.forward()
    gather.finish()


def exchange_call(chunks, lq, lk, sides, n, per, pairs):
    rows = chunks.shape[1]
    small = jax.ShapeDtypeStruct((per, MARKS, PAIR), f32)
    blocks = (2, n // 2, rows, PAIR)
    out = pl.pallas_call(
        functools.partial(exchange_kernel, n, per, pairs),
        out_shape=[
            jax.ShapeDtypeStruct((per, PAIR, PAIR), f32),
            jax.ShapeDtypeStruct((NEWTON + 1, per, PAIR, PAIR), f32),
            small,
            small,
            small,
            jax.ShapeDtypeStruct(blocks, f32),
            jax.ShapeDtypeStruct(sides.shape, f32),
        ],
        in_specs=[pl.BlockSpec(memory_space=VM)] * 4,
        out_specs=[pl.BlockSpec(memory_space=VM)] * 7,
        scratch_shapes=[VM((rows, PAIR), f32)]
        + Reduce.scratch(n, (rows, PAIR))
        + Gather.scratch(n)
        + Edges.scratch(sides.shape),
        compiler_params=params(collective_id=1, has_side_effects=True),
        name="exchange",
    )(chunks.reshape(blocks), lq, lk, sides)
    return list(out[:5]) + [out[5].reshape(n, rows, PAIR), out[6]]


def toeplitz(taps_row, rows):
    wide = jnp.broadcast_to(taps_row, (rows, 2 * PAIR))
    return pltpu.roll(wide, 0, 1, stride=1, stride_axis=0)


def keep_taps(taps_ref, into, heads):
    for h in range(heads):
        hi, lo = split(toeplitz(taps_ref[h : h + 1, :], PAIR))
        into[0, h] = hi
        into[1, h] = lo


def keep_window(win, left, middle, right, margin, span):
    for rows, part in (
        (slice(0, margin), left),
        (slice(margin, margin + span), middle),
        (slice(margin + span, 2 * margin + span), right),
    ):
        hi, lo = split(part)
        win[0, rows, :] = hi
        win[1, rows, :] = lo


def convolve(taps, win, p, block, window):
    lanes = slice(p * PAIR, (p + 1) * PAIR)
    rows = slice(block * PAIR, block * PAIR + window)
    v = (win[0, rows, lanes], win[1, rows, lanes])
    halves = []
    for h in (2 * p, 2 * p + 1):
        t = (taps[0, h, :, :window], taps[1, h, :, :window])
        halves.append(dots(t, v, 1, 0))
    return jnp.where(lane_low((PAIR, PAIR)), halves[0], halves[1])


def owned_by(g, per):
    return g // per, g % per


def mix_kernel(per, pairs, margin, held, k1_ref, v_ref, use_ref, left_ref, right_ref, taps_ref, out_ref, taps, win):
    item = pl.program_id(0)
    span = v_ref.shape[1]
    window = PAIR + 2 * margin

    @pl.when(item == 0)
    def _():
        keep_taps(taps_ref, taps, 2 * pairs)

    keep_window(win, left_ref[0, 0], v_ref[0] * use_ref[0], right_ref[0, 0], margin, span)
    for p in range(pairs):
        lanes = slice(p * PAIR, (p + 1) * PAIR)
        slot, place = owned_by(item * pairs + p, per)
        mixed = held[slot, pl.ds(pl.multiple_of(place * MARKS, MARKS), MARKS), :]
        nystrom = dot3(k1_ref[0, lanes, :], spread(mixed), 0, 0)
        for block in range(span // PAIR):
            rows = slice(block * PAIR, (block + 1) * PAIR)
            out_ref[0, rows, lanes] = nystrom[rows] + convolve(taps, win, p, block, window)


def halo_specs(margin, width):
    return [
        pl.BlockSpec((1, 1, margin, width), lambda i, side=side: (side, i, 0, 0))
        for side in range(2)
    ]


def mix_call(blocks, k1, v, use_col, halos, taps, per, pairs, margin):
    items, span, width = v.shape
    return pl.pallas_call(
        functools.partial(mix_kernel, per, pairs, margin),
        out_shape=jax.ShapeDtypeStruct((items, span, width), f32),
        grid=(items,),
        in_specs=[whole(blocks.shape)]
        + [per_item((width, span)), per_item((span, width)), per_item((span, 1))]
        + halo_specs(margin, width)
        + [whole(taps.shape)],
        out_specs=per_item((span, width)),
        scratch_shapes=[
            VM((2, 2 * pairs, PAIR, 2 * PAIR), bf16),
            VM((2, span + 2 * margin, width), bf16),
        ],
        compiler_params=params(),
        name="mix",
    )(blocks, k1, v, use_col, halos, halos, taps)


def erf(x):
    x = jnp.clip(x, -3.832506856900711, 3.832506856900711)
    s = x * x
    a = 0.00022905065861350646
    for c in (0.0034082910107109506, 0.050955695062380861, 0.18520832239976145, 1.128379143519084):
        a = a * s + c
    b = -1.1791602954361697e-7
    for c in (
        0.000023547966471313185,
        0.0010179625278914885,
        0.014070470171167667,
        0.11098505178285362,
        0.49746925110067538,
        1.0,
    ):
        b = b * s + c
    return x * a / b


def normalize(x):
    center = x - jnp.mean(x, axis=-1, keepdims=True)
    inv_root = lax.rsqrt(jnp.mean(center * center, axis=-1, keepdims=True) + epsilon)
    return center * inv_root, inv_root


def norm_back(grad, scaled, inv_root):
    first = jnp.mean(grad, axis=-1, keepdims=True)
    second = jnp.mean(grad * scaled, axis=-1, keepdims=True)
    return inv_root * (grad - first - scaled * second)


def rows_kernel(
    x_ref, tok_ref, cot_ref, vec_ref, bup_ref, wo_ref, wu_ref, wd_ref,
    out_ref, act_ref, u_ref, r2t_ref, h1t_ref, r1t_ref, r1_ref, og_ref, sums_ref, bsum_ref,
    slope, wo_h, wo_l, wu_h, wu_l, wd_h, wd_l, staged, sems,
):
    step = pl.program_id(0)
    width = tok_ref.shape[1]
    ff = wu_ref.shape[1]
    tiles = [slice(c, c + width) for c in range(0, ff, width)]

    @pl.when(step == 0)
    def _():
        sums_ref[...] = jnp.zeros_like(sums_ref)
        bsum_ref[...] = jnp.zeros_like(bsum_ref)
        jobs = [(wo_ref, slice(None), slice(None), wo_h, wo_l)]
        jobs += [(wu_ref, slice(None), c, wu_h, wu_l) for c in tiles]
        jobs += [(wd_ref, c, slice(None), wd_h, wd_l) for c in tiles]
        depth, pieces = sems.shape
        size = width // pieces

        def load(i):
            w, r, c, _, _ = jobs[i]
            start = r.start or 0
            return [
                pltpu.make_async_copy(
                    w.at[pl.ds(start + k * size, size), c],
                    staged.at[i % depth, pl.ds(k * size, size)],
                    sems.at[i % depth, k],
                )
                for k in range(pieces)
            ]

        loads = [load(i) for i in range(len(jobs))]
        for copies in loads[:depth]:
            for copy in copies:
                copy.start()
        for i, (_, r, c, hi_ref, lo_ref) in enumerate(jobs):
            for copy in loads[i]:
                copy.wait()
            base = r.start or 0

            def lap(k, _, i=i, c=c, base=base, hi_ref=hi_ref, lo_ref=lo_ref):
                start = pl.multiple_of(k * 64, 64)
                hi, lo = split(staged[i % depth, pl.ds(start, 64), :])
                hi_ref[pl.ds(base + start, 64), c] = hi
                lo_ref[pl.ds(base + start, 64), c] = lo
                return 0

            lax.fori_loop(0, width // 64, lap, 0)
            if i + depth < len(jobs):
                for copy in loads[i + depth]:
                    copy.start()

    b_out, gain_one, shift_one = vec_ref[0:1, :], vec_ref[1:2, :], vec_ref[2:3, :]
    b_down, gain_two, shift_two = vec_ref[3:4, :], vec_ref[4:5, :], vec_ref[5:6, :]
    wo = (wo_h[...], wo_l[...])
    attention = dots(split(x_ref[...]), wo, 1, 0) + b_out
    scaled_one, root_one = normalize(tok_ref[...] + attention)
    hidden = scaled_one * gain_one + shift_one
    h1t_ref[0] = jnp.transpose(hidden)
    hs = split(hidden)
    down = b_down
    for i, c in enumerate(tiles):
        pre = dots(hs, (wu_h[:, c], wu_l[:, c]), 1, 0) + bup_ref[:, c]
        phi = 0.5 + 0.5 * erf(pre * 0.7071067811865476)
        slope[:, c] = phi + pre * (0.3989422804014327 * jnp.exp(-0.5 * pre * pre))
        act = pre * phi
        act_ref[i] = act
        act = split(act)
        down = down + dots(act, (wd_h[c, :], wd_l[c, :]), 1, 0)
    scaled_two, root_two = normalize(hidden + down)
    out_ref[...] = scaled_two * gain_two + shift_two
    cot = cot_ref[...]
    r2 = norm_back(cot * gain_two, scaled_two, root_two)
    r2t_ref[0] = jnp.transpose(r2)
    rs = split(r2)
    grad_hidden = r2
    for i, c in enumerate(tiles):
        u = dots(rs, (wd_h[c, :], wd_l[c, :]), 1, 1) * slope[:, c]
        halves = split(u)
        u_ref[i] = u
        bsum_ref[:, c] += jnp.sum(u, axis=0, keepdims=True)
        grad_hidden = grad_hidden + dots(halves, (wu_h[:, c], wu_l[:, c]), 1, 1)
    r1 = norm_back(grad_hidden * gain_one, scaled_one, root_one)
    r1_ref[...] = r1
    r1t_ref[0] = jnp.transpose(r1)
    og_ref[...] = dots(split(r1), wo, 1, 1)
    for row, value in enumerate(
        (cot * scaled_two, cot, r2, grad_hidden * scaled_one, grad_hidden, r1)
    ):
        sums_ref[row : row + 1, :] += jnp.sum(value, axis=0, keepdims=True)


def rows_call(x, tokens, cotangent, w_out, w_up, w_down, vectors, b_up):
    rows, width = tokens.shape
    ff = w_up.shape[1]
    tile = 256
    count = ff // width
    wide = pl.BlockSpec((tile, width), lambda i: (i, 0))
    any_space = pl.BlockSpec(memory_space=pl.ANY)

    def fixed(shape):
        return pl.BlockSpec(shape, lambda i: (0, 0))

    narrow = jax.ShapeDtypeStruct((rows, width), f32)
    broad = jax.ShapeDtypeStruct((count, rows, width), f32)
    tall = jax.ShapeDtypeStruct((rows // tile, width, tile), f32)
    return pl.pallas_call(
        rows_kernel,
        out_shape=[narrow]
        + [broad] * 2
        + [tall] * 3
        + [narrow, narrow, jax.ShapeDtypeStruct((8, width), f32), jax.ShapeDtypeStruct((1, ff), f32)],
        grid=(rows // tile,),
        in_specs=[wide] * 3 + [fixed(vectors.shape), fixed(b_up.shape)] + [any_space] * 3,
        out_specs=[wide]
        + [pl.BlockSpec((count, tile, width), lambda i: (0, i, 0))] * 2
        + [pl.BlockSpec((1, width, tile), lambda i: (i, 0, 0))] * 3
        + [wide, wide, fixed((8, width)), fixed((1, ff))],
        scratch_shapes=[VM((tile, ff), f32)]
        + [VM((width, width), bf16)] * 2
        + [VM((width, ff), bf16)] * 2
        + [VM((ff, width), bf16)] * 2
        + [VM((2, width, width), f32), pltpu.SemaphoreType.DMA((2, 6))],
        compiler_params=params(),
        name="rows",
    )(x, tokens, cotangent, vectors, b_up, w_out, w_up, w_down)


def one_back_kernel(per, pairs, held, k1_ref, og_ref, q_ref, lk_ref, gq_ref, chunk):
    item = pl.program_id(0)

    @pl.when(item == 0)
    def _():
        chunk[...] = jnp.zeros_like(chunk)

    for p in range(pairs):
        lanes = slice(p * PAIR, (p + 1) * PAIR)
        owner, place = owned_by(item * pairs + p, per)
        mixed = spread(held[owner, pl.ds(pl.multiple_of(place * MARKS, MARKS), MARKS), :])
        k1 = k1_ref[0, lanes, :]
        og = split(og_ref[0, :, lanes])
        part_mixed = compacted(dots(split(k1), og, 1, 0))
        grad = dots(split(mixed), og, 1, 1)
        scores = k1 * (grad - block_sum(k1 * grad))
        ss = split(scores)
        gq_ref[0, :, lanes] = dots(ss, split(spread(lk_ref[0, :, lanes])), 0, 0)
        part_key = compacted(dots(ss, split(q_ref[0, :, lanes]), 1, 0))
        chunk[owner, pl.ds(pl.multiple_of(place * 2 * MARKS, 2 * MARKS), MARKS), :] = part_mixed
        chunk[owner, pl.ds(pl.multiple_of(place * 2 * MARKS + MARKS, MARKS), MARKS), :] = part_key


def one_back_call(blocks, k1, og, q, lk, per, pairs):
    items, span, width = q.shape
    out = (blocks.shape[0], 2 * per * MARKS, PAIR)
    wide = per_item((span, width))
    return pl.pallas_call(
        functools.partial(one_back_kernel, per, pairs),
        out_shape=[
            jax.ShapeDtypeStruct((items, span, width), f32),
            jax.ShapeDtypeStruct(out, f32),
        ],
        grid=(items,),
        in_specs=[whole(blocks.shape), per_item((width, span)), wide, wide]
        + [per_item((MARKS, width))],
        out_specs=[wide, whole(out)],
        compiler_params=params(),
        name="one_back",
    )(blocks, k1, og, q, lk)


class ConvBack:
    def __init__(self, pairs, margin, og, ghalo, v, vhalo, use, taps_ref, gv, gtaps, scratch):
        self.pairs, self.margin, self.ghalo, self.vhalo = pairs, margin, ghalo, vhalo
        self.og, self.v, self.use, self.gv, self.gtaps = og, v, use, gv, gtaps
        self.taps_ref = taps_ref
        self.taps, self.gwin, self.vwin, self.acc = scratch
        self.span = v.shape[1]
        self.window = PAIR + 2 * margin

    def begin(self):
        keep_taps(self.taps_ref, self.taps, 2 * self.pairs)
        self.acc[...] = jnp.zeros_like(self.acc)

    def item(self, item):
        margin, window, gwin, vwin = self.margin, self.window, self.gwin, self.vwin
        use = self.use[item]
        keep_window(gwin, self.ghalo[0, item], self.og[item], self.ghalo[1, item], margin, self.span)
        values = self.v[item] * use
        keep_window(vwin, self.vhalo[0, item], values, self.vhalo[1, item], margin, self.span)
        for p in range(self.pairs):
            lanes = slice(p * PAIR, (p + 1) * PAIR)
            for block in range(self.span // PAIR):
                rows = slice(block * PAIR, (block + 1) * PAIR)
                self.gv[item, rows, lanes] = convolve(self.taps, gwin, p, block, window) * use[rows]
                inner = slice(margin + block * PAIR, margin + (block + 1) * PAIR)
                outer = slice(block * PAIR, block * PAIR + window)
                v = (vwin[0, outer, lanes], vwin[1, outer, lanes])
                low = lane_low((PAIR, PAIR))
                hi, lo = gwin[0, inner, lanes], gwin[1, inner, lanes]
                zero = jnp.zeros_like(hi)
                first = (jnp.where(low, hi, zero), jnp.where(low, lo, zero))
                second = (jnp.where(low, zero, hi), jnp.where(low, zero, lo))
                self.acc[2 * p] += dots(first, v, 1, 1)
                self.acc[2 * p + 1] += dots(second, v, 1, 1)

    def end(self):
        rows = lax.broadcasted_iota(jnp.int32, (PAIR, PAIR), 0)
        flip = (rows + lax.broadcasted_iota(jnp.int32, (PAIR, PAIR), 1) == PAIR - 1).astype(bf16)
        for h in range(2 * self.pairs):
            c = self.acc[h]
            c = jnp.concatenate([c, jnp.zeros((PAIR, 2 * PAIR - self.window), f32)], axis=1)
            hi = c.astype(bf16)
            rest = c - hi.astype(f32)
            mid = rest.astype(bf16)
            low = (rest - mid.astype(f32)).astype(bf16)
            c = dg(flip, hi, 1, 0) + dg(flip, mid, 1, 0) + dg(flip, low, 1, 0)
            c = pltpu.roll(c, 0, 1, stride=1, stride_axis=0)
            self.gtaps[h : h + 1, :] = jnp.sum(c, axis=0, keepdims=True)

    @staticmethod
    def scratch(pairs, margin, span, width):
        return [
            VM((2, 2 * pairs, PAIR, 2 * PAIR), bf16),
            VM((2, span + 2 * margin, width), bf16),
            VM((2, span + 2 * margin, width), bf16),
            VM((2 * pairs, PAIR, PAIR + 2 * margin), f32),
        ]


def exchange_back_kernel(n, per, fused, *refs):
    refs = list(refs)
    chunk_ref, side_ref, ctx_ref, a_ref, z_ref, lq_ref, lk_ref = refs[:7]
    r2_ref, act_ref = refs[7:9] if fused else [None] * 2
    refs = refs[9:] if fused else refs[7:]
    out_ref, gq_ref, gk_ref, halo_ref = refs[:4]
    part_ref = refs[4] if fused else None
    gm, gz, ga, *scratch = refs[5:] if fused else refs[4:]
    seat = Seat(n)
    reduce = Reduce(seat, chunk_ref, *scratch[:5])
    gather = Gather(seat, out_ref, *scratch[5:7])
    edges = Edges(seat, side_ref, *scratch[7:10])
    if fused:
        links = Links()
        whole_ref, send, recv = scratch[10:13]
        tiles = Tiles(links, True, r2_ref, act_ref, whole_ref, scratch[13:])
        scatter = Scatter(0, links, [whole_ref, part_ref], send, recv)
        seat.hello(True, links.devices[2:])
    else:
        seat.hello(True)
    reduce.start()
    edges.start()
    reduce.middle(add_all)
    if fused:
        tiles.compute(0)
        tiles.compute(1)
        tiles.absorb(0)
        tiles.compute(2)
        tiles.absorb(1)
    diagonal = diagonal_mask()
    eye = unit()
    stats = per * MARKS
    gm[...] = reduce.finish(add_all)
    block = out_ref.at[seat.core, seat.z]
    block[stats:, :] = jnp.zeros((block.shape[0] - stats, PAIR), f32)
    for place in range(per):
        mixed = spread(gm[place * 2 * MARKS : place * 2 * MARKS + MARKS, :])
        context = spread(ctx_ref[place])
        grad = dot3(jnp.transpose(z_ref[NEWTON, place]), mixed)
        block[place * MARKS : (place + 1) * MARKS, :] = compacted(grad)
        dot = jnp.sum(grad * context, axis=1, keepdims=True)
        block[stats + place : stats + place + 1, :] = row_of(dot)
        gz[place] = jnp.where(diagonal, dot3(mixed, context, 1, 1), 0.0)
        ga[place] = jnp.zeros((PAIR, PAIR), f32)
    gather.start()

    def lap(back, _):
        step = NEWTON - 1 - back
        for place in range(per):
            a, z, g = a_ref[place], z_ref[step, place], 0.25 * gz[place]
            pr, n1, n2, n3 = newton_step(a, z, eye)
            back_three = dot3(jnp.transpose(z), g)
            turned = jnp.transpose(pr)
            back_two = -dot3(turned, back_three)
            back_one = -dot3(turned, back_two)
            grad = -dot3(back_three, n2, 1, 1) - dot3(back_two, n1, 1, 1) - back_one
            ga[place] += dot3(grad, z, 1, 1)
            gz[place] = dot3(g, n3, 1, 1) + dot3(jnp.transpose(a), grad)
        return 0

    if fused:
        tiles.compute(3)
        tiles.absorb(2)
        tiles.absorb(3)
        scatter.start()
        gather.forward()
        lax.fori_loop(0, NEWTON, lap, 0)
    else:
        lax.fori_loop(0, NEWTON - 1, lap, 0)
        gather.forward()
        lax.fori_loop(NEWTON - 1, NEWTON, lap, 0)
    for place in range(per):
        a, g = a_ref[place], jnp.transpose(gz[place])
        norm = head_total(a * a)
        slope = -head_total(g * a) / (norm * norm)
        grad = ga[place] + g / norm + 2.0 * slope * a
        scores = a * (grad - jnp.sum(a * grad, axis=1, keepdims=True))
        gq_ref[place] = compacted(dot3(scores, spread(lk_ref[place])))
        gk_ref[place] = gm[place * 2 * MARKS + MARKS : (place + 1) * 2 * MARKS, :] + compacted(
            dot3(jnp.transpose(scores), spread(lq_ref[place]))
        )
    edges.finish(halo_ref)
    gather.finish()
    if fused:
        scatter.advance()


def exchange_back_call(chunks, sides, ctx, a, z, lq, lk, n, rows, r2=None, act=None):
    per = ctx.shape[0]
    small = jax.ShapeDtypeStruct(ctx.shape, f32)
    chunk = chunks.shape[1:]
    blocks = (2, n // 2, rows, PAIR)
    fused = r2 is not None
    more_in, more_shapes, more_scratch = (), [], []
    if fused:
        more_in = (r2, act)
        more_shapes = [jax.ShapeDtypeStruct(landing(BIG, 0), f32)]
        more_scratch = [VM(landing(BIG, -1), f32)] + [pltpu.SemaphoreType.DMA((12,))] * 2
        more_scratch += Tiles.scratch(*act.shape[1:])
    out = pl.pallas_call(
        functools.partial(exchange_back_kernel, n, per, fused),
        out_shape=[
            jax.ShapeDtypeStruct(blocks, f32),
            small,
            small,
            jax.ShapeDtypeStruct(sides.shape, f32),
        ]
        + more_shapes,
        in_specs=[pl.BlockSpec(memory_space=VM)] * 7
        + [pl.BlockSpec(memory_space=pl.ANY)] * len(more_in),
        out_specs=[pl.BlockSpec(memory_space=VM)] * (4 + len(more_shapes)),
        scratch_shapes=[VM(chunk, f32)]
        + [VM((per, PAIR, PAIR), f32)] * 2
        + Reduce.scratch(n, chunk)
        + Gather.scratch(n)
        + Edges.scratch(sides.shape)
        + more_scratch,
        compiler_params=params(collective_id=2, has_side_effects=True),
        name="exchange_back",
    )(chunks.reshape((2, n // 2) + chunk), sides, ctx, a, z, lq, lk, *more_in)
    return [out[0].reshape(n, rows, PAIR)] + list(out[1:])


def keep_both(value, lanes, out_ref, turned_ref):
    out_ref[0, :, lanes] = value
    turned_ref[0, lanes, :] = jnp.transpose(value)


def both_specs(items, span, width):
    shapes = [(items, span, width), (items, width, span)]
    shapes = [jax.ShapeDtypeStruct(shape, f32) for shape in shapes]
    return shapes, [per_item((span, width)), per_item((width, span))]


def three_back_kernel(per, pairs, held, stat, w3_ref, top_ref, v_ref, k_ref, lq_ref,
                      gk_ref, gv_ref, chunk):
    item = pl.program_id(0)
    stats = per * MARKS

    @pl.when(item == 0)
    def _():
        chunk[...] = jnp.zeros_like(chunk)

    for p in range(pairs):
        lanes = slice(p * PAIR, (p + 1) * PAIR)
        owner, place = owned_by(item * pairs + p, per)
        grad = split(spread(held[owner, pl.ds(pl.multiple_of(place * MARKS, MARKS), MARKS), :]))
        row_dot = column_of(held[owner, pl.ds(stats + place, 1), :])
        largest = stat[owner, pl.ds(stats + 2 * place, 1), :]
        total = stat[owner, pl.ds(stats + 2 * place + 1, 1), :]
        scale = column_of(jnp.exp(top_ref[0, p : p + 1, :] - largest) / total)
        k3 = w3_ref[0, lanes, :] * scale[:, 0:1]
        gk3 = dots(grad, split(v_ref[0, :, lanes]), 1, 1)
        scores = split(k3 * (gk3 - row_dot[:, 0:1]))
        gv_ref[0, :, lanes] = dots(split(k3), grad, 0, 0)
        gk_ref[0, :, lanes] = dots(scores, split(spread(lq_ref[0, :, lanes])), 0, 0)
        part = compacted(dots(scores, split(k_ref[0, :, lanes]), 1, 0))
        chunk[owner, pl.ds(pl.multiple_of(place * MARKS, MARKS), MARKS), :] = part


def three_back_call(grads, blocks, w3, top, v, k, lq, per, pairs):
    items, span, width = v.shape
    out = (blocks.shape[0], per * MARKS, PAIR)
    wide = per_item((span, width))
    shape = jax.ShapeDtypeStruct((items, span, width), f32)
    return pl.pallas_call(
        functools.partial(three_back_kernel, per, pairs),
        out_shape=[shape, shape, jax.ShapeDtypeStruct(out, f32)],
        grid=(items,),
        in_specs=[whole(blocks.shape)] * 2
        + [per_item((width, span)), per_item((8, PAIR)), wide, wide]
        + [per_item((MARKS, width))],
        out_specs=[wide, wide, whole(out)],
        compiler_params=params(),
        name="three_back",
    )(grads, blocks, w3, top, v, k, lq)


def land_exchange_kernel(n, per, pairs, margin, fused, *refs):
    refs = list(refs)
    chunk_ref, q_ref, k_ref = refs[:3]
    convolution, refs = refs[3:9], refs[9:]
    if fused:
        in_down, hid_ref, u_ref, out_ref, gv_ref, gtaps_ref, down_ref, part_ref, *scratch = refs
    else:
        out_ref, gv_ref, gtaps_ref, *scratch = refs
    conv = ConvBack(pairs, margin, *convolution, gv_ref, gtaps_ref, scratch[:4])
    scratch = scratch[4:]

    def conv_lap(item, _):
        conv.item(item)
        return 0

    seat = Seat(n)
    reduce = Reduce(seat, chunk_ref, *scratch[:5])
    gather = Gather(seat, out_ref, *scratch[5:7])
    if fused:
        links = Links()
        second, third, whole_ref, send, recv = scratch[7:12]
        down = Scatter(0, links, [in_down, second, third, down_ref], send, recv, 1)
        up = Scatter(1, links, [whole_ref, part_ref], send, recv)
        tiles = Tiles(links, False, hid_ref, u_ref, whole_ref, scratch[12:])
        seat.hello(False, links.devices[2:])
    else:
        seat.hello(False)
    reduce.start()
    reduce.middle(add_all)
    if fused:
        down.start()
        tiles.compute(0)
    half = per * MARKS
    block = out_ref.at[seat.core, seat.z]
    block[half:, :] = k_ref[...]
    block[:half, :] = q_ref[...] + reduce.finish(add_all)
    gather.start()
    if fused:
        tiles.compute(1)
        tiles.absorb(0)
        down.advance()
        tiles.compute(2)
        tiles.absorb(1)
        tiles.compute(3)
        tiles.absorb(2)
        down.advance()
    conv.begin()
    items = gv_ref.shape[0]
    if fused:
        tiles.absorb(3)
        up.start()
    lax.fori_loop(0, items // 2, conv_lap, 0)
    gather.forward()
    lax.fori_loop(items // 2, items, conv_lap, 0)
    conv.end()
    gather.finish()
    if fused:
        down.advance()
        up.advance()


def land_exchange_call(chunks, own_q, own_k, convolution, n, pairs, margin, in_down=None, hidden=None, u=None):
    per = own_q.shape[0]
    half = per * MARKS
    blocks = (2, n // 2, 2 * half, PAIR)
    fused = in_down is not None
    conv_shapes = [convolution[0].shape, (-(-2 * pairs // 8) * 8, 2 * PAIR)]
    vmem = pl.BlockSpec(memory_space=VM)
    more_in, more_specs, more_shapes, more_scratch = (), [], [], []
    if fused:
        more_in = (in_down, hidden, u)
        more_specs = [vmem] + [pl.BlockSpec(memory_space=pl.ANY)] * 2
        more_shapes = [landing(BIG, 3), landing(BIG, 0)]
        more_scratch = [VM(landing(BIG, stage), f32) for stage in (1, 2, -1)]
        more_scratch += [pltpu.SemaphoreType.DMA((24,))] * 2
        more_scratch += Tiles.scratch(*u.shape[1:])
    out = pl.pallas_call(
        functools.partial(land_exchange_kernel, n, per, pairs, margin, fused),
        out_shape=[jax.ShapeDtypeStruct(shape, f32) for shape in [blocks, *conv_shapes] + more_shapes],
        in_specs=[vmem] * 9 + more_specs,
        out_specs=[vmem] * (3 + len(more_shapes)),
        scratch_shapes=ConvBack.scratch(pairs, margin, *convolution[0].shape[1:])
        + Reduce.scratch(n, (half, PAIR)) + Gather.scratch(n) + more_scratch,
        compiler_params=params(collective_id=3, has_side_effects=True),
        name="land_exchange",
    )(
        chunks.reshape(2, n // 2, half, PAIR),
        own_q.reshape(half, PAIR),
        own_k.reshape(half, PAIR),
        *convolution,
        *more_in,
    )
    return [out[0].reshape(n, 2 * half, PAIR)] + list(out[1:])


def land_back_kernel(per, pairs, factor, held, gq_ref, gk_ref, gv_ref, gvc_ref, mem_ref, inv_ref, *outs):
    sums_ref = outs[6]
    item = pl.program_id(0)
    half = per * MARKS

    @pl.when(item == 0)
    def _():
        sums_ref[...] = jnp.zeros_like(sums_ref)

    member = mem_ref[0].astype(bf16)
    inv = inv_ref[0]
    for p in range(pairs):
        lanes = slice(p * PAIR, (p + 1) * PAIR)
        slot, place = owned_by(item * pairs + p, per)
        for ref, out, base in ((gq_ref, outs[:2], 0), (gk_ref, outs[2:4], half)):
            grad = held[slot, pl.ds(pl.multiple_of(base + place * MARKS, MARKS), MARKS), :]
            hi, lo = split(grad * inv)
            landed = dg(member, hi, 0, 0) + dg(member, lo, 0, 0)
            total = (ref[0, :, lanes] + landed) * factor
            keep_both(total, lanes, *out)
            if base == 0:
                sums_ref[0:1, lanes] += jnp.sum(total, axis=0, keepdims=True)
        total = gv_ref[0, :, lanes] + gvc_ref[0, :, lanes]
        keep_both(total, lanes, *outs[4:6])
        sums_ref[1:2, lanes] += jnp.sum(total, axis=0, keepdims=True)


def land_back_call(blocks, gq, gk, gv, gv_conv, member_t, inv, per, pairs, factor):
    items, span, width = gq.shape
    wide = per_item((span, width))
    shapes, specs = both_specs(items, span, width)
    out = pl.pallas_call(
        functools.partial(land_back_kernel, per, pairs, factor),
        out_shape=shapes * 3 + [jax.ShapeDtypeStruct((8, width), f32)],
        grid=(items,),
        in_specs=[whole(blocks.shape)] + [wide] * 4
        + [per_item((MARKS, span)), per_item((MARKS, PAIR))],
        out_specs=specs * 3 + [whole((8, width))],
        compiler_params=params(),
        name="land_back",
    )(blocks, gq, gk, gv, gv_conv, member_t, inv)
    return out[:2], out[2:4], out[4:6], out[6]


def grads_kernel(
    r1t_ref, x_ref, gqt_ref, gkt_ref, gvt_ref, tok_ref, gq_ref, gk_ref, gv_ref, wq_ref, wk_ref, wv_ref, r1_ref,
    in_up, sums_ref, late_ref, bsum_ref, taps_ref,
    vo_ref, up_ref, qk_ref, gt_ref, total_ref,
    s_slots, s_first, s_second, t_slots, w_s, p_pair, product_s, *scratch
):
    vo_bufs, qk_bufs, up_bufs = list(scratch[:4]), list(scratch[4:8]), list(scratch[8:10])
    held, caught, load_sem, s_sem, t_sem, core_send, core_recv, send, recv, sum_send, sum_recv = scratch[10:]
    links = Links()
    width = tok_ref.shape[1]
    ff = bsum_ref.shape[1]
    s_loads = Loads([gvt_ref, r1t_ref, gqt_ref, gkt_ref], s_slots, s_sem)
    t_loads = Loads(
        [tok_ref, x_ref, gv_ref, wv_ref, gq_ref, wq_ref, gk_ref, wk_ref], t_slots, t_sem
    )
    residual = pltpu.make_async_copy(r1_ref, gt_ref, load_sem.at[0])
    residual.start()
    barrier = pltpu.get_barrier_semaphore()
    for device in (links.partner, *links.devices):
        pl.semaphore_signal(barrier, inc=1, device_id=device, device_id_type=MESH)
    pl.semaphore_wait(barrier, 5)
    up = Scatter(0, links, [in_up, *up_bufs, up_ref], send, recv, 1, EVEN)
    vo = Scatter(1, links, [*vo_bufs, vo_ref], send, recv, orders=EVEN)
    qk = Scatter(2, links, [*qk_bufs, qk_ref], send, recv, orders=EVEN)
    up.start()

    def halfway(step):
        return pltpu.make_async_remote_copy(
            src_ref=held.at[step], dst_ref=caught.at[step],
            send_sem=sum_send.at[step], recv_sem=sum_recv.at[step],
            device_id=(links.partner, *links.devices)[step], device_id_type=MESH,
        )

    held[0] = jnp.zeros(held.shape[1:], f32)
    held[0, 0:8, :] = sums_ref[...]
    held[0, 8:16, :] = late_ref[...]
    for i, t in enumerate(range(0, ff, width)):
        held[0, 16 + i : 17 + i, :] = bsum_ref[:, t : t + width]
    held[0, 24:40, : 2 * PAIR] = taps_ref[...]
    halfway(0).start()

    def sums_on(step):
        halfway(step).wait()
        added = held[step] + caught[step]
        if step < 4:
            held[step + 1] = added
            halfway(step + 1).start()
        else:
            total_ref[...] = added

    def pair_job(first, second, t_first, t_second):
        half = PAIR // 2
        for which, (s, t) in enumerate(((first, t_first), (second, t_second))):

            def lap(third, _, s=s, t=t):
                lanes = pl.ds(pl.multiple_of(third * 256, 256), 256)
                product_s[:, lanes] = times(s, t, lanes)
                return 0

            lax.fori_loop(0, 3, lap, 0)

            def place(j, _, which=which):
                rows = pl.ds(pl.multiple_of(j * 96, 96), 96)
                z = j // 2
                parity = lax.rem(j, 2)
                side_of = links.core + parity * (1 - 2 * links.core)
                for unit in range(12):
                    block, k = divmod(unit, 3)
                    color, side = divmod(3 * which + k, 2)
                    at = (side_of, color, z // 2, lax.rem(z, 2), block // 2, block % 2)
                    p_pair[(*at, slice(None), slice(side * half, (side + 1) * half))] = product_s[
                        rows, unit * half : (unit + 1) * half
                    ]
                return 0

            lax.fori_loop(0, 8, place, 0)

    def absorb(copy, buffer):
        copy.wait()
        buffer[...] = buffer[...] + p_pair[0]

    def token_job(i):
        x, w = t_loads.get(2 + 2 * i), t_loads.get(3 + 2 * i)
        halved(w, w_s)

        def lap(c, _):
            rows = pl.ds(pl.multiple_of(c * 256, 256), 256)
            gt_ref[rows, :] += dots(split(x[rows, :]), (w_s[0], w_s[1]), 1, 1)
            return 0

        lax.fori_loop(0, gt_ref.shape[0] // 256, lap, 0)
        t_loads.release(2 + 2 * i)
        t_loads.release(3 + 2 * i)

    tokens = t_loads.get(0)
    halved(s_loads.get(0), s_first)
    s_loads.release(0)
    halved(s_loads.get(1), s_second)
    s_loads.release(1)
    pair_job(s_first, s_second, tokens, t_loads.get(1))
    t_loads.release(1)
    vo_copy = links.copy(0, p_pair.at[1], vo_bufs[0], core_send, core_recv)
    vo_copy.start()
    sums_on(0)
    up.advance()
    residual.wait()
    token_job(0)
    absorb(vo_copy, vo_bufs[0])
    vo.start()
    halved(s_loads.get(2), s_first)
    halved(s_loads.get(3), s_second)
    pair_job(s_first, s_second, tokens, tokens)
    t_loads.release(0)
    qk_copy = links.copy(1, p_pair.at[1], qk_bufs[0], core_send, core_recv)
    qk_copy.start()
    vo.advance()
    up.advance()
    sums_on(1)
    token_job(1)
    absorb(qk_copy, qk_bufs[0])
    qk.start()
    vo.advance()
    sums_on(2)
    token_job(2)
    up.advance()
    qk.advance()
    vo.advance()
    sums_on(3)
    qk.advance()
    sums_on(4)
    vo.advance()
    qk.advance()
    qk.advance()


def grads_call(arrays, r1, in_up, sums):
    rows, width = r1.shape
    any_space = pl.BlockSpec(memory_space=pl.ANY)
    vmem = pl.BlockSpec(memory_space=VM)
    dma = pltpu.SemaphoreType.DMA
    out_shapes = [
        landing(SMALL, 3), landing(BIG, 3), landing(SMALL, 3), (rows, width), (40, width),
    ]
    return pl.pallas_call(
        grads_kernel,
        out_shape=[jax.ShapeDtypeStruct(shape, f32) for shape in out_shapes],
        in_specs=[any_space] * (len(arrays) + 1) + [vmem] * (1 + len(sums)),
        out_specs=[vmem] * 5,
        scratch_shapes=[
            VM((2, width, rows), f32),
            VM((2, width, rows), bf16),
            VM((2, width, rows), bf16),
            VM((4, rows, width), f32),
            VM((2, width, width), bf16),
            VM((2, 3, 2, 2, 2, 2) + SMALL, f32),
            VM((width, width), f32),
        ]
        + [VM(landing(SMALL, stage), f32) for stage in (-1, 0, 1, 2)] * 2
        + [VM(landing(BIG, stage), f32) for stage in (1, 2)]
        + [VM((5, 40, width), f32)] * 2
        + [dma((1,)), dma((2, 4)), dma((4, 1)), dma((2,)), dma((2,))]
        + [dma((36,)), dma((36,)), dma((5,)), dma((5,))],
        compiler_params=params(collective_id=4, has_side_effects=True),
        name="grads",
    )(*arrays, r1, in_up, *sums)


def swap(x, axis, offset):
    count = lax.axis_size(axis)
    return lax.ppermute(x, axis, [(i, i ^ offset) for i in range(count)])


def both_sides(x, margin):
    return jnp.stack([x[:, :margin], x[:, -margin:]])


def bit_of(axis, bit):
    return lax.axis_index(axis) // bit % 2


def halve_rows(x, bit):
    blocks, rows, columns = x.shape
    y = x.reshape(blocks // 2, 2, rows, columns)
    mine = bit_of("seq", bit)
    keep = lax.dynamic_index_in_dim(y, mine, 1, False)
    send = lax.dynamic_index_in_dim(y, 1 - mine, 1, False)
    return keep + swap(send, "seq", bit)


def halve_columns(x, bits, bit):
    mine = bit_of("dp", bit)
    columns = x.shape[2]
    groups = 2 ** bits.index(bit)
    size = columns // (2 * groups)

    def pick(which):
        parts = [
            lax.dynamic_slice_in_dim(x, 2 * g * size + which * size, size, 2)
            for g in range(groups)
        ]
        return parts[0] if groups == 1 else jnp.concatenate(parts, axis=2)

    return pick(mine) + swap(pick(1 - mine), "dp", bit)


def powers(axis):
    count = lax.axis_size(axis)
    return [2**i for i in range(count.bit_length() - 1)]


def scatter_sum(x, order):
    seq_bits, dp_bits = powers("seq"), powers("dp")[::-1]
    count = lax.axis_size("seq")
    x = x.reshape(count, x.shape[0] // count, x.shape[1])
    x = halve_rows(x, seq_bits.pop(0))
    for axis in order:
        if axis == "z" and seq_bits:
            x = halve_rows(x, seq_bits.pop(0))
        elif axis in "xy" and dp_bits:
            half = len(powers("dp")) // 2
            low = [b for b in dp_bits if b < 2**half]
            high = [b for b in dp_bits if b >= 2**half]
            chosen = (low if axis == "x" else high) or dp_bits
            x = halve_columns(x, dp_bits, chosen[0])
            dp_bits.remove(chosen[0])
    while seq_bits:
        x = halve_rows(x, seq_bits.pop(0))
    while dp_bits:
        x = halve_columns(x, dp_bits, dp_bits[0])
        dp_bits.pop(0)
    return x[0]


def sum_everywhere(x):
    for axis in ("seq", "dp"):
        for bit in powers(axis):
            x = x + swap(x, axis, bit)
    return x


def product(a, b, ca, cb):
    return lax.dot_general(a, b, (((ca,), (cb,)), ((), ())), precision=HIGH)


def on_device(
    tokens,
    lengths,
    keep,
    w_query,
    b_query,
    w_key,
    w_value,
    b_value,
    conv_weight,
    w_out,
    b_out,
    gain_one,
    shift_one,
    w_up,
    b_up,
    w_down,
    b_down,
    gain_two,
    shift_two,
    cotangent,
):
    items, span, width = tokens.shape
    heads, taps = conv_weight.shape
    head_size = width // heads
    margin = taps // 2
    factor = head_size ** (-0.25)
    pairs = heads // 2
    n = lax.axis_size("seq")
    per = -(-items * pairs // n)
    chunk_rows = per * MARKS + 8
    position = lax.axis_index("seq") * span + jnp.arange(span, dtype=jnp.int32)
    inside = position[None, :] < lengths[:, None]
    usable = (inside & (keep > 0)).astype(f32)
    use_row, use_col = usable[:, None, :], usable[:, :, None]
    segment = jnp.where(inside, position[None, :] * MARKS // lengths[:, None], MARKS)
    marks = jnp.arange(MARKS, dtype=jnp.int32)
    member_t = (segment[:, None, :] == marks[None, :, None]).astype(f32) * use_row
    rows = tokens.reshape(items * span, width)
    taps_forward = jnp.pad(conv_weight, ((0, 4), (0, 2 * PAIR - taps)))
    taps_backward = jnp.pad(conv_weight[:, ::-1], ((0, 4), (0, 2 * PAIR - taps)))

    queries, key_rows, values, land_q, land_k, inverse_divisor = project_call(
        tokens, member_t, w_query, w_key, w_value, jnp.stack([b_query, b_value]), n, factor
    )
    k1, w3, top, chunks = scores_call(
        queries, key_rows, values, land_q, land_k, use_row, n, per, pairs, chunk_rows
    )
    use_sides = both_sides(use_col, margin)
    kernel_two, z, owned_q, owned_k, context, mixed, vhalos = exchange_call(
        chunks, land_q, land_k, both_sides(values, margin) * use_sides, n, per, pairs
    )
    x = mix_call(mixed, k1, values, use_col, vhalos, taps_forward, per, pairs, margin)

    def flat(array):
        return array.reshape(items * span, width)

    x = flat(x)
    vectors = jnp.stack([b_out, gain_one, shift_one, b_down, gain_two, shift_two])
    output, act, u, r2_t, hidden_t, r1_t, r1, og, row_sums, up_sums = rows_call(
        x, rows, cotangent.reshape(items * span, width), w_out, w_up, w_down, vectors, b_up[None, :]
    )
    og = og.reshape(items, span, width)
    grad_queries, chunks = one_back_call(mixed, k1, og, queries, land_k, per, pairs)
    ff = w_up.shape[1]
    fused = (n, lax.axis_size("dp"), width, ff) == (8, 4, 768, 3072)
    grad_context, own_q, own_k, ghalos, *down_part = exchange_back_call(
        chunks, both_sides(og, margin), context, kernel_two, z, owned_q, owned_k, n, chunk_rows,
        *((r2_t, act) if fused else ()),
    )
    grad_keys, grad_values, chunks = three_back_call(
        grad_context, mixed, w3, top, values, key_rows, land_q, per, pairs
    )
    land_grads, gv_conv, grad_taps, *ff_grads = land_exchange_call(
        chunks, own_q, own_k, (og, ghalos, values, vhalos, use_col, taps_backward), n, pairs, margin,
        *((*down_part, hidden_t, u) if fused else ()),
    )
    gq, gk, gv, late_sums = land_back_call(
        land_grads, grad_queries, grad_keys, grad_values, gv_conv,
        member_t, inverse_divisor, per, pairs, factor,
    )
    if fused:
        down, up_part = ff_grads
        vo, up, qk, grad_tokens, totals = grads_call(
            [r1_t, x, gq[1], gk[1], gv[1], rows, flat(gq[0]), flat(gk[0]), flat(gv[0])]
            + [w_query, w_key, w_value],
            r1,
            up_part,
            [row_sums, late_sums, up_sums, grad_taps],
        )
        vo, qk = (jnp.transpose(both, (0, 2, 1)).reshape(2, -1, both.shape[1]) for both in (vo, qk))
        grad_w_value, grad_w_out = vo[0], vo[1]
        grad_w_query, grad_w_key = qk[0], qk[1]
        down = down.reshape(3, 2, -1, PAIR)
        grad_w_down = jnp.transpose(down, (0, 1, 3, 2)).reshape(-1, down.shape[2])
        grad_w_up = jnp.transpose(up, (1, 0, 2)).reshape(up.shape[1], -1)
    else:
        def unturned(array):
            return flat(jnp.swapaxes(array, 1, 2))

        def untiled(array):
            return jnp.swapaxes(array, 0, 1).reshape(items * span, ff)

        gq, gk, gv = (flat(pair[0]) for pair in (gq, gk, gv))
        grad_w_down = scatter_sum(product(unturned(r2_t), untiled(act), 0, 0), "yxzz").T
        grad_w_up = scatter_sum(product(untiled(u), unturned(hidden_t), 0, 0), "xzyz").T
        grad_w_out = scatter_sum(product(r1, x, 0, 0), "zyxz").T
        grad_w_value = scatter_sum(product(gv, rows, 0, 0), "zyxz").T
        grad_w_query = scatter_sum(product(gq, rows, 0, 0), "yxzz").T
        grad_w_key = scatter_sum(product(gk, rows, 0, 0), "xzyz").T
        grad_tokens = (
            r1
            + product(gv, w_value, 1, 1)
            + product(gq, w_query, 1, 1)
            + product(gk, w_key, 1, 1)
        )
        taps_rows = jnp.pad(grad_taps, ((0, 0), (0, width - grad_taps.shape[1])))
        up_rows = jnp.pad(up_sums.reshape(-1, width), ((0, 8 - ff // width), (0, 0)))
        totals = sum_everywhere(jnp.concatenate([row_sums, late_sums, up_rows, taps_rows]))
    row_sums, late = totals[:8], totals[8:16]
    up_sums = totals[16 : 16 + ff // width].reshape(ff)
    grad_conv = totals[24 : 24 + heads, PAIR - 1 : PAIR - 1 + taps]
    return (
        output.reshape(tokens.shape),
        grad_tokens.reshape(tokens.shape),
        grad_w_query,
        late[0],
        grad_w_key,
        grad_w_value,
        late[1],
        grad_conv,
        grad_w_out,
        row_sums[5],
        row_sums[3],
        row_sums[4],
        grad_w_up,
        up_sums,
        grad_w_down,
        row_sums[2],
        row_sums[0],
        row_sums[1],
    )


def solution(mesh):
    rows = P("dp", "seq", None)
    block = P("dp", "seq")
    in_specs = (rows, P("dp"), block) + (P(),) * 16 + (rows,)
    out_specs = (
        rows, rows, block, P(), block, block, P(), P(), block,
        P(), P(), P(), block, P(), block, P(), P(), P(),
    )
    return jax.shard_map(
        on_device, mesh=mesh, in_specs=in_specs, out_specs=out_specs, check_vma=False
    )
```
